32 devices in a mesh: dp: 8 (over y, x, core), seq: 4 (over z).
Axes of the slice: x: 2, y: 2, z: 4, core: 2. Of those that a mesh axis runs over, the one named last changes fastest.
Arguments:
- tokens: bfloat16 [16, 1536, 768], P('dp', 'seq'), may hold values from -6 to 6
- teacher: bfloat16 [16, 1536, 768], P('dp', 'seq'), may hold values from -6 to 6
- teach_mask: int32 [16, 1536], P('dp', 'seq'), may hold values from 0 to 1
- lengths: int32 [16], replicated, may hold values from 1 to 1536, 18432 in all
- deal_group: int32 [16], replicated, may hold values from 0 to 7, as said below
- ln1_gain: bfloat16 [768], P('dp'), may hold values from 0.25 to 1.75
- ln1_bias: bfloat16 [768], P('dp'), may hold values from -3 to 3
- qkv_weight: bfloat16 [768, 2304], P('dp'), may hold values from -0.3125 to 0.3125
- out_weight: bfloat16 [768, 768], P('dp'), may hold values from -0.875 to 0.875
- ln2_gain: bfloat16 [768], P('dp'), may hold values from 0.25 to 1.75
- ln2_bias: bfloat16 [768], P('dp'), may hold values from -3 to 3
- up_weight: bfloat16 [768, 3072], P('dp'), may hold values from -0.21875 to 0.21875
- down_weight: bfloat16 [3072, 768], P('dp'), may hold values from -0.109375 to 0.109375
Outputs:
- activations: bfloat16 [16, 1536, 768], P('dp', 'seq')
- loss: float32 [], replicated
- input_grad: bfloat16 [16, 1536, 768], P('dp', 'seq')
- ln1_gain_grad: float32 [768], P('dp')
- ln1_bias_grad: float32 [768], P('dp')
- qkv_weight_grad: float32 [768, 2304], P('dp')
- out_weight_grad: float32 [768, 768], P('dp')
- ln2_gain_grad: float32 [768], P('dp')
- ln2_bias_grad: float32 [768], P('dp')
- up_weight_grad: float32 [768, 3072], P('dp')
- down_weight_grad: float32 [3072, 768], P('dp')
The draws below stay inside these ranges and needn't reach their ends.
Inputs may be any that keep to these rules, and one draw needn't show every extreme that they name: Sequence 2 g + j (j = 0 or 1) goes to slot j of group deal_group[2 g + j] = g XOR mask_j, where mask_0 is one number of 0 to 7 and mask_1 = mask_0 XOR (7). The lengths add up to 18432 and one of them is 1536.
All inputs are finite; a program needn't handle non-finite values.
Results may differ from the reference program's by a relative error of at most 0.012.
The reference program's roundings to bfloat16 on the way count: a program that leaves them out, or rounds other values in their place, can miss the bound.
Values may be sent and summed in bfloat16 or wider, within the bound.
No kernel may reach another device: no remote copies, remote signals or barrier semaphores. Data moves between devices by JAX's collectives and lax.ppermute only.
A program may use at most 256 MiB of HBM per device.

```python
import math
import jax
import jax.numpy as jnp
import numpy as np
from jax import lax

D = 768
HEADS = 12
HEAD_DIM = 64
FF = 3072
SEQ_LEN = 1536
SEQS = 16
TOTAL = 18432


def draw_deal_group(key, part):
    groups = SEQS // 2
    mask_zero = jax.random.randint(jax.random.fold_in(key, 11), (), 0, groups, dtype=jnp.int32)
    mask_one = jnp.bitwise_xor(mask_zero, groups - 1)
    index_all = jnp.arange(SEQS, dtype=jnp.int32)
    chosen = jnp.where(index_all % 2 == 0, mask_zero, mask_one)
    return jnp.bitwise_xor(index_all // 2, chosen)


def draw_teach_mask(key, part):
    groups = SEQS // 2
    group_row = jnp.arange(SEQS, dtype=jnp.int32) // 2
    limit = 250 + 650 * group_row // max(groups - 1, 1)
    ticket = jax.random.randint(jax.random.fold_in(key, 23), (SEQS, SEQ_LEN), 0, 1000, dtype=jnp.int32)
    return (ticket < limit[:, None]).astype(jnp.int32)


def level_of(own_key, extent, pieces, least, largest):
    factor_of = 1.0
    for position, blocks in pieces:
        steps = jax.random.uniform(jax.random.fold_in(jax.random.fold_in(own_key, 6), position), (blocks,), jnp.float32, least / len(pieces), largest / len(pieces))
        factor_of = factor_of * jnp.repeat(jnp.exp(steps), extent[position] // blocks).reshape((-1,) + (1,) * (len(extent) - 1 - position))
    return factor_of


def length_profile(count, total, bound, lean):
    weights = [(1 << 20) // math.isqrt(rank ** lean) + 1 for rank in range(2, count + 1)]
    surplus, counts = total - bound - (count - 1), [1] * (count - 1)
    while surplus > 0:
        candidates = [i for i in range(count - 1) if counts[i] < bound]
        mass, left = sum([weights[i] for i in candidates]), surplus
        for i in candidates:
            extra = min(bound - counts[i], max(1, left * weights[i] // mass), surplus)
            counts[i] = counts[i] + extra
            surplus = surplus - extra
    return np.array([bound] + counts)


def ragged(rng, number_of, total, most, skew):
    if number_of == 2:
        one = jax.random.randint(rng, (), max(1, total - most), min(most, total - 1) + 1)
        return jnp.stack([one, total - one])
    sizes = jnp.asarray(length_profile(number_of, total, most, skew), jnp.int32)
    twos = (number_of - 1) // 2
    donor, sink = sizes[1:1 + 2 * twos:2], sizes[2:2 + 2 * twos:2]
    margin = jnp.minimum(donor - 1, most - sink)
    passed = jax.random.randint(jax.random.fold_in(rng, 1), (twos,), 0, 1 << 20) % (margin + 1)
    sizes = sizes.at[1:1 + 2 * twos:2].set(donor - passed).at[2:2 + 2 * twos:2].set(sink + passed)
    return sizes[jax.random.permutation(jax.random.fold_in(rng, 2), number_of)]


def bell_draw(rng, dims, scale, most, pieces=(), kind=jnp.bfloat16):
    values = scale * jax.random.normal(rng, dims, jnp.float32)
    if pieces:
        values = values * level_of(rng, dims, pieces, -0.22, 0.18)
    return jnp.clip(values, -most, most).astype(kind)


def setup_inputs(seed: int = 0) -> dict:
    arg_keys = jax.random.split(jax.random.key(seed), 14)
    return {
        "tokens": bell_draw(arg_keys[0], (SEQS, SEQ_LEN, D), 1.0, 6.0, ((0, 8), (1, 4))),
        "teacher": bell_draw(arg_keys[1], (SEQS, SEQ_LEN, D), 1.0, 6.0, ((0, 8), (1, 4))),
        "teach_mask": draw_teach_mask(jax.random.fold_in(arg_keys[13], 71), 0),
        "lengths": ragged(arg_keys[3], SEQS, TOTAL, SEQ_LEN, 2).astype(jnp.int32),
        "deal_group": draw_deal_group(jax.random.fold_in(arg_keys[13], 71), 0),
        "ln1_gain": jnp.clip(1.0 + 0.15 * jax.random.normal(arg_keys[5], (D,), jnp.float32), 0.25, 1.75).astype(jnp.bfloat16),
        "ln1_bias": bell_draw(arg_keys[6], (D,), 0.2, 3.0, ((0, 8),)),
        "qkv_weight": bell_draw(arg_keys[7], (D, 3 * D), (D // 2) ** -0.5, 0.3125, ((0, 8),)),
        "out_weight": bell_draw(arg_keys[8], (D, D), (D // 16) ** -0.5, 0.875, ((0, 8),)),
        "ln2_gain": jnp.clip(1.0 + 0.15 * jax.random.normal(arg_keys[9], (D,), jnp.float32), 0.25, 1.75).astype(jnp.bfloat16),
        "ln2_bias": bell_draw(arg_keys[10], (D,), 0.2, 3.0, ((0, 8),)),
        "up_weight": bell_draw(arg_keys[11], (D, FF), D ** -0.5, 0.21875, ((0, 8),)),
        "down_weight": bell_draw(arg_keys[12], (FF, D), FF ** -0.5, 0.109375, ((0, 8),)),
    }


@jax.custom_vjp
def low(v):
    return lax.optimization_barrier(v.astype(jnp.bfloat16)).astype(jnp.float32)

@jax.custom_vjp
def low_back(v):
    return v

def low_keep(v):
    return (low(v), None)

def low_pass(kept, grad):
    return (grad,)

def back_keep(v):
    return (v, None)

def back_low(kept, grad):
    return (low(grad),)
low.defvjp(low_keep, low_pass)
low_back.defvjp(back_keep, back_low)
EPSILON = 1e-12
NEGATIVE = -1e+30

def dense_mm(left, right):
    return jnp.dot(left, right, precision=lax.Precision.HIGHEST)

def layer_norm(values, gain, shift):
    center = values - lax.optimization_barrier(jnp.mean(values, axis=-1, keepdims=True))
    variance = lax.optimization_barrier(jnp.mean(center * center, axis=-1, keepdims=True))
    return center * lax.rsqrt(variance + EPSILON) * gain + shift

def block_forward(params, values, length):
    gain_one, shift_one, w_qkv, w_out, gain_two, shift_two, w_up, w_down = params
    count_rows = values.shape[0]
    normed = low(layer_norm(values, gain_one, shift_one))
    mixed_all = low(low_back(dense_mm(normed, w_qkv)))
    split_all = mixed_all.reshape(count_rows, HEADS, 3, HEAD_DIM)
    queries = split_all[:, :, 0]
    keys_all = split_all[:, :, 1]
    values_all = split_all[:, :, 2]
    raw_scores = jnp.einsum('qhe,khe->hqk', queries, keys_all, precision=lax.Precision.HIGHEST) * (1.0 / math.sqrt(HEAD_DIM))
    key_keep = jnp.arange(count_rows, dtype=jnp.int32) < length
    scores = jnp.where(key_keep[None, None, :], low_back(raw_scores), NEGATIVE)
    probs_all = jax.nn.softmax(scores, axis=-1)
    attended = jnp.einsum('hqk,khe->qhe', low(probs_all), values_all, precision=lax.Precision.HIGHEST)
    attended = low(low_back(attended.reshape(count_rows, HEADS * HEAD_DIM)))
    middle = values + low_back(dense_mm(attended, w_out))
    normed_two = low(layer_norm(middle, gain_two, shift_two))
    hidden = low_back(dense_mm(normed_two, w_up))
    active = low(jax.nn.gelu(hidden, approximate=False))
    return middle + low_back(dense_mm(active, w_down))

def reference(tokens, teacher, teach_mask, lengths, deal_group, ln1_gain, ln1_bias, qkv_weight, out_weight, ln2_gain, ln2_bias, up_weight, down_weight):
    params = (ln1_gain.astype(jnp.float32), ln1_bias.astype(jnp.float32), qkv_weight.astype(jnp.float32), out_weight.astype(jnp.float32), ln2_gain.astype(jnp.float32), ln2_bias.astype(jnp.float32), up_weight.astype(jnp.float32), down_weight.astype(jnp.float32))
    parity = jnp.arange(SEQS, dtype=jnp.int32) % 2
    target = (deal_group * 2 + parity).astype(jnp.int32)
    positions = jnp.arange(SEQ_LEN, dtype=jnp.int32)
    valid_mask = (positions[None, :] < lengths[:, None]) & (teach_mask[target] == 1)
    valid_count = jnp.sum(valid_mask.astype(jnp.float32))
    pull_scale = SEQS * SEQ_LEN * 1.0 / valid_count

    def one_sequence(carry, inputs):
        grad_sums, total_sq = carry
        token_rows, chosen, length, keep_rows = inputs
        goal_rows = lax.dynamic_index_in_dim(teacher, chosen.astype(jnp.int32), 0, keepdims=False).astype(jnp.float32)

        def objective(weights_in, values_in):
            result_rows = block_forward(weights_in, values_in, length)
            error_rows = result_rows - goal_rows
            return (jnp.sum(jnp.where(keep_rows[:, None], error_rows * error_rows, 0.0)), result_rows)
        part_sq, pullback, result_rows = jax.vjp(objective, params, token_rows.astype(jnp.float32), has_aux=True)
        grad_params, grad_values = pullback(pull_scale)
        grad_sums = jax.tree.map(jnp.add, grad_sums, grad_params)
        return ((grad_sums, total_sq + part_sq), (result_rows.astype(jnp.bfloat16), grad_values.astype(jnp.bfloat16)))
    start = (jax.tree.map(jnp.zeros_like, params), jnp.zeros((), jnp.float32))
    (grad_sums, total_sq), (outputs, grads_in) = lax.scan(one_sequence, start, (tokens, target, lengths, valid_mask))
    loss = total_sq / (valid_count * D)
    return (outputs, loss, grads_in, grad_sums[0], grad_sums[1], grad_sums[2], grad_sums[3], grad_sums[4], grad_sums[5], grad_sums[6], grad_sums[7])
```

```python
import functools
import math

import jax
import jax.numpy as jnp
from jax import lax
from jax.experimental import pallas as pl
from jax.experimental.pallas import tpu as pltpu
from jax.sharding import Mesh
from jax.sharding import PartitionSpec as P

HEADS = 12
HEAD_DIM = 64
EPSILON = 1e-12
NEGATIVE = -1e30
SCALE = 1.0 / math.sqrt(HEAD_DIM)
AXES = ("pair", "core", "seq")
NT = (((1,), (1,)), ((), ()))
NN = (((1,), (0,)), ((), ()))
TN = (((0,), (0,)), ((), ()))
LOW = jnp.bfloat16
FULL = jnp.float32


def dot(left, right, form):
    return lax.dot_general(left, right, form, preferred_element_type=FULL)


def moved(value, target):
    pairs, cores, depth = (lax.axis_size(name) for name in AXES)
    links = []
    for p in range(pairs):
        for c in range(cores):
            for z in range(depth):
                q, e, w = target(p, c, z)
                links.append(((p * cores + c) * depth + z, (q * cores + e) * depth + w))
    return lax.ppermute(value, AXES, links)


def across_cores(value):
    return moved(value, lambda p, c, z: (p, 1 - c, z))


def across_pairs(value, bit):
    return moved(value, lambda p, c, z: (p ^ bit, c, z))


def across_depth(value, bit):
    return moved(value, lambda p, c, z: (p, c, z ^ bit))


def pair_bits():
    return [1 << level for level in range(lax.axis_size("pair").bit_length() - 1)]


def turned(stack):
    z = lax.axis_index("seq")
    got = []
    for step in range(2):
        piece = lax.dynamic_index_in_dim(stack, (z + step) % 2, 0, keepdims=False)
        got.append(moved(piece, lambda p, c, w: (p, w // 2, 2 * c + (w + step) % 2)))
    even = z % 2 == 0
    return jnp.stack([jnp.where(even, got[0], got[1]), jnp.where(even, got[1], got[0])])


def summed_everywhere(value):
    value = value + across_cores(value)
    for bit in pair_bits():
        value = value + across_pairs(value, bit)
    for level in range(lax.axis_size("seq").bit_length() - 1):
        value = value + across_depth(value, 1 << level)
    return value


def gathered_over_pairs(value):
    p = lax.axis_index("pair")
    rows, width = value.shape
    bits = pair_bits()
    count = 1 << len(bits)
    halves = []
    for which in range(2):
        order = bits if which == 0 else bits[::-1]
        current = value[which * rows // 2 : (which + 1) * rows // 2]
        for bit in order:
            other = across_pairs(current, bit)
            flag = jnp.bitwise_and(p, bit) != 0
            current = jnp.stack(
                [jnp.where(flag, other, current), jnp.where(flag, current, other)]
            )
        if which == 1:
            lead = tuple(range(len(bits)))[::-1]
            current = jnp.transpose(current, lead + (len(bits), len(bits) + 1))
        halves.append(current.reshape(count, rows // 2, width))
    return jnp.concatenate(halves, axis=1).reshape(count * rows, width)


def scattered_over_pairs(value):
    p = lax.axis_index("pair")
    bits = pair_bits()
    count = 1 << len(bits)
    rows, width = value.shape[0] // count, value.shape[1]
    blocks = value.reshape(count, rows, width)
    halves = []
    for which in range(2):
        order = bits if which == 0 else bits[::-1]
        current = blocks[:, which * rows // 2 : (which + 1) * rows // 2]
        current = current.reshape((2,) * len(bits) + (rows // 2, width))
        left = bits[::-1]
        for bit in order:
            axis = left.index(bit)
            mine = jnp.where(jnp.bitwise_and(p, bit) != 0, 1, 0)
            keep = lax.dynamic_index_in_dim(current, mine, axis, keepdims=False)
            send = lax.dynamic_index_in_dim(current, 1 - mine, axis, keepdims=False)
            current = keep + across_pairs(send, bit)
            left = [other for other in left if other != bit]
        halves.append(current)
    return jnp.concatenate(halves, axis=0)


def summed_over_depth(value):
    z = lax.axis_index("seq")
    current = value
    trail = []
    for level in range(lax.axis_size("seq").bit_length() - 1):
        bit = 1 << level
        mine = jnp.where(jnp.bitwise_and(z, bit) != 0, 1, 0)
        parts = current.reshape((2, current.shape[0] // 2) + current.shape[1:])
        keep = lax.dynamic_index_in_dim(parts, mine, 0, keepdims=False)
        send = lax.dynamic_index_in_dim(parts, 1 - mine, 0, keepdims=False)
        current = keep + across_depth(send, bit)
        trail.append((bit, mine))
    for bit, mine in trail[::-1]:
        other = across_depth(current, bit)
        first = jnp.where(mine == 0, current, other)
        second = jnp.where(mine == 0, other, current)
        current = jnp.concatenate([first, second], axis=0)
    return current


def keys_with_mask(k_ref, counts_ref, ka, rows):
    lane = lax.broadcasted_iota(jnp.int32, (rows, 128), 1)
    spot = lax.broadcasted_iota(jnp.int32, (rows, 128), 0)
    limit = jnp.where(spot < rows // 2, counts_ref[0], counts_ref[1] + rows // 2)
    bias = jnp.where(spot < limit, 0.0, NEGATIVE)
    k = k_ref[...].astype(FULL)
    ka[0] = jnp.where(lane < 64, k, jnp.where(lane == 64, bias, 0.0)).astype(LOW)
    ka[1] = jnp.where(lane >= 64, k, jnp.where(lane == 0, bias, 0.0)).astype(LOW)


def forward_kernel(counts_ref, q_ref, k_ref, v_ref, o_ref, lse_ref, ka, vt, *, rows, block):
    @pl.when(pl.program_id(1) == 0)
    def _():
        keys_with_mask(k_ref, counts_ref, ka, rows)
        vt[...] = v_ref[...].T

    lane = lax.broadcasted_iota(jnp.int32, (block, 128), 1)
    q = q_ref[...].astype(FULL) * SCALE
    mixed = []
    for h in range(2):
        mine = (lane < 64) if h == 0 else (lane >= 64)
        flag = lane == (64 if h == 0 else 0)
        qa = jnp.where(mine, q, jnp.where(flag, 1.0, 0.0)).astype(LOW)
        scores = dot(ka[h], qa, NT)
        highest = jnp.max(scores, axis=0, keepdims=True)
        exponent = jnp.exp(scores - highest)
        totals = jnp.sum(exponent, axis=0, keepdims=True)
        part = dot(vt[pl.ds(64 * h, 64), :], exponent.astype(LOW), NN)
        mixed.append(part * (1.0 / totals))
        lse_ref[0, pl.ds(h, 1), :] = highest + jnp.log(totals)
    o_ref[...] = jnp.concatenate(mixed, axis=0).T.astype(LOW)


def attention_forward(counts, qkv, block):
    rows, width = qkv.shape
    pairs = width // 384
    return pl.pallas_call(
        functools.partial(forward_kernel, rows=rows, block=block),
        grid_spec=pltpu.PrefetchScalarGridSpec(
            num_scalar_prefetch=1,
            grid=(pairs, rows // block),
            in_specs=[
                pl.BlockSpec((block, 128), lambda h, i, n: (i, h)),
                pl.BlockSpec((rows, 128), lambda h, i, n: (0, pairs + h)),
                pl.BlockSpec((rows, 128), lambda h, i, n: (0, 2 * pairs + h)),
            ],
            out_specs=[
                pl.BlockSpec((block, 128), lambda h, i, n: (i, h)),
                pl.BlockSpec((1, 2, block), lambda h, i, n: (h, 0, i)),
            ],
            scratch_shapes=[pltpu.VMEM((2, rows, 128), LOW), pltpu.VMEM((128, rows), LOW)],
        ),
        out_shape=[
            jax.ShapeDtypeStruct((rows, pairs * 128), LOW),
            jax.ShapeDtypeStruct((pairs, 2, rows), FULL),
        ],
        cost_estimate=pl.CostEstimate(
            flops=8 * pairs * rows * rows * 128,
            bytes_accessed=rows * width * 3,
            transcendentals=2 * pairs * rows * rows,
        ),
        name="attention_forward",
    )(counts, qkv, qkv, qkv)


def backward_kernel(
    counts_ref, q_ref, k_ref, v_ref, o_ref, g_ref, lse_ref, grad_ref,
    ka, va, kt, dk, dv, *, rows, block, steps, chunk, pairs,
):
    pair, step = pl.program_id(0), pl.program_id(1)

    @pl.when(step == 0)
    def _():
        keys_with_mask(k_ref, counts_ref, ka, rows)
        lane = lax.broadcasted_iota(jnp.int32, (rows, 128), 1)
        v = v_ref[...].astype(FULL)
        va[0] = jnp.where(lane < 64, v, 0.0).astype(LOW)
        va[1] = jnp.where(lane >= 64, v, 0.0).astype(LOW)
        kt[...] = k_ref[...].T
        dk[...] = jnp.zeros_like(dk)
        dv[...] = jnp.zeros_like(dv)

    lane = lax.broadcasted_iota(jnp.int32, (block, 128), 1)
    q = q_ref[...].astype(FULL)
    g = g_ref[...]
    wide = g.astype(FULL)
    product = (wide * o_ref[...].astype(FULL)).T
    scaled = q * SCALE
    columns = []
    for h in range(2):
        mine = (lane < 64) if h == 0 else (lane >= 64)
        flag = lane == (64 if h == 0 else 0)
        qa = jnp.where(mine, scaled, jnp.where(flag, 1.0, 0.0)).astype(LOW)
        qm = jnp.where(mine, q, 0.0).astype(LOW)
        gm = jnp.where(mine, wide, 0.0).astype(LOW)
        delta = jnp.sum(product[64 * h : 64 * h + 64], axis=0, keepdims=True)
        lse = lse_ref[0, pl.ds(h, 1), :]
        total = jnp.zeros((64, block), FULL)
        for c in range(rows // chunk):
            part = pl.ds(c * chunk, chunk)
            probs = jnp.exp(dot(ka[h, part, :], qa, NT) - lse)
            grad_probs = dot(va[h, part, :], g, NT)
            grad_scores = (probs * (grad_probs - delta)).astype(LOW)
            dv[part, :] += dot(probs.astype(LOW), gm, NN)
            dk[part, :] += dot(grad_scores, qm, NN)
            total = total + dot(kt[pl.ds(64 * h, 64), part], grad_scores, NN)
        columns.append(total)
    spot = pl.ds(pl.multiple_of(step * block, block), block)
    here = pl.multiple_of(pair * 128, 128)
    grad_ref[spot, pl.ds(here, 128)] = (jnp.concatenate(columns, axis=0).T * SCALE).astype(LOW)

    @pl.when(step == steps - 1)
    def _():
        grad_ref[:, pl.ds(here + pairs * 128, 128)] = (dk[...] * SCALE).astype(LOW)
        grad_ref[:, pl.ds(here + pairs * 256, 128)] = dv[...].astype(LOW)


def attention_backward(counts, qkv, mixed, grad, lse, block, chunk):
    rows, width = qkv.shape
    pairs = width // 384
    steps = rows // block
    return pl.pallas_call(
        functools.partial(
            backward_kernel, rows=rows, block=block, steps=steps, chunk=chunk, pairs=pairs
        ),
        grid_spec=pltpu.PrefetchScalarGridSpec(
            num_scalar_prefetch=1,
            grid=(pairs, steps),
            in_specs=[
                pl.BlockSpec((block, 128), lambda h, i, n: (i, h)),
                pl.BlockSpec((rows, 128), lambda h, i, n: (0, pairs + h)),
                pl.BlockSpec((rows, 128), lambda h, i, n: (0, 2 * pairs + h)),
                pl.BlockSpec((block, 128), lambda h, i, n: (i, h)),
                pl.BlockSpec((block, 128), lambda h, i, n: (i, h)),
                pl.BlockSpec((1, 2, block), lambda h, i, n: (h, 0, i)),
            ],
            out_specs=pl.BlockSpec((rows, width), lambda h, i, n: (0, 0)),
            scratch_shapes=[
                pltpu.VMEM((2, rows, 128), LOW),
                pltpu.VMEM((2, rows, 128), LOW),
                pltpu.VMEM((128, rows), LOW),
                pltpu.VMEM((rows, 128), FULL),
                pltpu.VMEM((rows, 128), FULL),
            ],
        ),
        out_shape=jax.ShapeDtypeStruct((rows, width), LOW),
        cost_estimate=pl.CostEstimate(
            flops=20 * pairs * rows * rows * 128,
            bytes_accessed=rows * width * 5,
            transcendentals=2 * pairs * rows * rows,
        ),
        name="attention_backward",
    )(counts, qkv, qkv, qkv, mixed, grad, lse)


def norm_parts(values):
    center = values - jnp.mean(values, axis=-1, keepdims=True)
    inverse = lax.rsqrt(jnp.mean(center * center, axis=-1, keepdims=True) + EPSILON)
    return center * inverse, inverse


def norm_backward(upstream, unit, inverse, gain):
    scaled = upstream * gain
    first = jnp.mean(scaled, axis=-1, keepdims=True)
    second = jnp.mean(scaled * unit, axis=-1, keepdims=True)
    result = inverse * (scaled - first - unit * second)
    return result, jnp.sum(upstream * unit, axis=0), jnp.sum(upstream, axis=0)


def gelu_parts(values):
    share = 0.5 * (1.0 + lax.erf(values * (1.0 / math.sqrt(2.0))))
    density = jnp.exp(-0.5 * values * values) * (1.0 / math.sqrt(2.0 * math.pi))
    return values * share, share + values * density


def shards(
    tokens, teacher, teach_mask, lengths, deal_group,
    ln1_gain, ln1_bias, qkv_weight, out_weight, ln2_gain, ln2_bias, up_weight, down_weight,
):
    pairs, cores, depth = (lax.axis_size(name) for name in AXES)
    p, c, z = (lax.axis_index(name) for name in AXES)
    groups = pairs * cores
    slot_rows, width = tokens.shape[1], tokens.shape[2]
    rows = 2 * slot_rows
    full_len = depth * slot_rows
    seq_count = lengths.shape[0]
    ff = up_weight.shape[1]
    own_rows = width // groups
    pair_rows = cores * own_rows
    half_width = width // 2
    half_ff = ff // 2
    is_first = c == 0

    def in_order(mine, other, axis):
        return jnp.concatenate(
            [jnp.where(is_first, mine, other), jnp.where(is_first, other, mine)], axis=axis
        )

    sequence = 2 * cores * p + z
    length = jnp.sum(jnp.where(jnp.arange(seq_count) == sequence, lengths, 0))
    base = c * rows
    counts = jnp.stack([length - base, length - (rows - base)])
    counts = jnp.clip(counts, 0, rows).astype(jnp.int32)

    x_rows = turned(tokens).reshape(rows, width)

    masks = deal_group[0:2]
    group = p * cores + c
    sources = jnp.bitwise_xor(group, masks) * 2 + jnp.arange(2, dtype=jnp.int32)
    picked = jnp.arange(seq_count, dtype=jnp.int32)[None, :] == sources[:, None]
    dealt_len = jnp.sum(jnp.where(picked, lengths[None, :], 0), axis=1)
    positions = z * slot_rows + jnp.arange(slot_rows, dtype=jnp.int32)
    live = (positions[None, :] < dealt_len[:, None]) & (teach_mask == 1)
    valid_count = summed_everywhere(jnp.full((8, 128), jnp.sum(live.astype(FULL))))[0, 0]

    heads_half = HEADS // 2
    shard = qkv_weight.reshape(own_rows, 2, heads_half, 3, HEAD_DIM)
    shard = jnp.transpose(shard, (1, 0, 3, 2, 4)).reshape(2, own_rows, 3 * half_width)
    keep = lax.dynamic_index_in_dim(shard, c, 0, keepdims=False)
    send = lax.dynamic_index_in_dim(shard, 1 - c, 0, keepdims=False)
    w_qkv = gathered_over_pairs(in_order(keep, across_cores(send), 0))

    block = ff // groups
    up_shard = up_weight.reshape(own_rows, pairs, cores, 2, block // 2)
    up_shard = jnp.transpose(up_shard, (2, 0, 3, 1, 4)).reshape(cores, own_rows, half_ff)
    out_shard = jnp.transpose(out_weight.reshape(own_rows, 2, half_width), (1, 0, 2))
    both = jnp.concatenate([up_shard, out_shard], axis=2)
    keep = lax.dynamic_index_in_dim(both, c, 0, keepdims=False)
    send = lax.dynamic_index_in_dim(both, 1 - c, 0, keepdims=False)
    both = in_order(keep, across_cores(send), 0)
    down_shard = jnp.concatenate([down_weight[: block // 2], down_weight[block // 2 :]], axis=1)
    mine = gathered_over_pairs(jnp.concatenate([both, down_shard], axis=1))
    other = across_cores(mine)

    def unpacked(stack):
        up = stack[:, :half_ff]
        out = stack[:, half_ff : half_ff + half_width]
        down = stack[:, half_ff + half_width :]
        return up, out, jnp.concatenate([down[:, :width], down[:, width:]], axis=0)

    up_mine, out_mine, down_mine = unpacked(mine)
    up_other, out_other, down_other = unpacked(other)
    w_out = in_order(out_mine, out_other, 1)

    vectors = jnp.stack([ln1_gain, ln1_bias, ln2_gain, ln2_bias])
    vectors = lax.all_gather(vectors, ("pair", "core"), axis=1, tiled=True).astype(FULL)
    gain_one, shift_one, gain_two, shift_two = vectors[0], vectors[1], vectors[2], vectors[3]

    mask_rows = jnp.pad(
        teach_mask.astype(LOW)[:, None, :], ((0, 0), (0, 15), (0, width - slot_rows))
    )
    slots = jnp.concatenate([teacher, mask_rows], axis=1)
    for level in range(groups.bit_length() - 1):
        flagged = jnp.bitwise_and(jnp.right_shift(masks[0], level), 1) == 1
        outgoing = jnp.where(flagged, slots[0], slots[1])
        incoming = across_cores(outgoing) if level == 0 else across_pairs(outgoing, 1 << (level - 1))
        slots = jnp.stack(
            [jnp.where(flagged, incoming, slots[0]), jnp.where(flagged, slots[1], incoming)]
        )
    goal = turned(slots)
    spots = base + jnp.arange(rows, dtype=jnp.int32)
    taught = goal[:, slot_rows, :slot_rows].reshape(rows)
    valid = ((spots < length) & (taught == 1)).astype(FULL)[:, None]
    goal = goal[:, :slot_rows].reshape(rows, width).astype(FULL)

    x_full = x_rows.astype(FULL)
    unit_one, inverse_one = norm_parts(x_full)
    norm_mine = (unit_one * gain_one + shift_one).astype(LOW)
    norm_one = jnp.concatenate([norm_mine, across_cores(norm_mine)], axis=0)
    qkv = dot(norm_one, w_qkv, NN).astype(LOW)
    mixed, lse = attention_forward(counts, qkv, 512)
    attended = in_order(mixed[:rows], across_cores(mixed[rows:]), 1)
    middle = x_full + dot(attended, w_out, NN)
    unit_two, inverse_two = norm_parts(middle)
    norm_two = (unit_two * gain_two + shift_two).astype(LOW)
    value_mine, slope_mine = gelu_parts(dot(norm_two, up_mine, NN))
    value_other, slope_other = gelu_parts(dot(norm_two, up_other, NN))
    active_mine = value_mine.astype(LOW)
    active_other = value_other.astype(LOW)
    output = middle + dot(active_mine, down_mine, NN) + dot(active_other, down_other, NN)
    activations = turned(output.astype(LOW).reshape(2, slot_rows, width))

    error = output - goal
    squares = jnp.sum(valid * error * error)
    factor = seq_count * full_len * 1.0 / valid_count
    grad_out = valid * (2.0 * factor) * error
    grad_ff = grad_out.astype(LOW)
    down_grad_mine = dot(active_mine, grad_ff, TN).astype(LOW)
    down_grad_other = dot(active_other, grad_ff, TN).astype(LOW)
    hidden_mine = (dot(grad_ff, down_mine, NT) * slope_mine).astype(LOW)
    hidden_other = (dot(grad_ff, down_other, NT) * slope_other).astype(LOW)
    up_grad_mine = dot(norm_two, hidden_mine, TN).astype(LOW)
    up_grad_other = dot(norm_two, hidden_other, TN).astype(LOW)
    grad_norm_two = dot(hidden_mine, up_mine, NT) + dot(hidden_other, up_other, NT)
    grad_mid, gain_two_grad, shift_two_grad = norm_backward(
        grad_norm_two, unit_two, inverse_two, gain_two
    )
    grad_middle = grad_out + grad_mid
    grad_branch = grad_middle.astype(LOW)
    out_grad = dot(attended, grad_branch, TN).astype(LOW)
    grad_attended = dot(grad_branch, w_out, NT).astype(LOW)
    keep = jnp.where(is_first, grad_attended[:, :half_width], grad_attended[:, half_width:])
    send = jnp.where(is_first, grad_attended[:, half_width:], grad_attended[:, :half_width])
    grad_mixed = jnp.concatenate([keep, across_cores(send)], axis=0)

    def packed(up, out, down):
        return jnp.concatenate([up, out, down[:width], down[width:]], axis=1)

    out_halves = jnp.stack([out_grad[:, :half_width], out_grad[:, half_width:]])
    out_keep = lax.dynamic_index_in_dim(out_halves, c, 0, keepdims=False)
    out_send = lax.dynamic_index_in_dim(out_halves, 1 - c, 0, keepdims=False)
    grads = packed(up_grad_mine, out_keep, down_grad_mine) + across_cores(
        packed(up_grad_other, out_send, down_grad_other)
    )
    grads = summed_over_depth(scattered_over_pairs(grads))

    grad_qkv = attention_backward(counts, qkv, mixed, grad_mixed, lse, 512, 512)
    partial = dot(grad_qkv, w_qkv, NT)
    grad_norm_one = partial[:rows] + across_cores(partial[rows:].astype(LOW)).astype(FULL)
    qkv_grad = dot(norm_one, grad_qkv, TN).astype(LOW)
    qkv_grad = summed_over_depth(scattered_over_pairs(qkv_grad))
    grad_in, gain_one_grad, shift_one_grad = norm_backward(
        grad_norm_one, unit_one, inverse_one, gain_one
    )
    input_grad = turned((grad_middle + grad_in).astype(LOW).reshape(2, slot_rows, width))

    small = jnp.stack(
        [
            gain_one_grad, shift_one_grad, gain_two_grad, shift_two_grad,
            jnp.full((width,), squares), jnp.zeros((width,)), jnp.zeros((width,)),
            jnp.zeros((width,)),
        ]
    )
    small = summed_everywhere(small)
    loss = small[4, 0] / (valid_count * width)
    own_small = lax.dynamic_slice_in_dim(small, group * own_rows, own_rows, 1)

    def own_block(stack, index):
        return lax.dynamic_slice_in_dim(stack, index * own_rows, own_rows, 0)

    wide = jnp.concatenate([grads[:, : half_ff + half_width], qkv_grad], axis=1)
    mine = own_block(wide, c)
    other = across_cores(own_block(wide, 1 - c))
    halves = jnp.stack([jnp.where(is_first, mine, other), jnp.where(is_first, other, mine)])
    halves = halves.astype(FULL)
    up_own = halves[:, :, :half_ff].reshape(cores, own_rows, 2, pairs, block // 2)
    up_own = jnp.transpose(up_own, (1, 3, 0, 2, 4)).reshape(own_rows, ff)
    out_own = jnp.transpose(halves[:, :, half_ff : half_ff + half_width], (1, 0, 2))
    out_own = out_own.reshape(own_rows, width)
    qkv_own = halves[:, :, half_ff + half_width :].reshape(2, own_rows, 3, heads_half, HEAD_DIM)
    qkv_own = jnp.transpose(qkv_own, (1, 0, 3, 2, 4)).reshape(own_rows, 3 * width)
    down_own = grads[:, half_ff + half_width :]
    down_own = jnp.concatenate([down_own[:, :width], down_own[:, width:]], axis=0).astype(FULL)
    return (
        activations, loss, input_grad, own_small[0], own_small[1], qkv_own, out_own,
        own_small[2], own_small[3], up_own, down_own,
    )


def solution(mesh):
    groups, depth = mesh.shape["dp"], mesh.shape["seq"]
    split = Mesh(mesh.devices.reshape(groups // 2, 2, depth), AXES)
    dp = ("pair", "core")
    rows3 = P(dp, "seq", None)
    in_specs = (
        rows3, rows3, P(dp, "seq"), P(), P(), P(dp), P(dp), P(dp, None), P(dp, None),
        P(dp), P(dp), P(dp, None), P(dp, None),
    )
    out_specs = (
        rows3, P(), rows3, P(dp), P(dp), P(dp, None), P(dp, None), P(dp), P(dp),
        P(dp, None), P(dp, None),
    )
    return jax.shard_map(shards, mesh=split, in_specs=in_specs, out_specs=out_specs, check_vma=False)
```

```python
import functools
import math

import jax
import jax.numpy as jnp
from jax import lax
from jax.experimental import pallas as pl
from jax.experimental.pallas import tpu as pltpu
from jax.sharding import Mesh
from jax.sharding import PartitionSpec as P

HEADS = 12
HEAD_DIM = 64
EPSILON = 1e-12
NEGATIVE = -1e30
SCALE = 1.0 / math.sqrt(HEAD_DIM)
AXES = ("pair", "core", "seq")
NT = (((1,), (1,)), ((), ()))
NN = (((1,), (0,)), ((), ()))
TN = (((0,), (0,)), ((), ()))
LOW = jnp.bfloat16
FULL = jnp.float32


def dot(left, right, form):
    return lax.dot_general(left, right, form, preferred_element_type=FULL)


def moved(value, target):
    pairs, cores, depth = (lax.axis_size(name) for name in AXES)
    links = []
    for p in range(pairs):
        for c in range(cores):
            for z in range(depth):
                q, e, w = target(p, c, z)
                links.append(((p * cores + c) * depth + z, (q * cores + e) * depth + w))
    return lax.ppermute(value, AXES, links)


def across_cores(value):
    return moved(value, lambda p, c, z: (p, 1 - c, z))


def across_pairs(value, bit):
    return moved(value, lambda p, c, z: (p ^ bit, c, z))


def across_depth(value, bit):
    return moved(value, lambda p, c, z: (p, c, z ^ bit))


def pair_bits():
    return [1 << level for level in range(lax.axis_size("pair").bit_length() - 1)]


def turned(stack):
    z = lax.axis_index("seq")
    got = []
    for step in range(2):
        piece = lax.dynamic_index_in_dim(stack, (z + step) % 2, 0, keepdims=False)
        got.append(moved(piece, lambda p, c, w: (p, w // 2, 2 * c + (w + step) % 2)))
    even = z % 2 == 0
    return jnp.stack([jnp.where(even, got[0], got[1]), jnp.where(even, got[1], got[0])])


def summed_everywhere(value):
    value = value + across_cores(value)
    for bit in pair_bits():
        value = value + across_pairs(value, bit)
    for level in range(lax.axis_size("seq").bit_length() - 1):
        value = value + across_depth(value, 1 << level)
    return value


def gathered_over_pairs(value):
    p = lax.axis_index("pair")
    if lax.axis_size("pair") <= 4:
        return ([value] + [across_pairs(value, k) for k in range(1, lax.axis_size("pair"))], p)
    rows, width = value.shape
    bits = pair_bits()
    count = 1 << len(bits)
    halves = []
    for which in range(2):
        order = bits if which == 0 else bits[::-1]
        current = value[which * rows // 2 : (which + 1) * rows // 2]
        for bit in order:
            other = across_pairs(current, bit)
            flag = jnp.bitwise_and(p, bit) != 0
            current = jnp.stack(
                [jnp.where(flag, other, current), jnp.where(flag, current, other)]
            )
        if which == 1:
            lead = tuple(range(len(bits)))[::-1]
            current = jnp.transpose(current, lead + (len(bits), len(bits) + 1))
        halves.append(current.reshape(count, rows // 2, width))
    return ([jnp.concatenate(halves, axis=1).reshape(count * rows, width)], None)


def assembled(gathered):
    pieces, p = gathered
    if p is None:
        return pieces[0]
    rows, width = pieces[0].shape
    whole = jnp.zeros((len(pieces) * rows, width), pieces[0].dtype)
    for k, piece in enumerate(pieces):
        whole = lax.dynamic_update_slice_in_dim(whole, piece, jnp.bitwise_xor(p, k) * rows, 0)
    return whole


def scattered_over_pairs(value):
    p = lax.axis_index("pair")
    if lax.axis_size("pair") <= 4:
        rows = value.shape[0] // lax.axis_size("pair")
        pieces = []
        for k in range(lax.axis_size("pair")):
            piece = lax.dynamic_slice_in_dim(value, jnp.bitwise_xor(p, k) * rows, rows, 0)
            pieces.append(across_pairs(piece, k) if k else piece)
        return pieces
    bits = pair_bits()
    count = 1 << len(bits)
    rows, width = value.shape[0] // count, value.shape[1]
    blocks = value.reshape(count, rows, width)
    halves = []
    for which in range(2):
        order = bits if which == 0 else bits[::-1]
        current = blocks[:, which * rows // 2 : (which + 1) * rows // 2]
        current = current.reshape((2,) * len(bits) + (rows // 2, width))
        left = bits[::-1]
        for bit in order:
            axis = left.index(bit)
            mine = jnp.where(jnp.bitwise_and(p, bit) != 0, 1, 0)
            keep = lax.dynamic_index_in_dim(current, mine, axis, keepdims=False)
            send = lax.dynamic_index_in_dim(current, 1 - mine, axis, keepdims=False)
            current = keep + across_pairs(send, bit)
            left = [other for other in left if other != bit]
        halves.append(current)
    return [jnp.concatenate(halves, axis=0)]


def added(pieces):
    total = pieces[0].astype(FULL)
    for piece in pieces[1:]:
        total = total + piece.astype(FULL)
    return total.astype(LOW)


def depth_flag(bit):
    return jnp.where(jnp.bitwise_and(lax.axis_index("seq"), bit) != 0, 1, 0)


def depth_halved(value, bit):
    mine = depth_flag(bit)
    parts = value.reshape((2, value.shape[0] // 2) + value.shape[1:])
    keep = lax.dynamic_index_in_dim(parts, mine, 0, keepdims=False)
    send = lax.dynamic_index_in_dim(parts, 1 - mine, 0, keepdims=False)
    return [keep, across_depth(send, bit)]


def depth_doubled(value, other, bit):
    mine = depth_flag(bit)
    return jnp.concatenate(
        [jnp.where(mine == 0, value, other), jnp.where(mine == 0, other, value)], axis=0
    )


def tied(*values):
    return lax.optimization_barrier(values)


def keys_with_mask(k_ref, counts_ref, ka, rows):
    lane = lax.broadcasted_iota(jnp.int32, (rows, 128), 1)
    spot = lax.broadcasted_iota(jnp.int32, (rows, 128), 0)
    limit = jnp.where(spot < rows // 2, counts_ref[0], counts_ref[1] + rows // 2)
    bias = jnp.where(spot < limit, 0.0, NEGATIVE)
    k = k_ref[...].astype(FULL)
    ka[0] = jnp.where(lane < 64, k, jnp.where(lane == 64, bias, 0.0)).astype(LOW)
    ka[1] = jnp.where(lane >= 64, k, jnp.where(lane == 0, bias, 0.0)).astype(LOW)


def forward_kernel(counts_ref, q_ref, k_ref, v_ref, o_ref, lse_ref, ka, vt, *, rows, block):
    @pl.when(pl.program_id(1) == 0)
    def _():
        keys_with_mask(k_ref, counts_ref, ka, rows)
        vt[...] = v_ref[...].T

    lane = lax.broadcasted_iota(jnp.int32, (block, 128), 1)
    q = q_ref[...].astype(FULL) * SCALE
    mixed = []
    for h in range(2):
        mine = (lane < 64) if h == 0 else (lane >= 64)
        flag = lane == (64 if h == 0 else 0)
        qa = jnp.where(mine, q, jnp.where(flag, 1.0, 0.0)).astype(LOW)
        scores = dot(ka[h], qa, NT)
        highest = jnp.max(scores, axis=0, keepdims=True)
        exponent = jnp.exp(scores - highest)
        totals = jnp.sum(exponent, axis=0, keepdims=True)
        part = dot(vt[pl.ds(64 * h, 64), :], exponent.astype(LOW), NN)
        mixed.append(part * (1.0 / totals))
        lse_ref[0, pl.ds(h, 1), :] = highest + jnp.log(totals)
    o_ref[...] = jnp.concatenate(mixed, axis=0).T.astype(LOW)


def attention_forward(counts, qkv, block):
    rows, width = qkv.shape
    pairs = width // 384
    return pl.pallas_call(
        functools.partial(forward_kernel, rows=rows, block=block),
        grid_spec=pltpu.PrefetchScalarGridSpec(
            num_scalar_prefetch=1,
            grid=(pairs, rows // block),
            in_specs=[
                pl.BlockSpec((block, 128), lambda h, i, n: (i, 3 * h)),
                pl.BlockSpec((rows, 128), lambda h, i, n: (0, 3 * h + 1)),
                pl.BlockSpec((rows, 128), lambda h, i, n: (0, 3 * h + 2)),
            ],
            out_specs=[
                pl.BlockSpec((block, 128), lambda h, i, n: (i, h)),
                pl.BlockSpec((1, 2, block), lambda h, i, n: (h, 0, i)),
            ],
            scratch_shapes=[pltpu.VMEM((2, rows, 128), LOW), pltpu.VMEM((128, rows), LOW)],
        ),
        out_shape=[
            jax.ShapeDtypeStruct((rows, pairs * 128), LOW),
            jax.ShapeDtypeStruct((pairs, 2, rows), FULL),
        ],
        cost_estimate=pl.CostEstimate(
            flops=8 * pairs * rows * rows * 128,
            bytes_accessed=rows * width * 3,
            transcendentals=2 * pairs * rows * rows,
        ),
        name="attention_forward",
    )(counts, qkv, qkv, qkv)


def backward_kernel(
    counts_ref, q_ref, k_ref, v_ref, o_ref, g_ref, lse_ref, grad_ref,
    ka, va, kt, dk, dv, *, rows, block, steps, chunk,
):
    step = pl.program_id(0)

    @pl.when(step == 0)
    def _():
        keys_with_mask(k_ref, counts_ref, ka, rows)
        lane = lax.broadcasted_iota(jnp.int32, (rows, 128), 1)
        v = v_ref[...].astype(FULL)
        va[0] = jnp.where(lane < 64, v, 0.0).astype(LOW)
        va[1] = jnp.where(lane >= 64, v, 0.0).astype(LOW)
        kt[...] = k_ref[...].T
        dk[...] = jnp.zeros_like(dk)
        dv[...] = jnp.zeros_like(dv)

    lane = lax.broadcasted_iota(jnp.int32, (block, 128), 1)
    q = q_ref[...].astype(FULL)
    g = g_ref[...]
    wide = g.astype(FULL)
    product = (wide * o_ref[...].astype(FULL)).T
    scaled = q * SCALE
    columns = []
    for h in range(2):
        mine = (lane < 64) if h == 0 else (lane >= 64)
        flag = lane == (64 if h == 0 else 0)
        qa = jnp.where(mine, scaled, jnp.where(flag, 1.0, 0.0)).astype(LOW)
        qm = jnp.where(mine, q, 0.0).astype(LOW)
        gm = jnp.where(mine, wide, 0.0).astype(LOW)
        delta = jnp.sum(product[64 * h : 64 * h + 64], axis=0, keepdims=True)
        lse = lse_ref[0, pl.ds(h, 1), :]
        total = jnp.zeros((64, block), FULL)
        for c in range(rows // chunk):
            part = pl.ds(c * chunk, chunk)
            probs = jnp.exp(dot(ka[h, part, :], qa, NT) - lse)
            grad_probs = dot(va[h, part, :], g, NT)
            grad_scores = (probs * (grad_probs - delta)).astype(LOW)
            dv[part, :] += dot(probs.astype(LOW), gm, NN)
            dk[part, :] += dot(grad_scores, qm, NN)
            total = total + dot(kt[pl.ds(64 * h, 64), part], grad_scores, NN)
        columns.append(total)
    spot = pl.ds(pl.multiple_of(step * block, block), block)
    grad_ref[spot, 0:128] = (jnp.concatenate(columns, axis=0).T * SCALE).astype(LOW)

    @pl.when(step == steps - 1)
    def _():
        grad_ref[:, 128:256] = (dk[...] * SCALE).astype(LOW)
        grad_ref[:, 256:384] = dv[...].astype(LOW)


def attention_backward(counts, qkv, mixed, grad, lse, pair, block, chunk):
    rows = qkv.shape[0]
    steps = rows // block
    return pl.pallas_call(
        functools.partial(backward_kernel, rows=rows, block=block, steps=steps, chunk=chunk),
        grid_spec=pltpu.PrefetchScalarGridSpec(
            num_scalar_prefetch=1,
            grid=(steps,),
            in_specs=[
                pl.BlockSpec((block, 128), lambda i, n: (i, 3 * pair)),
                pl.BlockSpec((rows, 128), lambda i, n: (0, 3 * pair + 1)),
                pl.BlockSpec((rows, 128), lambda i, n: (0, 3 * pair + 2)),
                pl.BlockSpec((block, 128), lambda i, n: (i, pair)),
                pl.BlockSpec((block, 128), lambda i, n: (i, pair)),
                pl.BlockSpec((1, 2, block), lambda i, n: (pair, 0, i)),
            ],
            out_specs=pl.BlockSpec((rows, 384), lambda i, n: (0, 0)),
            scratch_shapes=[
                pltpu.VMEM((2, rows, 128), LOW),
                pltpu.VMEM((2, rows, 128), LOW),
                pltpu.VMEM((128, rows), LOW),
                pltpu.VMEM((rows, 128), FULL),
                pltpu.VMEM((rows, 128), FULL),
            ],
        ),
        out_shape=jax.ShapeDtypeStruct((rows, 384), LOW),
        cost_estimate=pl.CostEstimate(
            flops=20 * rows * rows * 128,
            bytes_accessed=rows * 384 * 5,
            transcendentals=2 * rows * rows,
        ),
        name="attention_backward",
    )(counts, qkv, qkv, qkv, mixed, grad, lse)


def norm_parts(values):
    center = values - jnp.mean(values, axis=-1, keepdims=True)
    inverse = lax.rsqrt(jnp.mean(center * center, axis=-1, keepdims=True) + EPSILON)
    return center * inverse, inverse


def norm_backward(upstream, unit, inverse, gain):
    scaled = upstream * gain
    first = jnp.mean(scaled, axis=-1, keepdims=True)
    second = jnp.mean(scaled * unit, axis=-1, keepdims=True)
    result = inverse * (scaled - first - unit * second)
    return result, jnp.sum(upstream * unit, axis=0), jnp.sum(upstream, axis=0)


def gelu_parts(values):
    share = 0.5 * (1.0 + lax.erf(values * (1.0 / math.sqrt(2.0))))
    density = jnp.exp(-0.5 * values * values) * (1.0 / math.sqrt(2.0 * math.pi))
    return values * share, share + values * density


def shards(
    tokens, teacher, teach_mask, lengths, deal_group,
    ln1_gain, ln1_bias, qkv_weight, out_weight, ln2_gain, ln2_bias, up_weight, down_weight,
):
    pairs, cores, depth = (lax.axis_size(name) for name in AXES)
    p, c, z = (lax.axis_index(name) for name in AXES)
    groups = pairs * cores
    slot_rows, width = tokens.shape[1], tokens.shape[2]
    rows = 2 * slot_rows
    full_len = depth * slot_rows
    seq_count = lengths.shape[0]
    ff = up_weight.shape[1]
    own_rows = width // groups
    pair_rows = cores * own_rows
    half_width = width // 2
    half_ff = ff // 2
    is_first = c == 0

    def in_order(mine, other, axis):
        return jnp.concatenate(
            [jnp.where(is_first, mine, other), jnp.where(is_first, other, mine)], axis=axis
        )

    sequence = 2 * cores * p + z
    length = jnp.sum(jnp.where(jnp.arange(seq_count) == sequence, lengths, 0))
    base = c * rows
    counts = jnp.stack([length - base, length - (rows - base)])
    counts = jnp.clip(counts, 0, rows).astype(jnp.int32)

    x_rows = turned(tokens).reshape(rows, width)

    heads_half = HEADS // 2
    head_pairs = heads_half // 2
    shard = qkv_weight.reshape(own_rows, 2, head_pairs, 2, 3, HEAD_DIM)
    shard = jnp.transpose(shard, (1, 0, 2, 4, 3, 5)).reshape(2, own_rows, 3 * half_width)
    vectors = jnp.stack([ln1_gain, ln1_bias, ln2_gain, ln2_bias], axis=1)
    vectors = jnp.pad(vectors, ((0, 0), (0, 124)))
    vectors = jnp.broadcast_to(vectors[None], (2, own_rows, 128))
    shard = jnp.concatenate([shard, vectors], axis=2)
    keep = lax.dynamic_index_in_dim(shard, c, 0, keepdims=False)
    send = lax.dynamic_index_in_dim(shard, 1 - c, 0, keepdims=False)
    w_qkv = assembled(gathered_over_pairs(in_order(keep, across_cores(send), 0)))
    vectors = w_qkv[:, 3 * half_width :].T.astype(FULL)
    w_qkv = w_qkv[:, : 3 * half_width]
    gain_one, shift_one, gain_two, shift_two = vectors[0], vectors[1], vectors[2], vectors[3]

    block = ff // groups

    def unit_blocks(part):
        return jnp.concatenate(
            [up_weight[:, (2 * q + part) * block : (2 * q + part + 1) * block] for q in range(pairs)],
            axis=1,
        )

    halves = [unit_blocks(0), unit_blocks(1)]
    keep = jnp.where(is_first, halves[0], halves[1])
    send = jnp.where(is_first, halves[1], halves[0])
    up_pieces = gathered_over_pairs(in_order(keep, across_cores(send), 0))
    down_pieces = gathered_over_pairs(down_weight)
    out_pieces = gathered_over_pairs(out_weight)

    masks = deal_group[0:2]
    group = p * cores + c
    mask_rows = jnp.pad(
        teach_mask.astype(LOW)[:, None, :], ((0, 0), (0, 15), (0, width - slot_rows))
    )
    slots = jnp.concatenate([teacher, mask_rows], axis=1)
    for level in range(groups.bit_length() - 1):
        flagged = jnp.bitwise_and(jnp.right_shift(masks[0], level), 1) == 1
        outgoing = jnp.where(flagged, slots[0], slots[1])
        incoming = across_cores(outgoing) if level == 0 else across_pairs(outgoing, 1 << (level - 1))
        slots = jnp.stack(
            [jnp.where(flagged, incoming, slots[0]), jnp.where(flagged, slots[1], incoming)]
        )
    goal = turned(slots)

    sources = jnp.bitwise_xor(group, masks) * 2 + jnp.arange(2, dtype=jnp.int32)
    picked = jnp.arange(seq_count, dtype=jnp.int32)[None, :] == sources[:, None]
    dealt_len = jnp.sum(jnp.where(picked, lengths[None, :], 0), axis=1)
    positions = z * slot_rows + jnp.arange(slot_rows, dtype=jnp.int32)
    live = (positions[None, :] < dealt_len[:, None]) & (teach_mask == 1)
    valid_count = summed_everywhere(jnp.full((8, 128), jnp.sum(live.astype(FULL))))[0, 0]

    x_full = x_rows.astype(FULL)
    unit_one, inverse_one = norm_parts(x_full)
    norm_mine = (unit_one * gain_one + shift_one).astype(LOW)
    norm_one = jnp.concatenate([norm_mine, across_cores(norm_mine)], axis=0)
    qkv = dot(norm_one, w_qkv, NN).astype(LOW)
    mixed, lse = attention_forward(counts, qkv, 512)

    flat, tree = jax.tree.flatten((up_pieces[0], down_pieces[0], out_pieces[0]))
    *flat, mixed = tied(*flat, mixed)
    up_list, down_list, out_list = jax.tree.unflatten(tree, flat)
    w_up = assembled((up_list, up_pieces[1]))
    w_down = assembled((down_list, down_pieces[1]))
    out_mine = assembled((out_list, out_pieces[1])).reshape(pairs, own_rows, width)
    out_other = across_cores(out_mine)
    w_out = jnp.stack(
        [jnp.where(is_first, out_mine, out_other), jnp.where(is_first, out_other, out_mine)], axis=1
    ).reshape(width, width)

    attended = in_order(mixed[:rows], across_cores(mixed[rows:]), 1)
    middle = x_full + dot(attended, w_out, NN)
    unit_two, inverse_two = norm_parts(middle)
    norm_two = (unit_two * gain_two + shift_two).astype(LOW)
    norm_other = across_cores(norm_two)

    def expanded(low):
        value, slope = gelu_parts(dot(low, w_up, NN))
        return value.astype(LOW), slope.astype(LOW)

    active_mine, slope_mine = expanded(norm_two)
    active_other, slope_other = expanded(norm_other)
    part_other = dot(active_other, w_down, NN).astype(LOW)
    part_mine = dot(active_mine, w_down, NN)
    output = middle + part_mine + across_cores(part_other).astype(FULL)
    activations = turned(output.astype(LOW).reshape(2, slot_rows, width))

    spots = base + jnp.arange(rows, dtype=jnp.int32)
    taught = goal[:, slot_rows, :slot_rows].reshape(rows)
    valid = ((spots < length) & (taught == 1)).astype(FULL)[:, None]
    error = output - goal[:, :slot_rows].reshape(rows, width).astype(FULL)
    squares = jnp.sum(valid * error * error)
    factor = seq_count * full_len * 1.0 / valid_count
    grad_out = valid * (2.0 * factor) * error
    grad_ff = grad_out.astype(LOW)
    grad_ff_other = across_cores(grad_ff)
    hidden_mine = (dot(grad_ff, w_down, NT) * slope_mine.astype(FULL)).astype(LOW)
    hidden_other = (dot(grad_ff_other, w_down, NT) * slope_other.astype(FULL)).astype(LOW)
    back_other = dot(hidden_other, w_up, NT).astype(LOW)
    back_got = across_cores(back_other)
    back_mine = dot(hidden_mine, w_up, NT)
    down_grad = (dot(active_mine, grad_ff, TN) + dot(active_other, grad_ff_other, TN)).astype(LOW)
    down_sum = scattered_over_pairs(down_grad)
    grad_mid, gain_two_grad, shift_two_grad = norm_backward(
        back_mine + back_got.astype(FULL), unit_two, inverse_two, gain_two
    )
    grad_middle = grad_out + grad_mid
    grad_branch = grad_middle.astype(LOW)
    grad_attended = dot(grad_branch, w_out, NT).astype(LOW)
    keep = jnp.where(is_first, grad_attended[:, :half_width], grad_attended[:, half_width:])
    send = jnp.where(is_first, grad_attended[:, half_width:], grad_attended[:, :half_width])
    grad_mixed = jnp.concatenate([keep, across_cores(send)], axis=0)
    up_grad = (dot(norm_two, hidden_mine, TN) + dot(norm_other, hidden_other, TN)).astype(LOW)
    up_sum = scattered_over_pairs(up_grad)
    out_grad = dot(attended, grad_branch, TN).astype(LOW).reshape(pairs, 2, own_rows, width)
    out_keep = lax.dynamic_index_in_dim(out_grad, c, 1, keepdims=False)
    out_send = lax.dynamic_index_in_dim(out_grad, 1 - c, 1, keepdims=False)
    out_own = (out_keep + across_cores(out_send)).reshape(pairs * own_rows, width)
    out_sum = scattered_over_pairs(out_own)

    def attend(pair, gate):
        return attention_backward(gate, qkv, mixed, grad_mixed, lse, pair, 512, 512)

    def weight_part(grads):
        return dot(norm_one, grads, TN).astype(LOW)

    low_bit, high_bit = 1, depth // 2
    *down_sum, gate = tied(*down_sum, counts)
    down_step = depth_halved(added(down_sum), low_bit)
    first = attend(0, gate)
    flat, tree = jax.tree.flatten((down_step, up_sum, out_sum))
    *flat, first, gate = tied(*flat, first, counts)
    down_step, up_sum, out_sum = jax.tree.unflatten(tree, flat)
    down_step = depth_halved(added(down_step), high_bit)
    up_step = depth_halved(added(up_sum), low_bit)
    out_step = depth_halved(added(out_sum), low_bit)
    second = attend(1, gate)
    flat, tree = jax.tree.flatten((down_step, up_step, out_step))
    *flat, second, gate = tied(*flat, second, counts)
    down_step, up_step, out_step = jax.tree.unflatten(tree, flat)
    down_own = added(down_step)
    down_got = across_depth(down_own, high_bit)
    up_step = depth_halved(added(up_step), high_bit)
    out_step = depth_halved(added(out_step), high_bit)
    early = scattered_over_pairs(weight_part(jnp.concatenate([first, second], axis=1)))
    third = attend(2, gate)
    flat, tree = jax.tree.flatten((up_step, out_step, early))
    *flat, third, down_own, down_got = tied(*flat, third, down_own, down_got)
    up_step, out_step, early = jax.tree.unflatten(tree, flat)

    partial = dot(jnp.concatenate([first, second, third], axis=1), w_qkv, NT)
    back_got = across_cores(partial[rows:].astype(LOW))
    late = scattered_over_pairs(weight_part(third))
    grad_norm_one = partial[:rows] + back_got.astype(FULL)
    grad_in, gain_one_grad, shift_one_grad = norm_backward(
        grad_norm_one, unit_one, inverse_one, gain_one
    )
    input_grad = turned((grad_middle + grad_in).astype(LOW).reshape(2, slot_rows, width))

    def finished(value):
        value = depth_doubled(value, across_depth(value, high_bit), high_bit)
        return depth_doubled(value, across_depth(value, low_bit), low_bit)

    down_own = depth_doubled(down_own, down_got, high_bit)
    down_own = depth_doubled(down_own, across_depth(down_own, low_bit), low_bit)
    up_own = finished(added(up_step))
    out_own = finished(added(out_step))
    early = finished(added(depth_halved(added(depth_halved(added(early), low_bit)), high_bit)))
    late = finished(added(depth_halved(added(depth_halved(added(late), low_bit)), high_bit)))

    small = jnp.stack(
        [
            gain_one_grad, shift_one_grad, gain_two_grad, shift_two_grad,
            jnp.full((width,), squares), jnp.zeros((width,)), jnp.zeros((width,)),
            jnp.zeros((width,)),
        ]
    )
    small = summed_everywhere(small)
    loss = small[4, 0] / (valid_count * width)
    own_small = lax.dynamic_slice_in_dim(small, group * own_rows, own_rows, 1)

    def own_block(stack, index):
        return lax.dynamic_slice_in_dim(stack, index * own_rows, own_rows, 0)

    sums = jnp.concatenate([up_own, early, late], axis=1)
    mine = own_block(sums, c)
    other = across_cores(own_block(sums, 1 - c))
    sides = [jnp.where(is_first, mine, other), jnp.where(is_first, other, mine)]
    up_own = jnp.concatenate(
        [side[:, q * block : (q + 1) * block] for q in range(pairs) for side in sides], axis=1
    )
    qkv_own = jnp.stack([side[:, half_ff:] for side in sides])
    qkv_own = qkv_own.reshape(2, own_rows, head_pairs, 3, 2, HEAD_DIM)
    qkv_own = jnp.transpose(qkv_own, (1, 0, 2, 4, 3, 5)).reshape(own_rows, 3 * width)
    return (
        activations, loss, input_grad, own_small[0], own_small[1], qkv_own.astype(FULL),
        out_own.astype(FULL), own_small[2], own_small[3], up_own.astype(FULL),
        down_own.astype(FULL),
    )


def solution(mesh):
    groups, depth = mesh.shape["dp"], mesh.shape["seq"]
    split = Mesh(mesh.devices.reshape(groups // 2, 2, depth), AXES)
    dp = ("pair", "core")
    rows3 = P(dp, "seq", None)
    in_specs = (
        rows3, rows3, P(dp, "seq"), P(), P(), P(dp), P(dp), P(dp, None), P(dp, None),
        P(dp), P(dp), P(dp, None), P(dp, None),
    )
    out_specs = (
        rows3, P(), rows3, P(dp), P(dp), P(dp, None), P(dp, None), P(dp), P(dp),
        P(dp, None), P(dp, None),
    )
    return jax.shard_map(shards, mesh=split, in_specs=in_specs, out_specs=out_specs, check_vma=False)
```

```python
import functools
import math

import jax
import jax.numpy as jnp
from jax import lax
from jax.experimental import pallas as pl
from jax.experimental.pallas import tpu as pltpu
from jax.sharding import Mesh
from jax.sharding import PartitionSpec as P

HEADS = 12
HEAD_DIM = 64
EPSILON = 1e-12
NEGATIVE = -1e30
SCALE = 1.0 / math.sqrt(HEAD_DIM)
AXES = ("pair", "core", "seq")
NT = (((1,), (1,)), ((), ()))
NN = (((1,), (0,)), ((), ()))
TN = (((0,), (0,)), ((), ()))
LOW = jnp.bfloat16
FULL = jnp.float32


def dot(left, right, form):
    return lax.dot_general(left, right, form, preferred_element_type=FULL)


def moved(value, target):
    pairs, cores, depth = (lax.axis_size(name) for name in AXES)
    links = []
    for p in range(pairs):
        for c in range(cores):
            for z in range(depth):
                q, e, w = target(p, c, z)
                links.append(((p * cores + c) * depth + z, (q * cores + e) * depth + w))
    return lax.ppermute(value, AXES, links)


def across_cores(value):
    return moved(value, lambda p, c, z: (p, 1 - c, z))


def across_pairs(value, bit):
    return moved(value, lambda p, c, z: (p ^ bit, c, z))


def across_depth(value, bit):
    return moved(value, lambda p, c, z: (p, c, z ^ bit))


def pair_bits():
    return [1 << level for level in range(lax.axis_size("pair").bit_length() - 1)]


def turned_parts(stack):
    z = lax.axis_index("seq")
    got = []
    for step in range(2):
        piece = lax.dynamic_index_in_dim(stack, (z + step) % 2, 0, keepdims=False)
        got.append(moved(piece, lambda p, c, w: (p, w // 2, 2 * c + (w + step) % 2)))
    return got


def turned_settled(got):
    even = lax.axis_index("seq") % 2 == 0
    return jnp.stack([jnp.where(even, got[0], got[1]), jnp.where(even, got[1], got[0])])


def turned(stack):
    return turned_settled(turned_parts(stack))


def sum_steps():
    depth_steps = [
        functools.partial(across_depth, bit=1 << level)
        for level in range(lax.axis_size("seq").bit_length() - 1)
    ]
    pair_steps = [functools.partial(across_pairs, bit=bit) for bit in pair_bits()]
    return depth_steps, [across_cores] + pair_steps


def gathered_over_pairs(value):
    p = lax.axis_index("pair")
    if lax.axis_size("pair") <= 4:
        return ([value] + [across_pairs(value, k) for k in range(1, lax.axis_size("pair"))], p)
    rows, width = value.shape
    bits = pair_bits()
    count = 1 << len(bits)
    halves = []
    for which in range(2):
        order = bits if which == 0 else bits[::-1]
        current = value[which * rows // 2 : (which + 1) * rows // 2]
        for bit in order:
            other = across_pairs(current, bit)
            flag = jnp.bitwise_and(p, bit) != 0
            current = jnp.stack(
                [jnp.where(flag, other, current), jnp.where(flag, current, other)]
            )
        if which == 1:
            lead = tuple(range(len(bits)))[::-1]
            current = jnp.transpose(current, lead + (len(bits), len(bits) + 1))
        halves.append(current.reshape(count, rows // 2, width))
    return ([jnp.concatenate(halves, axis=1).reshape(count * rows, width)], None)


def place_kernel(p_ref, *refs, segments, pairs, outs):
    pieces, results, done = refs[:pairs], refs[pairs : pairs + outs], refs[-1]
    copies = []
    for k in range(pairs):
        spot = jnp.bitwise_xor(p_ref[0], k)
        for index, row, rows, column, width, target in segments:
            copies.append(
                pltpu.make_async_copy(
                    pieces[k].at[pl.ds(row, rows), pl.ds(column, width)],
                    results[index].at[
                        pl.ds(pl.multiple_of(spot * rows, 16), rows), pl.ds(target, width)
                    ],
                    done.at[len(copies)],
                )
            )
    for copy in copies:
        copy.start()
    for copy in copies:
        copy.wait()


def placed(gathered, segments):
    pieces, p = gathered
    pairs = lax.axis_size("pair")
    outs = 1 + max(segment[0] for segment in segments)
    if p is None:
        stack = pieces[0].reshape(pairs, -1, pieces[0].shape[1])
        results = []
        for index in range(outs):
            parts = [
                stack[:, row : row + rows, column : column + width].reshape(pairs * rows, width)
                for which, row, rows, column, width, _ in segments
                if which == index
            ]
            results.append(jnp.concatenate(parts, axis=1))
        return results
    shapes = []
    for index in range(outs):
        mine = [segment for segment in segments if segment[0] == index]
        shapes.append(
            jax.ShapeDtypeStruct((pairs * mine[0][2], sum(part[4] for part in mine)), LOW)
        )
    anywhere = pl.BlockSpec(memory_space=pl.ANY)
    return pl.pallas_call(
        functools.partial(place_kernel, segments=segments, pairs=pairs, outs=outs),
        in_specs=[pl.BlockSpec(memory_space=pltpu.SMEM)] + [anywhere] * pairs,
        out_specs=[anywhere] * outs,
        out_shape=shapes,
        scratch_shapes=[pltpu.SemaphoreType.DMA((pairs * len(segments),))],
        name="place",
    )(p.astype(jnp.int32).reshape(1), *pieces)


def scattered_over_pairs(value):
    p = lax.axis_index("pair")
    if lax.axis_size("pair") <= 4:
        rows = value.shape[0] // lax.axis_size("pair")
        pieces = []
        for k in range(lax.axis_size("pair")):
            piece = lax.dynamic_slice_in_dim(value, jnp.bitwise_xor(p, k) * rows, rows, 0)
            pieces.append(across_pairs(piece, k) if k else piece)
        return pieces
    bits = pair_bits()
    count = 1 << len(bits)
    rows, width = value.shape[0] // count, value.shape[1]
    blocks = value.reshape(count, rows, width)
    halves = []
    for which in range(2):
        order = bits if which == 0 else bits[::-1]
        current = blocks[:, which * rows // 2 : (which + 1) * rows // 2]
        current = current.reshape((2,) * len(bits) + (rows // 2, width))
        left = bits[::-1]
        for bit in order:
            axis = left.index(bit)
            mine = jnp.where(jnp.bitwise_and(p, bit) != 0, 1, 0)
            keep = lax.dynamic_index_in_dim(current, mine, axis, keepdims=False)
            send = lax.dynamic_index_in_dim(current, 1 - mine, axis, keepdims=False)
            current = keep + across_pairs(send, bit)
            left = [other for other in left if other != bit]
        halves.append(current)
    return [jnp.concatenate(halves, axis=0)]


def added(pieces):
    total = pieces[0].astype(FULL)
    for piece in pieces[1:]:
        total = total + piece.astype(FULL)
    return total.astype(LOW)


def depth_flag(bit):
    return jnp.where(jnp.bitwise_and(lax.axis_index("seq"), bit) != 0, 1, 0)


def depth_halved(value, bit):
    mine = depth_flag(bit)
    parts = value.reshape((2, value.shape[0] // 2) + value.shape[1:])
    keep = lax.dynamic_index_in_dim(parts, mine, 0, keepdims=False)
    send = lax.dynamic_index_in_dim(parts, 1 - mine, 0, keepdims=False)
    return [keep, across_depth(send, bit)]


def depth_doubled(value, other, bit):
    mine = depth_flag(bit)
    return jnp.concatenate(
        [jnp.where(mine == 0, value, other), jnp.where(mine == 0, other, value)], axis=0
    )


def tied(*values):
    return lax.optimization_barrier(values)


def keys_with_mask(k_ref, counts_ref, ka, rows):
    lane = lax.broadcasted_iota(jnp.int32, (rows, 128), 1)
    spot = lax.broadcasted_iota(jnp.int32, (rows, 128), 0)
    limit = jnp.where(spot < rows // 2, counts_ref[0], counts_ref[1] + rows // 2)
    bias = jnp.where(spot < limit, 0.0, NEGATIVE)
    k = k_ref[...].astype(FULL)
    ka[0] = jnp.where(lane < 64, k, jnp.where(lane == 64, bias, 0.0)).astype(LOW)
    ka[1] = jnp.where(lane >= 64, k, jnp.where(lane == 0, bias, 0.0)).astype(LOW)


def forward_kernel(counts_ref, q_ref, k_ref, v_ref, o_ref, lse_ref, ka, vt, *, rows, block):
    @pl.when(pl.program_id(1) == 0)
    def _():
        keys_with_mask(k_ref, counts_ref, ka, rows)
        vt[...] = v_ref[...].T

    lane = lax.broadcasted_iota(jnp.int32, (block, 128), 1)
    q = q_ref[...].astype(FULL) * SCALE
    mixed = []
    for h in range(2):
        mine = (lane < 64) if h == 0 else (lane >= 64)
        flag = lane == (64 if h == 0 else 0)
        qa = jnp.where(mine, q, jnp.where(flag, 1.0, 0.0)).astype(LOW)
        scores = dot(ka[h], qa, NT)
        highest = jnp.max(scores, axis=0, keepdims=True)
        exponent = jnp.exp(scores - highest)
        totals = jnp.sum(exponent, axis=0, keepdims=True)
        part = dot(vt[pl.ds(64 * h, 64), :], exponent.astype(LOW), NN)
        mixed.append(part * (1.0 / totals))
        lse_ref[0, pl.ds(h, 1), :] = highest + jnp.log(totals)
    o_ref[...] = jnp.concatenate(mixed, axis=0).T.astype(LOW)


def attention_forward(counts, qkv, block):
    rows, width = qkv.shape
    pairs = width // 384
    return pl.pallas_call(
        functools.partial(forward_kernel, rows=rows, block=block),
        grid_spec=pltpu.PrefetchScalarGridSpec(
            num_scalar_prefetch=1,
            grid=(pairs, rows // block),
            in_specs=[
                pl.BlockSpec((block, 128), lambda h, i, n: (i, 3 * h)),
                pl.BlockSpec((rows, 128), lambda h, i, n: (0, 3 * h + 1)),
                pl.BlockSpec((rows, 128), lambda h, i, n: (0, 3 * h + 2)),
            ],
            out_specs=[
                pl.BlockSpec((block, 128), lambda h, i, n: (i, h)),
                pl.BlockSpec((1, 2, block), lambda h, i, n: (h, 0, i)),
            ],
            scratch_shapes=[pltpu.VMEM((2, rows, 128), LOW), pltpu.VMEM((128, rows), LOW)],
        ),
        out_shape=[
            jax.ShapeDtypeStruct((rows, pairs * 128), LOW),
            jax.ShapeDtypeStruct((pairs, 2, rows), FULL),
        ],
        cost_estimate=pl.CostEstimate(flops=1, bytes_accessed=1, transcendentals=0),
        name="attention_forward",
    )(counts, qkv, qkv, qkv)


def backward_kernel(
    counts_ref, q_ref, k_ref, v_ref, o_ref, g_ref, lse_ref, grad_ref,
    ka, va, kt, dk, dv, *, rows, block, steps, chunk,
):
    step = pl.program_id(0)

    @pl.when(step == 0)
    def _():
        keys_with_mask(k_ref, counts_ref, ka, rows)
        lane = lax.broadcasted_iota(jnp.int32, (rows, 128), 1)
        v = v_ref[...].astype(FULL)
        va[0] = jnp.where(lane < 64, v, 0.0).astype(LOW)
        va[1] = jnp.where(lane >= 64, v, 0.0).astype(LOW)
        kt[...] = k_ref[...].T
        dk[...] = jnp.zeros_like(dk)
        dv[...] = jnp.zeros_like(dv)

    lane = lax.broadcasted_iota(jnp.int32, (block, 128), 1)
    q = q_ref[...].astype(FULL)
    g = g_ref[...]
    wide = g.astype(FULL)
    product = (wide * o_ref[...].astype(FULL)).T
    scaled = q * SCALE
    columns = []
    for h in range(2):
        mine = (lane < 64) if h == 0 else (lane >= 64)
        flag = lane == (64 if h == 0 else 0)
        qa = jnp.where(mine, scaled, jnp.where(flag, 1.0, 0.0)).astype(LOW)
        qm = jnp.where(mine, q, 0.0).astype(LOW)
        gm = jnp.where(mine, wide, 0.0).astype(LOW)
        delta = jnp.sum(product[64 * h : 64 * h + 64], axis=0, keepdims=True)
        lse = lse_ref[0, pl.ds(h, 1), :]
        total = jnp.zeros((64, block), FULL)
        for c in range(rows // chunk):
            part = pl.ds(c * chunk, chunk)
            probs = jnp.exp(dot(ka[h, part, :], qa, NT) - lse)
            grad_probs = dot(va[h, part, :], g, NT)
            grad_scores = (probs * (grad_probs - delta)).astype(LOW)
            dv[part, :] += dot(probs.astype(LOW), gm, NN)
            dk[part, :] += dot(grad_scores, qm, NN)
            total = total + dot(kt[pl.ds(64 * h, 64), part], grad_scores, NN)
        columns.append(total)
    spot = pl.ds(pl.multiple_of(step * block, block), block)
    grad_ref[spot, 0:128] = (jnp.concatenate(columns, axis=0).T * SCALE).astype(LOW)

    @pl.when(step == steps - 1)
    def _():
        grad_ref[:, 128:256] = (dk[...] * SCALE).astype(LOW)
        grad_ref[:, 256:384] = dv[...].astype(LOW)


def attention_backward(counts, qkv, mixed, grad, lse, pair, block, chunk):
    rows = qkv.shape[0]
    steps = rows // block
    return pl.pallas_call(
        functools.partial(backward_kernel, rows=rows, block=block, steps=steps, chunk=chunk),
        grid_spec=pltpu.PrefetchScalarGridSpec(
            num_scalar_prefetch=1,
            grid=(steps,),
            in_specs=[
                pl.BlockSpec((block, 128), lambda i, n: (i, 3 * pair)),
                pl.BlockSpec((rows, 128), lambda i, n: (0, 3 * pair + 1)),
                pl.BlockSpec((rows, 128), lambda i, n: (0, 3 * pair + 2)),
                pl.BlockSpec((block, 128), lambda i, n: (i, pair)),
                pl.BlockSpec((block, 128), lambda i, n: (i, pair)),
                pl.BlockSpec((1, 2, block), lambda i, n: (pair, 0, i)),
            ],
            out_specs=pl.BlockSpec((rows, 384), lambda i, n: (0, 0)),
            scratch_shapes=[
                pltpu.VMEM((2, rows, 128), LOW),
                pltpu.VMEM((2, rows, 128), LOW),
                pltpu.VMEM((128, rows), LOW),
                pltpu.VMEM((rows, 128), FULL),
                pltpu.VMEM((rows, 128), FULL),
            ],
        ),
        out_shape=jax.ShapeDtypeStruct((rows, 384), LOW),
        cost_estimate=pl.CostEstimate(flops=1, bytes_accessed=1, transcendentals=0),
        name="attention_backward",
    )(counts, qkv, qkv, qkv, mixed, grad, lse)


def norm_parts(values):
    center = values - jnp.mean(values, axis=-1, keepdims=True)
    inverse = lax.rsqrt(jnp.mean(center * center, axis=-1, keepdims=True) + EPSILON)
    return center * inverse, inverse


def norm_backward(upstream, unit, inverse, gain):
    scaled = upstream * gain
    first = jnp.mean(scaled, axis=-1, keepdims=True)
    second = jnp.mean(scaled * unit, axis=-1, keepdims=True)
    result = inverse * (scaled - first - unit * second)
    return result, jnp.sum(upstream * unit, axis=0), jnp.sum(upstream, axis=0)


def gelu_parts(values):
    share = 0.5 * (1.0 + lax.erf(values * (1.0 / math.sqrt(2.0))))
    density = jnp.exp(-0.5 * values * values) * (1.0 / math.sqrt(2.0 * math.pi))
    return values * share, share + values * density


def shards(
    tokens, teacher, teach_mask, lengths, deal_group,
    ln1_gain, ln1_bias, qkv_weight, out_weight, ln2_gain, ln2_bias, up_weight, down_weight,
):
    pairs, cores, depth = (lax.axis_size(name) for name in AXES)
    p, c, z = (lax.axis_index(name) for name in AXES)
    groups = pairs * cores
    slot_rows, width = tokens.shape[1], tokens.shape[2]
    rows = 2 * slot_rows
    full_len = depth * slot_rows
    seq_count = lengths.shape[0]
    ff = up_weight.shape[1]
    own_rows = width // groups
    pair_rows = cores * own_rows
    half_width = width // 2
    half_ff = ff // 2
    is_first = c == 0

    def in_order(mine, other, axis):
        return jnp.concatenate(
            [jnp.where(is_first, mine, other), jnp.where(is_first, other, mine)], axis=axis
        )

    sequence = 2 * cores * p + z
    length = jnp.sum(jnp.where(jnp.arange(seq_count) == sequence, lengths, 0))
    base = c * rows
    counts = jnp.stack([length - base, length - (rows - base)])
    counts = jnp.clip(counts, 0, rows).astype(jnp.int32)

    heads_half = HEADS // 2
    head_pairs = heads_half // 2
    wide_half = 3 * half_width
    shard = qkv_weight.reshape(own_rows, 2, head_pairs, 2, 3, HEAD_DIM)
    shard = jnp.transpose(shard, (1, 0, 2, 4, 3, 5)).reshape(2, own_rows, wide_half)
    vectors = jnp.stack([ln1_gain, ln1_bias, ln2_gain, ln2_bias], axis=1)
    vectors = jnp.pad(vectors, ((0, 0), (0, 124)))
    vectors = jnp.broadcast_to(vectors[None], (2, own_rows, 128))
    shard = jnp.concatenate([shard, vectors], axis=2)
    keep = lax.dynamic_index_in_dim(shard, c, 0, keepdims=False)
    send = lax.dynamic_index_in_dim(shard, 1 - c, 0, keepdims=False)
    qkv_shard = in_order(keep, across_cores(send), 0)
    qkv_pieces = gathered_over_pairs(qkv_shard)

    x_rows = turned(tokens).reshape(rows, width)

    masks = deal_group[0:2]
    group = p * cores + c
    sources = jnp.bitwise_xor(group, masks) * 2 + jnp.arange(2, dtype=jnp.int32)
    picked = jnp.arange(seq_count, dtype=jnp.int32)[None, :] == sources[:, None]
    dealt_len = jnp.sum(jnp.where(picked, lengths[None, :], 0), axis=1)
    positions = z * slot_rows + jnp.arange(slot_rows, dtype=jnp.int32)
    live = (positions[None, :] < dealt_len[:, None]) & (teach_mask == 1)
    tally = jnp.full((8, 128), jnp.sum(live.astype(FULL)))
    tally = tally + across_cores(tally)

    mask_rows = jnp.pad(
        teach_mask.astype(LOW)[:, None, :], ((0, 0), (0, 15), (0, width - slot_rows))
    )
    slots = jnp.concatenate([teacher, mask_rows], axis=1)

    def dealt(slots, level):
        flagged = jnp.bitwise_and(jnp.right_shift(masks[0], level), 1) == 1
        outgoing = jnp.where(flagged, slots[0], slots[1])
        incoming = across_cores(outgoing) if level == 0 else across_pairs(outgoing, 1 << (level - 1))
        return [flagged, slots, incoming]

    def settled(flagged, slots, incoming):
        return jnp.stack(
            [jnp.where(flagged, incoming, slots[0]), jnp.where(flagged, slots[1], incoming)]
        )

    levels = groups.bit_length() - 1
    deal = dealt(slots, 0)

    block = ff // groups

    def unit_blocks(part):
        return jnp.concatenate(
            [up_weight[:, (2 * q + part) * block : (2 * q + part + 1) * block] for q in range(pairs)],
            axis=1,
        )

    up_parts = [unit_blocks(0), unit_blocks(1)]
    keep = jnp.where(is_first, up_parts[0], up_parts[1])
    send = jnp.where(is_first, up_parts[1], up_parts[0])
    got = across_cores(jnp.concatenate([send[:, :width], send[:, width:], out_weight], axis=0))
    up_shard = in_order(keep, jnp.concatenate([got[:own_rows], got[own_rows : 2 * own_rows]], axis=1), 0)
    out_shard = in_order(out_weight, got[2 * own_rows :], 0)
    payload = jnp.concatenate(
        [down_weight, up_shard[:, :width], up_shard[:, width:], out_shard], axis=0
    )
    down_rows = down_weight.shape[0]
    payload_plan = (
        (0, 0, down_rows, 0, width, 0),
        (1, down_rows, pair_rows, 0, width, 0),
        (1, down_rows + pair_rows, pair_rows, 0, width, width),
        (2, down_rows + 2 * pair_rows, pair_rows, 0, width, 0),
    )
    deal, tally = tied(deal, tally)
    x_rows, payload = tied(x_rows, payload)
    tally_steps = sum_steps()
    tally = tally + tally_steps[1][1](tally)
    deal = dealt(settled(*deal), 1)
    payload_pieces = gathered_over_pairs(payload)

    x_full = x_rows.astype(FULL)
    unit_one, inverse_one = norm_parts(x_full)
    w_qkv, vectors = placed(
        qkv_pieces,
        ((0, 0, pair_rows, 0, wide_half, 0), (1, 0, pair_rows, wide_half, 128, 0)),
    )
    pick = lax.broadcasted_iota(jnp.int32, (8, 128), 0) == lax.broadcasted_iota(jnp.int32, (8, 128), 1)
    vectors = dot(pick.astype(LOW), vectors, NT)
    gain_one, shift_one, gain_two, shift_two = vectors[0], vectors[1], vectors[2], vectors[3]
    norm_mine = (unit_one * gain_one + shift_one).astype(LOW)
    norm_one = jnp.concatenate([norm_mine, across_cores(norm_mine)], axis=0)
    norm_one, tally = tied(norm_one, tally)
    for step in tally_steps[1][2:]:
        tally = tally + step(tally)
    qkv = dot(norm_one, w_qkv, NN).astype(LOW)
    qkv, deal, tally = tied(qkv, deal, tally)
    for level in range(2, levels):
        deal = dealt(settled(*deal), level)
    tally = tally + tally_steps[0][0](tally)
    mixed, lse = attention_forward(counts, qkv, 512)

    mixed, payload_pieces, deal, tally = tied(mixed, payload_pieces, deal, tally)
    mixed_got = across_cores(mixed[rows:])
    goal = turned(settled(*deal))
    for step in tally_steps[0][1:]:
        tally = tally + step(tally)
    w_down, w_up, w_out = placed(payload_pieces, payload_plan)

    attended = in_order(mixed[:rows], mixed_got, 1)
    middle = x_full + dot(attended, w_out, NN)
    unit_two, inverse_two = norm_parts(middle)
    norm_two = (unit_two * gain_two + shift_two).astype(LOW)
    norm_other = across_cores(norm_two)

    def expanded(low):
        value, slope = gelu_parts(dot(low, w_up, NN))
        return value.astype(LOW), slope.astype(LOW)

    active_mine, slope_mine = expanded(norm_two)
    active_other, slope_other = expanded(norm_other)
    part_other = dot(active_other, w_down, NN).astype(LOW)
    part_mine = dot(active_mine, w_down, NN)
    output = middle + part_mine + across_cores(part_other).astype(FULL)

    output, goal, tally = tied(output, goal, tally)
    valid_count = tally[0, 0]
    spots = base + jnp.arange(rows, dtype=jnp.int32)
    taught = goal[:, slot_rows, :slot_rows].reshape(rows)
    valid = ((spots < length) & (taught == 1)).astype(FULL)[:, None]
    error = output - goal[:, :slot_rows].reshape(rows, width).astype(FULL)
    squares = jnp.sum(valid * error * error)
    factor = seq_count * full_len * 1.0 / valid_count
    grad_out = valid * (2.0 * factor) * error
    grad_ff = grad_out.astype(LOW)
    grad_ff_other = across_cores(grad_ff)
    output_moved = turned_parts(output.astype(LOW).reshape(2, slot_rows, width))
    hidden_mine = (dot(grad_ff, w_down, NT) * slope_mine.astype(FULL)).astype(LOW)
    down_grad = (dot(active_mine, grad_ff, TN) + dot(active_other, grad_ff_other, TN)).astype(LOW)
    down_grad, grad_ff_other, hidden_mine = tied(down_grad, grad_ff_other, hidden_mine)
    down_sum = scattered_over_pairs(down_grad)
    hidden_other = (dot(grad_ff_other, w_down, NT) * slope_other.astype(FULL)).astype(LOW)
    back_other = dot(hidden_other, w_up, NT).astype(LOW)
    back_got = across_cores(back_other)
    back_mine = dot(hidden_mine, w_up, NT)
    up_grad = (dot(norm_two, hidden_mine, TN) + dot(norm_other, hidden_other, TN)).astype(LOW)
    grad_mid, gain_two_grad, shift_two_grad = norm_backward(
        back_mine + back_got.astype(FULL), unit_two, inverse_two, gain_two
    )
    grad_middle = grad_out + grad_mid
    grad_branch = grad_middle.astype(LOW)
    grad_attended = dot(grad_branch, w_out, NT).astype(LOW)
    keep = jnp.where(is_first, grad_attended[:, :half_width], grad_attended[:, half_width:])
    send = jnp.where(is_first, grad_attended[:, half_width:], grad_attended[:, :half_width])
    mixed_grad_got = across_cores(send)
    out_grad = dot(attended, grad_branch, TN).astype(LOW)
    rest_sum = scattered_over_pairs(jnp.concatenate([up_grad, out_grad], axis=1))
    grad_mixed = jnp.concatenate([keep, mixed_grad_got], axis=0)

    def attend(pair, gate):
        return attention_backward(gate, qkv, mixed, grad_mixed, lse, pair, 512, 512)

    def weight_part(grads):
        return dot(norm_one, grads, TN).astype(LOW)

    low_bit, high_bit = 1, depth // 2
    first = attend(0, counts)
    first, down_sum, output_moved, gate = tied(first, down_sum, output_moved, counts)
    activations = turned_settled(output_moved)
    down_step = depth_halved(added(down_sum), low_bit)
    second = attend(1, gate)
    second, first, down_step, rest_sum, gate = tied(second, first, down_step, rest_sum, counts)
    down_step = depth_halved(added(down_step), high_bit)
    rest_step = depth_halved(added(rest_sum), low_bit)
    early = scattered_over_pairs(weight_part(jnp.concatenate([first, second], axis=1)))
    third = attend(2, gate)
    third, first, second, down_step, rest_step, early = tied(
        third, first, second, down_step, rest_step, early
    )

    partial = dot(jnp.concatenate([first, second, third], axis=1), w_qkv, NT)
    back_got = across_cores(partial[rows:].astype(LOW))
    late = scattered_over_pairs(weight_part(third))
    down_own = added(down_step)
    down_got = across_depth(down_own, high_bit)
    rest_step = depth_halved(added(rest_step), high_bit)
    early = added(early)
    grad_norm_one = partial[:rows] + back_got.astype(FULL)
    grad_in, gain_one_grad, shift_one_grad = norm_backward(
        grad_norm_one, unit_one, inverse_one, gain_one
    )
    grad_rows = (grad_middle + grad_in).astype(LOW)

    row_index = lax.broadcasted_iota(jnp.int32, (8, width), 0)
    small = jnp.zeros((8, width), FULL)
    for index, value in enumerate(
        [gain_one_grad, shift_one_grad, gain_two_grad, shift_two_grad, jnp.full((width,), squares)]
    ):
        small = jnp.where(row_index == index, value[None, :], small)
    depth_steps, plane_steps = sum_steps()
    for step in depth_steps:
        small = small + step(small)
    grad_rows, small, down_got, rest_step, late = tied(grad_rows, small, down_got, rest_step, late)
    input_moved = turned_parts(grad_rows.reshape(2, slot_rows, width))

    qkv_step = depth_halved(jnp.concatenate([early, added(late)], axis=1), low_bit)
    down_own = depth_doubled(down_own, down_got, high_bit)
    down_got = across_depth(down_own, low_bit)
    rest_own = added(rest_step)
    rest_got = across_depth(rest_own, high_bit)
    small = small + plane_steps[0](small)
    qkv_step, down_got, rest_got, small = tied(qkv_step, down_got, rest_got, small)
    qkv_step = depth_halved(added(qkv_step), high_bit)
    rest_own = depth_doubled(rest_own, rest_got, high_bit)
    rest_got = across_depth(rest_own, low_bit)
    small = small + plane_steps[1](small)
    down_own = depth_doubled(down_own, down_got, low_bit)
    qkv_step, rest_got, small = tied(qkv_step, rest_got, small)
    qkv_own = added(qkv_step)
    qkv_got = across_depth(qkv_own, high_bit)
    rest_own = depth_doubled(rest_own, rest_got, low_bit)

    def own_block(stack, index):
        return lax.dynamic_slice_in_dim(stack, index * own_rows, own_rows, 0)

    rest_mine = own_block(rest_own, c)
    rest_other = across_cores(own_block(rest_own, 1 - c))
    for step in plane_steps[2:]:
        small = small + step(small)
    qkv_got, rest_other, small = tied(qkv_got, rest_other, small)
    qkv_own = depth_doubled(qkv_own, qkv_got, high_bit)
    qkv_own = depth_doubled(qkv_own, across_depth(qkv_own, low_bit), low_bit)
    qkv_mine = own_block(qkv_own, c)
    qkv_other = across_cores(own_block(qkv_own, 1 - c))
    qkv_other, input_moved = tied(qkv_other, input_moved)
    input_grad = turned_settled(input_moved)

    loss = small[4, 0] / (valid_count * width)
    own_small = lax.dynamic_slice_in_dim(small, group * own_rows, own_rows, 1)
    out_own = rest_mine[:, half_ff:].astype(FULL) + rest_other[:, half_ff:].astype(FULL)
    sides = [jnp.where(is_first, rest_mine, rest_other), jnp.where(is_first, rest_other, rest_mine)]
    up_own = jnp.concatenate(
        [side[:, q * block : (q + 1) * block] for q in range(pairs) for side in sides], axis=1
    )
    qkv_own = jnp.stack(
        [jnp.where(is_first, qkv_mine, qkv_other), jnp.where(is_first, qkv_other, qkv_mine)]
    )
    qkv_own = qkv_own.reshape(2, own_rows, head_pairs, 3, 2, HEAD_DIM)
    qkv_own = jnp.transpose(qkv_own, (1, 0, 2, 4, 3, 5)).reshape(own_rows, 3 * width)
    return (
        activations, loss, input_grad, own_small[0], own_small[1], qkv_own.astype(FULL),
        out_own, own_small[2], own_small[3], up_own.astype(FULL), down_own.astype(FULL),
    )


def solution(mesh):
    groups, depth = mesh.shape["dp"], mesh.shape["seq"]
    split = Mesh(mesh.devices.reshape(groups // 2, 2, depth), AXES)
    dp = ("pair", "core")
    rows3 = P(dp, "seq", None)
    in_specs = (
        rows3, rows3, P(dp, "seq"), P(), P(), P(dp), P(dp), P(dp, None), P(dp, None),
        P(dp), P(dp), P(dp, None), P(dp, None),
    )
    out_specs = (
        rows3, P(), rows3, P(dp), P(dp), P(dp, None), P(dp, None), P(dp), P(dp),
        P(dp, None), P(dp, None),
    )
    return jax.shard_map(shards, mesh=split, in_specs=in_specs, out_specs=out_specs, check_vma=False)
```

```python
import functools
import math

import jax
import jax.numpy as jnp
from jax import lax
from jax.experimental import pallas as pl
from jax.experimental.layout import Layout, with_layout_constraint
from jax.experimental.pallas import tpu as pltpu
from jax.sharding import Mesh
from jax.sharding import PartitionSpec as P

HEADS = 12
HEAD_DIM = 64
EPSILON = 1e-12
NEGATIVE = -1e30
SCALE = 1.0 / math.sqrt(HEAD_DIM)
AXES = ("pair", "core", "seq")
NT = (((1,), (1,)), ((), ()))
NN = (((1,), (0,)), ((), ()))
TN = (((0,), (0,)), ((), ()))
LOW = jnp.bfloat16
FULL = jnp.float32


def dot(left, right, form):
    return lax.dot_general(left, right, form, preferred_element_type=FULL)


def row_major(value):
    return with_layout_constraint(value, Layout(major_to_minor=tuple(range(value.ndim))))


def moved(value, target):
    pairs, cores, depth = (lax.axis_size(name) for name in AXES)
    links = []
    for p in range(pairs):
        for c in range(cores):
            for z in range(depth):
                q, e, w = target(p, c, z)
                links.append(((p * cores + c) * depth + z, (q * cores + e) * depth + w))
    return lax.ppermute(value, AXES, links)


def across_cores(value):
    return moved(value, lambda p, c, z: (p, 1 - c, z))


def across_pairs(value, bit):
    return moved(value, lambda p, c, z: (p ^ bit, c, z))


def across_depth(value, bit):
    return moved(value, lambda p, c, z: (p, c, z ^ bit))


def pair_bits():
    return [1 << level for level in range(lax.axis_size("pair").bit_length() - 1)]


def turned_parts(stack):
    z = lax.axis_index("seq")
    got = []
    for step in range(2):
        piece = lax.dynamic_index_in_dim(stack, (z + step) % 2, 0, keepdims=False)
        got.append(moved(piece, lambda p, c, w: (p, w // 2, 2 * c + (w + step) % 2)))
    return got


def turned_settled(got):
    even = lax.axis_index("seq") % 2 == 0
    return jnp.stack([jnp.where(even, got[0], got[1]), jnp.where(even, got[1], got[0])])


def turned(stack):
    return turned_settled(turned_parts(stack))


def sum_steps():
    depth_steps = [
        functools.partial(across_depth, bit=1 << level)
        for level in range(lax.axis_size("seq").bit_length() - 1)
    ]
    pair_steps = [functools.partial(across_pairs, bit=bit) for bit in pair_bits()]
    return depth_steps, [across_cores] + pair_steps


def gathered_over_pairs(value):
    p = lax.axis_index("pair")
    if lax.axis_size("pair") <= 4:
        count = lax.axis_size("pair")
        layout = tuple((k, k, 0, 0, value.shape[0]) for k in range(count))
        return [value] + [across_pairs(value, k) for k in range(1, count)], p, layout
    rows, width = value.shape
    bits = pair_bits()
    count = 1 << len(bits)
    halves = []
    for which in range(2):
        order = bits if which == 0 else bits[::-1]
        current = value[which * rows // 2 : (which + 1) * rows // 2]
        for bit in order:
            other = across_pairs(current, bit)
            flag = jnp.bitwise_and(p, bit) != 0
            current = jnp.stack(
                [jnp.where(flag, other, current), jnp.where(flag, current, other)]
            )
        if which == 1:
            lead = tuple(range(len(bits)))[::-1]
            current = jnp.transpose(current, lead + (len(bits), len(bits) + 1))
        halves.append(current.reshape(count, rows // 2, width))
    return [jnp.concatenate(halves, axis=1).reshape(count * rows, width)], None, ()


def halves_first(value):
    if lax.axis_size("pair") != 4:
        return value, None
    rows = value.shape[0] // 2
    return value, (across_pairs(value[:rows], 1), across_pairs(value[rows:], 2))


def halves_second(state):
    value, near = state
    if near is None:
        return gathered_over_pairs(value)
    rows = value.shape[0] // 2
    upper = across_pairs(jnp.concatenate([value[:rows], near[0]], axis=0), 2)
    lower = across_pairs(jnp.concatenate([value[rows:], near[1]], axis=0), 1)
    layout = (
        (0, 0, 0, 0, 2 * rows),
        (1, 1, 0, 0, rows), (1, 4, 0, rows, rows),
        (2, 3, 0, 0, rows), (2, 2, 0, rows, rows),
        (3, 3, rows, 0, rows), (3, 4, rows, rows, rows),
    )
    return [value, near[0], near[1], upper, lower], lax.axis_index("pair"), layout


def place_kernel(p_ref, *refs, segments, layout, count):
    sources, results = refs[:count], refs[count:]
    for k, source, origin, first, size in layout:
        spot = jnp.bitwise_xor(p_ref[0], k)
        for index, row, rows, column, width, target in segments:
            low, high = max(row, first), min(row + rows, first + size)
            if low < high:
                start = pl.multiple_of(spot * rows + (low - row), 16)
                results[index][pl.ds(start, high - low), target : target + width] = sources[source][
                    low - first + origin : high - first + origin, column : column + width
                ]


def placed(gathered, segments):
    pieces, p, layout = gathered
    pairs = lax.axis_size("pair")
    outs = 1 + max(segment[0] for segment in segments)
    if p is None:
        stack = pieces[0].reshape(pairs, -1, pieces[0].shape[1])
        results = []
        for index in range(outs):
            parts = [
                stack[:, row : row + rows, column : column + width].reshape(pairs * rows, width)
                for which, row, rows, column, width, _ in segments
                if which == index
            ]
            results.append(jnp.concatenate(parts, axis=1))
        return results
    shapes = []
    for index in range(outs):
        mine = [segment for segment in segments if segment[0] == index]
        shapes.append(
            jax.ShapeDtypeStruct((pairs * mine[0][2], sum(part[4] for part in mine)), LOW)
        )
    local = pl.BlockSpec(memory_space=pltpu.VMEM)
    return pl.pallas_call(
        functools.partial(place_kernel, segments=segments, layout=layout, count=len(pieces)),
        in_specs=[pl.BlockSpec(memory_space=pltpu.SMEM)] + [local] * len(pieces),
        out_specs=[local] * outs,
        out_shape=shapes,
        name="place",
    )(p.astype(jnp.int32).reshape(1), *pieces)


def scattered_over_pairs(value):
    p = lax.axis_index("pair")
    if lax.axis_size("pair") <= 4:
        rows = value.shape[0] // lax.axis_size("pair")
        pieces = []
        for k in range(lax.axis_size("pair")):
            piece = lax.dynamic_slice_in_dim(value, jnp.bitwise_xor(p, k) * rows, rows, 0)
            pieces.append(across_pairs(piece, k) if k else piece)
        return pieces
    bits = pair_bits()
    count = 1 << len(bits)
    rows, width = value.shape[0] // count, value.shape[1]
    blocks = value.reshape(count, rows, width)
    halves = []
    for which in range(2):
        order = bits if which == 0 else bits[::-1]
        current = blocks[:, which * rows // 2 : (which + 1) * rows // 2]
        current = current.reshape((2,) * len(bits) + (rows // 2, width))
        left = bits[::-1]
        for bit in order:
            axis = left.index(bit)
            mine = jnp.where(jnp.bitwise_and(p, bit) != 0, 1, 0)
            keep = lax.dynamic_index_in_dim(current, mine, axis, keepdims=False)
            send = lax.dynamic_index_in_dim(current, 1 - mine, axis, keepdims=False)
            current = keep + across_pairs(send, bit)
            left = [other for other in left if other != bit]
        halves.append(current)
    return [jnp.concatenate(halves, axis=0)]


def added(pieces):
    total = pieces[0].astype(FULL)
    for piece in pieces[1:]:
        total = total + piece.astype(FULL)
    return total.astype(LOW)


def depth_flag(bit):
    return jnp.where(jnp.bitwise_and(lax.axis_index("seq"), bit) != 0, 1, 0)


def depth_halved(value, bit):
    mine = depth_flag(bit)
    parts = value.reshape((2, value.shape[0] // 2) + value.shape[1:])
    keep = lax.dynamic_index_in_dim(parts, mine, 0, keepdims=False)
    send = lax.dynamic_index_in_dim(parts, 1 - mine, 0, keepdims=False)
    return [keep, across_depth(send, bit)]


def depth_doubled(value, other, bit):
    mine = depth_flag(bit)
    return jnp.concatenate(
        [jnp.where(mine == 0, value, other), jnp.where(mine == 0, other, value)], axis=0
    )


def tied(*values):
    return lax.optimization_barrier(values)


def keys_with_mask(k_ref, counts_ref, ka, rows):
    lane = lax.broadcasted_iota(jnp.int32, (rows, 128), 1)
    spot = lax.broadcasted_iota(jnp.int32, (rows, 128), 0)
    limit = jnp.where(spot < rows // 2, counts_ref[0], counts_ref[1] + rows // 2)
    bias = jnp.where(spot < limit, 0.0, NEGATIVE)
    k = k_ref[...].astype(FULL)
    ka[0] = jnp.where(lane < 64, k, jnp.where(lane == 64, bias, 0.0)).astype(LOW)
    ka[1] = jnp.where(lane >= 64, k, jnp.where(lane == 0, bias, 0.0)).astype(LOW)


def forward_kernel(counts_ref, q_ref, k_ref, v_ref, o_ref, lse_ref, ka, vt, *, rows, block):
    @pl.when(pl.program_id(1) == 0)
    def _():
        keys_with_mask(k_ref, counts_ref, ka, rows)
        vt[...] = v_ref[...].T

    lane = lax.broadcasted_iota(jnp.int32, (block, 128), 1)
    q = q_ref[...].astype(FULL) * SCALE
    mixed = []
    for h in range(2):
        mine = (lane < 64) if h == 0 else (lane >= 64)
        flag = lane == (64 if h == 0 else 0)
        qa = jnp.where(mine, q, jnp.where(flag, 1.0, 0.0)).astype(LOW)
        scores = dot(ka[h], qa, NT)
        highest = jnp.max(scores, axis=0, keepdims=True)
        exponent = jnp.exp(scores - highest)
        totals = jnp.sum(exponent, axis=0, keepdims=True)
        part = dot(vt[pl.ds(64 * h, 64), :], exponent.astype(LOW), NN)
        mixed.append(part * (1.0 / totals))
        lse_ref[0, pl.ds(h, 1), :] = highest + jnp.log(totals)
    o_ref[...] = jnp.concatenate(mixed, axis=0).T.astype(LOW)


def attention_forward(counts, qkv, block):
    rows, width = qkv.shape
    pairs = width // 384
    return pl.pallas_call(
        functools.partial(forward_kernel, rows=rows, block=block),
        grid_spec=pltpu.PrefetchScalarGridSpec(
            num_scalar_prefetch=1,
            grid=(pairs, rows // block),
            in_specs=[
                pl.BlockSpec((block, 128), lambda h, i, n: (i, 3 * h)),
                pl.BlockSpec((rows, 128), lambda h, i, n: (0, 3 * h + 1)),
                pl.BlockSpec((rows, 128), lambda h, i, n: (0, 3 * h + 2)),
            ],
            out_specs=[
                pl.BlockSpec((block, 128), lambda h, i, n: (i, h)),
                pl.BlockSpec((1, 2, block), lambda h, i, n: (h, 0, i)),
            ],
            scratch_shapes=[pltpu.VMEM((2, rows, 128), LOW), pltpu.VMEM((128, rows), LOW)],
        ),
        out_shape=[
            jax.ShapeDtypeStruct((rows, pairs * 128), LOW),
            jax.ShapeDtypeStruct((pairs, 2, rows), FULL),
        ],
        cost_estimate=pl.CostEstimate(flops=1, bytes_accessed=1, transcendentals=0),
        name="attention_forward",
    )(counts, qkv, qkv, qkv)


def backward_kernel(
    counts_ref, q_ref, k_ref, v_ref, o_ref, g_ref, lse_ref, grad_ref,
    ka, va, kt, dk, dv, *, rows, block, steps, chunk,
):
    step = pl.program_id(0)

    @pl.when(step == 0)
    def _():
        keys_with_mask(k_ref, counts_ref, ka, rows)
        lane = lax.broadcasted_iota(jnp.int32, (rows, 128), 1)
        v = v_ref[...].astype(FULL)
        va[0] = jnp.where(lane < 64, v, 0.0).astype(LOW)
        va[1] = jnp.where(lane >= 64, v, 0.0).astype(LOW)
        kt[...] = k_ref[...].T
        dk[...] = jnp.zeros_like(dk)
        dv[...] = jnp.zeros_like(dv)

    lane = lax.broadcasted_iota(jnp.int32, (block, 128), 1)
    q = q_ref[...].astype(FULL)
    g = g_ref[...]
    wide = g.astype(FULL)
    product = (wide * o_ref[...].astype(FULL)).T
    scaled = q * SCALE
    columns = []
    for h in range(2):
        mine = (lane < 64) if h == 0 else (lane >= 64)
        flag = lane == (64 if h == 0 else 0)
        qa = jnp.where(mine, scaled, jnp.where(flag, 1.0, 0.0)).astype(LOW)
        qm = jnp.where(mine, q, 0.0).astype(LOW)
        gm = jnp.where(mine, wide, 0.0).astype(LOW)
        delta = jnp.sum(product[64 * h : 64 * h + 64], axis=0, keepdims=True)
        lse = lse_ref[0, pl.ds(h, 1), :]
        total = jnp.zeros((64, block), FULL)
        for c in range(rows // chunk):
            part = pl.ds(c * chunk, chunk)
            probs = jnp.exp(dot(ka[h, part, :], qa, NT) - lse)
            grad_probs = dot(va[h, part, :], g, NT)
            grad_scores = (probs * (grad_probs - delta)).astype(LOW)
            dv[part, :] += dot(probs.astype(LOW), gm, NN)
            dk[part, :] += dot(grad_scores, qm, NN)
            total = total + dot(kt[pl.ds(64 * h, 64), part], grad_scores, NN)
        columns.append(total)
    spot = pl.ds(pl.multiple_of(step * block, block), block)
    grad_ref[spot, 0:128] = (jnp.concatenate(columns, axis=0).T * SCALE).astype(LOW)

    @pl.when(step == steps - 1)
    def _():
        grad_ref[:, 128:256] = (dk[...] * SCALE).astype(LOW)
        grad_ref[:, 256:384] = dv[...].astype(LOW)


def attention_backward(counts, qkv, mixed, grad, lse, pair, block, chunk):
    rows = qkv.shape[0]
    steps = rows // block
    return pl.pallas_call(
        functools.partial(backward_kernel, rows=rows, block=block, steps=steps, chunk=chunk),
        grid_spec=pltpu.PrefetchScalarGridSpec(
            num_scalar_prefetch=1,
            grid=(steps,),
            in_specs=[
                pl.BlockSpec((block, 128), lambda i, n: (i, 3 * pair)),
                pl.BlockSpec((rows, 128), lambda i, n: (0, 3 * pair + 1)),
                pl.BlockSpec((rows, 128), lambda i, n: (0, 3 * pair + 2)),
                pl.BlockSpec((block, 128), lambda i, n: (i, pair)),
                pl.BlockSpec((block, 128), lambda i, n: (i, pair)),
                pl.BlockSpec((1, 2, block), lambda i, n: (pair, 0, i)),
            ],
            out_specs=pl.BlockSpec((rows, 384), lambda i, n: (0, 0)),
            scratch_shapes=[
                pltpu.VMEM((2, rows, 128), LOW),
                pltpu.VMEM((2, rows, 128), LOW),
                pltpu.VMEM((128, rows), LOW),
                pltpu.VMEM((rows, 128), FULL),
                pltpu.VMEM((rows, 128), FULL),
            ],
        ),
        out_shape=jax.ShapeDtypeStruct((rows, 384), LOW),
        cost_estimate=pl.CostEstimate(flops=1, bytes_accessed=1, transcendentals=0),
        name="attention_backward",
    )(counts, qkv, qkv, qkv, mixed, grad, lse)


def norm_parts(values):
    center = values - jnp.mean(values, axis=-1, keepdims=True)
    inverse = lax.rsqrt(jnp.mean(center * center, axis=-1, keepdims=True) + EPSILON)
    return center * inverse, inverse


def norm_backward(upstream, unit, inverse, gain):
    scaled = upstream * gain
    first = jnp.mean(scaled, axis=-1, keepdims=True)
    second = jnp.mean(scaled * unit, axis=-1, keepdims=True)
    result = inverse * (scaled - first - unit * second)
    return result, jnp.sum(upstream * unit, axis=0), jnp.sum(upstream, axis=0)


def gelu_parts(values):
    share = 0.5 * (1.0 + lax.erf(values * (1.0 / math.sqrt(2.0))))
    density = jnp.exp(-0.5 * values * values) * (1.0 / math.sqrt(2.0 * math.pi))
    return values * share, share + values * density


def shards(
    tokens, teacher, teach_mask, lengths, deal_group,
    ln1_gain, ln1_bias, qkv_weight, out_weight, ln2_gain, ln2_bias, up_weight, down_weight,
):
    pairs, cores, depth = (lax.axis_size(name) for name in AXES)
    p, c, z = (lax.axis_index(name) for name in AXES)
    groups = pairs * cores
    slot_rows, width = tokens.shape[1], tokens.shape[2]
    rows = 2 * slot_rows
    full_len = depth * slot_rows
    seq_count = lengths.shape[0]
    ff = up_weight.shape[1]
    own_rows = width // groups
    pair_rows = cores * own_rows
    half_width = width // 2
    half_ff = ff // 2
    is_first = c == 0

    def in_order(mine, other, axis):
        return jnp.concatenate(
            [jnp.where(is_first, mine, other), jnp.where(is_first, other, mine)], axis=axis
        )

    sequence = 2 * cores * p + z
    length = jnp.sum(jnp.where(jnp.arange(seq_count) == sequence, lengths, 0))
    base = c * rows
    counts = jnp.stack([length - base, length - (rows - base)])
    counts = jnp.clip(counts, 0, rows).astype(jnp.int32)

    heads_half = HEADS // 2
    head_pairs = heads_half // 2
    wide_half = 3 * half_width
    shard = qkv_weight.reshape(own_rows, 2, head_pairs, 2, 3, HEAD_DIM)
    shard = jnp.transpose(shard, (1, 0, 2, 4, 3, 5)).reshape(2, own_rows, wide_half)
    vectors = jnp.stack([ln1_gain, ln1_bias, ln2_gain, ln2_bias], axis=1)
    vectors = jnp.pad(vectors, ((0, 0), (0, 124)))
    vectors = jnp.broadcast_to(vectors[None], (2, own_rows, 128))
    shard = jnp.concatenate([shard, vectors], axis=2)
    keep = lax.dynamic_index_in_dim(shard, c, 0, keepdims=False)
    send = lax.dynamic_index_in_dim(shard, 1 - c, 0, keepdims=False)
    qkv_shard = in_order(keep, across_cores(send), 0)
    qkv_pieces = gathered_over_pairs(qkv_shard)

    x_rows = turned(tokens).reshape(rows, width)

    masks = deal_group[0:2]
    group = p * cores + c
    sources = jnp.bitwise_xor(group, masks) * 2 + jnp.arange(2, dtype=jnp.int32)
    picked = jnp.arange(seq_count, dtype=jnp.int32)[None, :] == sources[:, None]
    dealt_len = jnp.sum(jnp.where(picked, lengths[None, :], 0), axis=1)
    positions = z * slot_rows + jnp.arange(slot_rows, dtype=jnp.int32)
    live = (positions[None, :] < dealt_len[:, None]) & (teach_mask == 1)
    tally = jnp.full((8, 128), jnp.sum(live.astype(FULL)))
    tally = tally + across_cores(tally)

    mask_rows = jnp.pad(
        teach_mask.astype(LOW)[:, None, :], ((0, 0), (0, 15), (0, width - slot_rows))
    )
    slots = jnp.concatenate([teacher, mask_rows], axis=1)

    def dealt(slots, level):
        flagged = jnp.bitwise_and(jnp.right_shift(masks[0], level), 1) == 1
        outgoing = jnp.where(flagged, slots[0], slots[1])
        incoming = across_cores(outgoing) if level == 0 else across_pairs(outgoing, 1 << (level - 1))
        return [flagged, slots, incoming]

    def settled(flagged, slots, incoming):
        return jnp.stack(
            [jnp.where(flagged, incoming, slots[0]), jnp.where(flagged, slots[1], incoming)]
        )

    levels = groups.bit_length() - 1
    deal = dealt(slots, 0)

    block = ff // groups

    def unit_blocks(part):
        return jnp.concatenate(
            [up_weight[:, (2 * q + part) * block : (2 * q + part + 1) * block] for q in range(pairs)],
            axis=1,
        )

    up_parts = [unit_blocks(0), unit_blocks(1)]
    keep = jnp.where(is_first, up_parts[0], up_parts[1])
    send = jnp.where(is_first, up_parts[1], up_parts[0])
    got = across_cores(jnp.concatenate([send[:, :width], send[:, width:], out_weight], axis=0))
    up_shard = in_order(keep, jnp.concatenate([got[:own_rows], got[own_rows : 2 * own_rows]], axis=1), 0)
    out_shard = in_order(out_weight, got[2 * own_rows :], 0)
    payload = jnp.concatenate(
        [down_weight, up_shard[:, :width], up_shard[:, width:], out_shard], axis=0
    )
    down_rows = down_weight.shape[0]
    payload_plan = (
        (0, 0, down_rows, 0, width, 0),
        (1, down_rows, pair_rows, 0, width, 0),
        (1, down_rows + pair_rows, pair_rows, 0, width, width),
        (2, down_rows + 2 * pair_rows, pair_rows, 0, width, 0),
    )
    depth_steps, plane_steps = sum_steps()
    for step in plane_steps[1:]:
        tally = tally + step(tally)
    x_rows, payload, tally = tied(x_rows, payload, tally)
    payload_first = halves_first(payload)

    x_full = x_rows.astype(FULL)
    unit_one, inverse_one = norm_parts(x_full)
    w_qkv, vectors = placed(
        qkv_pieces,
        ((0, 0, pair_rows, 0, wide_half, 0), (1, 0, pair_rows, wide_half, 128, 0)),
    )
    pick = lax.broadcasted_iota(jnp.int32, (8, 128), 0) == lax.broadcasted_iota(jnp.int32, (8, 128), 1)
    vectors = dot(pick.astype(LOW), vectors, NT)
    gain_one, shift_one, gain_two, shift_two = vectors[0], vectors[1], vectors[2], vectors[3]
    norm_mine = (unit_one * gain_one + shift_one).astype(LOW)
    norm_one = jnp.concatenate([norm_mine, across_cores(norm_mine)], axis=0)
    norm_one, tally, deal = tied(norm_one, tally, deal)
    deal = dealt(settled(*deal), 1)
    tally = tally + depth_steps[0](tally)
    qkv = dot(norm_one, w_qkv, NN).astype(LOW)
    qkv, deal, tally, payload_first = tied(qkv, deal, tally, payload_first)
    payload_pieces = halves_second(payload_first)
    for level in range(2, levels):
        deal = dealt(settled(*deal), level)
    for step in depth_steps[1:]:
        tally = tally + step(tally)
    mixed, lse = attention_forward(counts, qkv, 512)

    sources, *place_args = payload_pieces
    mixed, sources, deal, tally = tied(mixed, sources, deal, tally)
    mixed_got = across_cores(mixed[rows:])
    goal = turned(settled(*deal))
    w_down, w_up, w_out = placed((sources, *place_args), payload_plan)

    attended = in_order(mixed[:rows], mixed_got, 1)
    middle = x_full + dot(attended, w_out, NN)
    unit_two, inverse_two = norm_parts(middle)
    norm_two = (unit_two * gain_two + shift_two).astype(LOW)
    norm_other = across_cores(norm_two)

    def expanded(low):
        value, slope = gelu_parts(dot(low, w_up, NN))
        return value.astype(LOW), slope.astype(LOW)

    active_mine, slope_mine = expanded(norm_two)
    active_other, slope_other = expanded(norm_other)
    part_other = row_major(dot(active_other, w_down, NN).astype(LOW))
    part_mine = row_major(dot(active_mine, w_down, NN))
    output = middle + part_mine + across_cores(part_other).astype(FULL)

    output, goal, tally = tied(output, goal, tally)
    valid_count = tally[0, 0]
    spots = base + jnp.arange(rows, dtype=jnp.int32)
    taught = goal[:, slot_rows, :slot_rows].reshape(rows)
    valid = ((spots < length) & (taught == 1)).astype(FULL)[:, None]
    error = output - goal[:, :slot_rows].reshape(rows, width).astype(FULL)
    squares = jnp.sum(valid * error * error)
    factor = seq_count * full_len * 1.0 / valid_count
    grad_out = valid * (2.0 * factor) * error
    grad_ff = grad_out.astype(LOW)
    grad_ff_other = across_cores(grad_ff)
    output_moved = turned_parts(output.astype(LOW).reshape(2, slot_rows, width))
    hidden_mine = (dot(grad_ff, w_down, NT) * slope_mine.astype(FULL)).astype(LOW)
    down_grad = (dot(active_mine, grad_ff, TN) + dot(active_other, grad_ff_other, TN)).astype(LOW)
    down_grad, grad_ff_other, hidden_mine = tied(down_grad, grad_ff_other, hidden_mine)
    down_sum = scattered_over_pairs(down_grad)
    hidden_other = (dot(grad_ff_other, w_down, NT) * slope_other.astype(FULL)).astype(LOW)
    back_other = dot(hidden_other, w_up, NT).astype(LOW)
    back_got = across_cores(back_other)
    back_mine = dot(hidden_mine, w_up, NT)
    up_grad = (dot(norm_two, hidden_mine, TN) + dot(norm_other, hidden_other, TN)).astype(LOW)
    grad_mid, gain_two_grad, shift_two_grad = norm_backward(
        back_mine + back_got.astype(FULL), unit_two, inverse_two, gain_two
    )
    grad_middle = grad_out + grad_mid
    grad_branch = grad_middle.astype(LOW)
    grad_attended = dot(grad_branch, w_out, NT).astype(LOW)
    keep = jnp.where(is_first, grad_attended[:, :half_width], grad_attended[:, half_width:])
    send = jnp.where(is_first, grad_attended[:, half_width:], grad_attended[:, :half_width])
    mixed_grad_got = across_cores(send)
    out_grad = dot(attended, grad_branch, TN).astype(LOW)
    rest_sum = scattered_over_pairs(jnp.concatenate([up_grad, out_grad], axis=1))
    grad_mixed = jnp.concatenate([keep, mixed_grad_got], axis=0)

    def attend(pair, gate):
        return attention_backward(gate, qkv, mixed, grad_mixed, lse, pair, 512, 512)

    def weight_part(grads):
        return dot(norm_one, grads, TN).astype(LOW)

    low_bit, high_bit = 1, depth // 2
    first = attend(0, counts)
    first, down_sum, output_moved, gate = tied(first, down_sum, output_moved, counts)
    activations = turned_settled(output_moved)
    down_step = depth_halved(added(down_sum), low_bit)
    second = attend(1, gate)
    second, first, down_step, rest_sum, gate = tied(second, first, down_step, rest_sum, counts)
    down_step = depth_halved(added(down_step), high_bit)
    rest_step = depth_halved(added(rest_sum), low_bit)
    early = scattered_over_pairs(weight_part(jnp.concatenate([first, second], axis=1)))
    third = attend(2, gate)
    third, first, second, down_step, rest_step, early = tied(
        third, first, second, down_step, rest_step, early
    )

    partial = row_major(dot(jnp.concatenate([first, second, third], axis=1), w_qkv, NT))
    back_got = across_cores(partial[rows:].astype(LOW))
    early = depth_halved(added(early), low_bit)
    rest_step = depth_halved(added(rest_step), high_bit)
    down_own = added(down_step)
    down_got = across_depth(down_own, high_bit)
    late = scattered_over_pairs(weight_part(third))
    grad_norm_one = partial[:rows] + back_got.astype(FULL)
    grad_in, gain_one_grad, shift_one_grad = norm_backward(
        grad_norm_one, unit_one, inverse_one, gain_one
    )
    grad_rows = row_major((grad_middle + grad_in).astype(LOW))
    input_moved = turned_parts(grad_rows.reshape(2, slot_rows, width))

    row_index = lax.broadcasted_iota(jnp.int32, (8, width), 0)
    small = jnp.zeros((8, width), FULL)
    for index, value in enumerate(
        [gain_one_grad, shift_one_grad, gain_two_grad, shift_two_grad, jnp.full((width,), squares)]
    ):
        small = jnp.where(row_index == index, value[None, :], small)
    small = small + plane_steps[0](small)

    late = depth_halved(added(late), low_bit)
    rest_own = added(rest_step)
    rest_got = across_depth(rest_own, high_bit)
    late, early, rest_got, small, down_got, near = tied(
        late, early, rest_got, small, down_got, input_moved[0]
    )
    down_own = depth_doubled(down_own, down_got, high_bit)
    down_got = across_depth(down_own, low_bit)
    qkv_step = depth_halved(jnp.concatenate([added(early), added(late)], axis=1), high_bit)
    rest_own = depth_doubled(rest_own, rest_got, high_bit)
    rest_got = across_depth(rest_own, low_bit)
    small = small + plane_steps[1](small)
    qkv_step, small, down_got, far = tied(qkv_step, small, down_got, input_moved[1])
    input_grad = turned_settled([near, far])
    down_own = depth_doubled(down_own, down_got, low_bit)
    qkv_own = added(qkv_step)
    qkv_got = across_depth(qkv_own, high_bit)
    for step in plane_steps[2:]:
        small = small + step(small)
    qkv_got, rest_got, small = tied(qkv_got, rest_got, small)
    qkv_own = depth_doubled(qkv_own, qkv_got, high_bit)
    qkv_got = across_depth(qkv_own, low_bit)
    rest_own = depth_doubled(rest_own, rest_got, low_bit)
    small = small + depth_steps[0](small)

    def own_block(stack, index):
        return lax.dynamic_slice_in_dim(stack, index * own_rows, own_rows, 0)

    rest_mine = own_block(rest_own, c)
    rest_other = across_cores(own_block(rest_own, 1 - c))
    qkv_got, rest_other, small = tied(qkv_got, rest_other, small)
    qkv_own = depth_doubled(qkv_own, qkv_got, low_bit)
    qkv_mine = own_block(qkv_own, c)
    qkv_other = across_cores(own_block(qkv_own, 1 - c))
    for step in depth_steps[1:]:
        small = small + step(small)

    loss = small[4, 0] / (valid_count * width)
    own_small = lax.dynamic_slice_in_dim(small, group * own_rows, own_rows, 1)
    out_own = rest_mine[:, half_ff:].astype(FULL) + rest_other[:, half_ff:].astype(FULL)
    sides = [jnp.where(is_first, rest_mine, rest_other), jnp.where(is_first, rest_other, rest_mine)]
    up_own = jnp.concatenate(
        [side[:, q * block : (q + 1) * block] for q in range(pairs) for side in sides], axis=1
    )
    qkv_own = jnp.stack(
        [jnp.where(is_first, qkv_mine, qkv_other), jnp.where(is_first, qkv_other, qkv_mine)]
    )
    qkv_own = qkv_own.reshape(2, own_rows, head_pairs, 3, 2, HEAD_DIM)
    qkv_own = jnp.transpose(qkv_own, (1, 0, 2, 4, 3, 5)).reshape(own_rows, 3 * width)
    return (
        activations, loss, input_grad, own_small[0], own_small[1], qkv_own.astype(FULL),
        out_own, own_small[2], own_small[3], up_own.astype(FULL), down_own.astype(FULL),
    )


def solution(mesh):
    groups, depth = mesh.shape["dp"], mesh.shape["seq"]
    split = Mesh(mesh.devices.reshape(groups // 2, 2, depth), AXES)
    dp = ("pair", "core")
    rows3 = P(dp, "seq", None)
    in_specs = (
        rows3, rows3, P(dp, "seq"), P(), P(), P(dp), P(dp), P(dp, None), P(dp, None),
        P(dp), P(dp), P(dp, None), P(dp, None),
    )
    out_specs = (
        rows3, P(), rows3, P(dp), P(dp), P(dp, None), P(dp, None), P(dp), P(dp),
        P(dp, None), P(dp, None),
    )
    return jax.shard_map(shards, mesh=split, in_specs=in_specs, out_specs=out_specs, check_vma=False)
```

```python
import functools
import math

import jax
import jax.numpy as jnp
from jax import lax
from jax.experimental import pallas as pl
from jax.experimental.layout import Layout, with_layout_constraint
from jax.experimental.pallas import tpu as pltpu
from jax.sharding import Mesh
from jax.sharding import PartitionSpec as P

HEADS = 12
HEAD_DIM = 64
EPSILON = 1e-12
NEGATIVE = -1e30
SCALE = 1.0 / math.sqrt(HEAD_DIM)
AXES = ("pair", "core", "seq")
NT = (((1,), (1,)), ((), ()))
NN = (((1,), (0,)), ((), ()))
TN = (((0,), (0,)), ((), ()))
LOW = jnp.bfloat16
FULL = jnp.float32


def dot(left, right, form):
    return lax.dot_general(left, right, form, preferred_element_type=FULL)


def row_major(value):
    return with_layout_constraint(value, Layout(major_to_minor=tuple(range(value.ndim))))


def moved(value, target):
    pairs, cores, depth = (lax.axis_size(name) for name in AXES)
    links = []
    for p in range(pairs):
        for c in range(cores):
            for z in range(depth):
                q, e, w = target(p, c, z)
                links.append(((p * cores + c) * depth + z, (q * cores + e) * depth + w))
    return lax.ppermute(value, AXES, links)


def across_cores(value):
    return moved(value, lambda p, c, z: (p, 1 - c, z))


def across_pairs(value, bit):
    return moved(value, lambda p, c, z: (p ^ bit, c, z))


def across_depth(value, bit):
    return moved(value, lambda p, c, z: (p, c, z ^ bit))


def pair_bits():
    return [1 << level for level in range(lax.axis_size("pair").bit_length() - 1)]


def turned_parts(stack):
    z = lax.axis_index("seq")
    got = []
    for step in range(2):
        piece = lax.dynamic_index_in_dim(stack, (z + step) % 2, 0, keepdims=False)
        got.append(moved(piece, lambda p, c, w: (p, w // 2, 2 * c + (w + step) % 2)))
    return got


def turned_piece(stack, step):
    piece = lax.dynamic_index_in_dim(stack, (lax.axis_index("seq") + step) % 2, 0, keepdims=False)
    return [piece[: piece.shape[0] // 2], piece[piece.shape[0] // 2 :]]


def turned_send(piece, step):
    return moved(piece, lambda p, c, w: (p, w // 2, 2 * c + (w + step) % 2))


def turned_settled(got):
    even = lax.axis_index("seq") % 2 == 0
    return jnp.stack([jnp.where(even, got[0], got[1]), jnp.where(even, got[1], got[0])])


def turned(stack):
    return turned_settled(turned_parts(stack))


def sum_steps():
    depth_steps = [
        functools.partial(across_depth, bit=1 << level)
        for level in range(lax.axis_size("seq").bit_length() - 1)
    ]
    pair_steps = [functools.partial(across_pairs, bit=bit) for bit in pair_bits()]
    return depth_steps, [across_cores] + pair_steps


def gathered_over_pairs(value):
    p = lax.axis_index("pair")
    if lax.axis_size("pair") <= 4:
        count = lax.axis_size("pair")
        layout = tuple((k, k, 0, 0, value.shape[0]) for k in range(count))
        return [value] + [across_pairs(value, k) for k in range(1, count)], p, layout
    rows, width = value.shape
    bits = pair_bits()
    count = 1 << len(bits)
    halves = []
    for which in range(2):
        order = bits if which == 0 else bits[::-1]
        current = value[which * rows // 2 : (which + 1) * rows // 2]
        for bit in order:
            other = across_pairs(current, bit)
            flag = jnp.bitwise_and(p, bit) != 0
            current = jnp.stack(
                [jnp.where(flag, other, current), jnp.where(flag, current, other)]
            )
        if which == 1:
            lead = tuple(range(len(bits)))[::-1]
            current = jnp.transpose(current, lead + (len(bits), len(bits) + 1))
        halves.append(current.reshape(count, rows // 2, width))
    return [jnp.concatenate(halves, axis=1).reshape(count * rows, width)], None, ()


def halves_first(value):
    if lax.axis_size("pair") != 4:
        return value, None
    rows = value.shape[0] // 2
    return value, (across_pairs(value[:rows], 1), across_pairs(value[rows:], 2))


def halves_second(state):
    value, near = state
    if near is None:
        return gathered_over_pairs(value)
    rows = value.shape[0] // 2
    upper = across_pairs(jnp.concatenate([value[:rows], near[0]], axis=0), 2)
    lower = across_pairs(jnp.concatenate([value[rows:], near[1]], axis=0), 1)
    layout = (
        (0, 0, 0, 0, 2 * rows),
        (1, 1, 0, 0, rows), (1, 4, 0, rows, rows),
        (2, 3, 0, 0, rows), (2, 2, 0, rows, rows),
        (3, 3, rows, 0, rows), (3, 4, rows, rows, rows),
    )
    return [value, near[0], near[1], upper, lower], lax.axis_index("pair"), layout


def place_kernel(p_ref, *refs, segments, layout, count):
    sources, results = refs[:count], refs[count:]
    for k, source, origin, first, size in layout:
        spot = jnp.bitwise_xor(p_ref[0], k)
        for index, row, rows, column, width, target in segments:
            low, high = max(row, first), min(row + rows, first + size)
            if low < high:
                start = pl.multiple_of(spot * rows + (low - row), 16)
                results[index][pl.ds(start, high - low), target : target + width] = sources[source][
                    low - first + origin : high - first + origin, column : column + width
                ]


def placed(gathered, segments):
    pieces, p, layout = gathered
    pairs = lax.axis_size("pair")
    outs = 1 + max(segment[0] for segment in segments)
    if p is None:
        stack = pieces[0].reshape(pairs, -1, pieces[0].shape[1])
        results = []
        for index in range(outs):
            parts = [
                stack[:, row : row + rows, column : column + width].reshape(pairs * rows, width)
                for which, row, rows, column, width, _ in segments
                if which == index
            ]
            results.append(jnp.concatenate(parts, axis=1))
        return results
    shapes = []
    for index in range(outs):
        mine = [segment for segment in segments if segment[0] == index]
        shapes.append(
            jax.ShapeDtypeStruct((pairs * mine[0][2], sum(part[4] for part in mine)), LOW)
        )
    local = pl.BlockSpec(memory_space=pltpu.VMEM)
    return pl.pallas_call(
        functools.partial(place_kernel, segments=segments, layout=layout, count=len(pieces)),
        in_specs=[pl.BlockSpec(memory_space=pltpu.SMEM)] + [local] * len(pieces),
        out_specs=[local] * outs,
        out_shape=shapes,
        name="place",
    )(p.astype(jnp.int32).reshape(1), *pieces)


def scattered_over_pairs(value):
    p = lax.axis_index("pair")
    if lax.axis_size("pair") <= 4:
        rows = value.shape[0] // lax.axis_size("pair")
        pieces = []
        for k in range(lax.axis_size("pair")):
            piece = lax.dynamic_slice_in_dim(value, jnp.bitwise_xor(p, k) * rows, rows, 0)
            pieces.append(across_pairs(piece, k) if k else piece)
        return pieces
    bits = pair_bits()
    count = 1 << len(bits)
    rows, width = value.shape[0] // count, value.shape[1]
    blocks = value.reshape(count, rows, width)
    halves = []
    for which in range(2):
        order = bits if which == 0 else bits[::-1]
        current = blocks[:, which * rows // 2 : (which + 1) * rows // 2]
        current = current.reshape((2,) * len(bits) + (rows // 2, width))
        left = bits[::-1]
        for bit in order:
            axis = left.index(bit)
            mine = jnp.where(jnp.bitwise_and(p, bit) != 0, 1, 0)
            keep = lax.dynamic_index_in_dim(current, mine, axis, keepdims=False)
            send = lax.dynamic_index_in_dim(current, 1 - mine, axis, keepdims=False)
            current = keep + across_pairs(send, bit)
            left = [other for other in left if other != bit]
        halves.append(current)
    return [jnp.concatenate(halves, axis=0)]


def added(pieces):
    total = pieces[0].astype(FULL)
    for piece in pieces[1:]:
        total = total + piece.astype(FULL)
    return total.astype(LOW)


def depth_flag(bit):
    return jnp.where(jnp.bitwise_and(lax.axis_index("seq"), bit) != 0, 1, 0)


def depth_halved(value, bit):
    mine = depth_flag(bit)
    parts = value.reshape((2, value.shape[0] // 2) + value.shape[1:])
    keep = lax.dynamic_index_in_dim(parts, mine, 0, keepdims=False)
    send = lax.dynamic_index_in_dim(parts, 1 - mine, 0, keepdims=False)
    return [keep, across_depth(send, bit)]


def depth_doubled(value, other, bit):
    mine = depth_flag(bit)
    return jnp.concatenate(
        [jnp.where(mine == 0, value, other), jnp.where(mine == 0, other, value)], axis=0
    )


def tied(*values):
    return lax.optimization_barrier(values)


def keys_with_mask(k_ref, counts_ref, ka, rows):
    lane = lax.broadcasted_iota(jnp.int32, (rows, 128), 1)
    spot = lax.broadcasted_iota(jnp.int32, (rows, 128), 0)
    limit = jnp.where(spot < rows // 2, counts_ref[0], counts_ref[1] + rows // 2)
    bias = jnp.where(spot < limit, 0.0, NEGATIVE)
    k = k_ref[...].astype(FULL)
    ka[0] = jnp.where(lane < 64, k, jnp.where(lane == 64, bias, 0.0)).astype(LOW)
    ka[1] = jnp.where(lane >= 64, k, jnp.where(lane == 0, bias, 0.0)).astype(LOW)


def forward_kernel(counts_ref, q_ref, k_ref, v_ref, o_ref, lse_ref, ka, vt, *, rows, block):
    @pl.when(pl.program_id(1) == 0)
    def _():
        keys_with_mask(k_ref, counts_ref, ka, rows)
        vt[...] = v_ref[...].T

    lane = lax.broadcasted_iota(jnp.int32, (block, 128), 1)
    q = q_ref[...].astype(FULL) * SCALE
    mixed = []
    for h in range(2):
        mine = (lane < 64) if h == 0 else (lane >= 64)
        flag = lane == (64 if h == 0 else 0)
        qa = jnp.where(mine, q, jnp.where(flag, 1.0, 0.0)).astype(LOW)
        scores = dot(ka[h], qa, NT)
        highest = jnp.max(scores, axis=0, keepdims=True)
        exponent = jnp.exp(scores - highest)
        totals = jnp.sum(exponent, axis=0, keepdims=True)
        part = dot(vt[pl.ds(64 * h, 64), :], exponent.astype(LOW), NN)
        mixed.append(part * (1.0 / totals))
        lse_ref[0, pl.ds(h, 1), :] = highest + jnp.log(totals)
    o_ref[...] = jnp.concatenate(mixed, axis=0).T.astype(LOW)


def attention_forward(counts, qkv, block):
    rows, width = qkv.shape
    pairs = width // 384
    return pl.pallas_call(
        functools.partial(forward_kernel, rows=rows, block=block),
        grid_spec=pltpu.PrefetchScalarGridSpec(
            num_scalar_prefetch=1,
            grid=(pairs, rows // block),
            in_specs=[
                pl.BlockSpec((block, 128), lambda h, i, n: (i, 3 * h)),
                pl.BlockSpec((rows, 128), lambda h, i, n: (0, 3 * h + 1)),
                pl.BlockSpec((rows, 128), lambda h, i, n: (0, 3 * h + 2)),
            ],
            out_specs=[
                pl.BlockSpec((block, 128), lambda h, i, n: (i, h)),
                pl.BlockSpec((1, 2, block), lambda h, i, n: (h, 0, i)),
            ],
            scratch_shapes=[pltpu.VMEM((2, rows, 128), LOW), pltpu.VMEM((128, rows), LOW)],
        ),
        out_shape=[
            jax.ShapeDtypeStruct((rows, pairs * 128), LOW),
            jax.ShapeDtypeStruct((pairs, 2, rows), FULL),
        ],
        cost_estimate=pl.CostEstimate(flops=1, bytes_accessed=1, transcendentals=0),
        name="attention_forward",
    )(counts, qkv, qkv, qkv)


def backward_kernel(
    counts_ref, q_ref, k_ref, v_ref, o_ref, g_ref, lse_ref, grad_ref,
    ka, va, kt, dk, dv, *, rows, block, steps, chunk,
):
    step = pl.program_id(0)

    @pl.when(step == 0)
    def _():
        keys_with_mask(k_ref, counts_ref, ka, rows)
        lane = lax.broadcasted_iota(jnp.int32, (rows, 128), 1)
        v = v_ref[...].astype(FULL)
        va[0] = jnp.where(lane < 64, v, 0.0).astype(LOW)
        va[1] = jnp.where(lane >= 64, v, 0.0).astype(LOW)
        kt[...] = k_ref[...].T
        dk[...] = jnp.zeros_like(dk)
        dv[...] = jnp.zeros_like(dv)

    lane = lax.broadcasted_iota(jnp.int32, (block, 128), 1)
    q = q_ref[...].astype(FULL)
    g = g_ref[...]
    wide = g.astype(FULL)
    product = (wide * o_ref[...].astype(FULL)).T
    scaled = q * SCALE
    columns = []
    for h in range(2):
        mine = (lane < 64) if h == 0 else (lane >= 64)
        flag = lane == (64 if h == 0 else 0)
        qa = jnp.where(mine, scaled, jnp.where(flag, 1.0, 0.0)).astype(LOW)
        qm = jnp.where(mine, q, 0.0).astype(LOW)
        gm = jnp.where(mine, wide, 0.0).astype(LOW)
        delta = jnp.sum(product[64 * h : 64 * h + 64], axis=0, keepdims=True)
        lse = lse_ref[0, pl.ds(h, 1), :]
        total = jnp.zeros((64, block), FULL)
        for c in range(rows // chunk):
            part = pl.ds(c * chunk, chunk)
            probs = jnp.exp(dot(ka[h, part, :], qa, NT) - lse)
            grad_probs = dot(va[h, part, :], g, NT)
            grad_scores = (probs * (grad_probs - delta)).astype(LOW)
            dv[part, :] += dot(probs.astype(LOW), gm, NN)
            dk[part, :] += dot(grad_scores, qm, NN)
            total = total + dot(kt[pl.ds(64 * h, 64), part], grad_scores, NN)
        columns.append(total)
    spot = pl.ds(pl.multiple_of(step * block, block), block)
    grad_ref[spot, 0:128] = (jnp.concatenate(columns, axis=0).T * SCALE).astype(LOW)

    @pl.when(step == steps - 1)
    def _():
        grad_ref[:, 128:256] = (dk[...] * SCALE).astype(LOW)
        grad_ref[:, 256:384] = dv[...].astype(LOW)


def attention_backward(counts, qkv, mixed, grad, lse, pair, block, chunk):
    rows = qkv.shape[0]
    steps = rows // block
    return pl.pallas_call(
        functools.partial(backward_kernel, rows=rows, block=block, steps=steps, chunk=chunk),
        grid_spec=pltpu.PrefetchScalarGridSpec(
            num_scalar_prefetch=1,
            grid=(steps,),
            in_specs=[
                pl.BlockSpec((block, 128), lambda i, n: (i, 3 * pair)),
                pl.BlockSpec((rows, 128), lambda i, n: (0, 3 * pair + 1)),
                pl.BlockSpec((rows, 128), lambda i, n: (0, 3 * pair + 2)),
                pl.BlockSpec((block, 128), lambda i, n: (i, pair)),
                pl.BlockSpec((block, 128), lambda i, n: (i, pair)),
                pl.BlockSpec((1, 2, block), lambda i, n: (pair, 0, i)),
            ],
            out_specs=pl.BlockSpec((rows, 384), lambda i, n: (0, 0)),
            scratch_shapes=[
                pltpu.VMEM((2, rows, 128), LOW),
                pltpu.VMEM((2, rows, 128), LOW),
                pltpu.VMEM((128, rows), LOW),
                pltpu.VMEM((rows, 128), FULL),
                pltpu.VMEM((rows, 128), FULL),
            ],
        ),
        out_shape=jax.ShapeDtypeStruct((rows, 384), LOW),
        cost_estimate=pl.CostEstimate(flops=1, bytes_accessed=1, transcendentals=0),
        name="attention_backward",
    )(counts, qkv, qkv, qkv, mixed, grad, lse)


def norm_parts(values):
    center = values - jnp.mean(values, axis=-1, keepdims=True)
    inverse = lax.rsqrt(jnp.mean(center * center, axis=-1, keepdims=True) + EPSILON)
    return center * inverse, inverse


def norm_backward(upstream, unit, inverse, gain):
    scaled = upstream * gain
    first = jnp.mean(scaled, axis=-1, keepdims=True)
    second = jnp.mean(scaled * unit, axis=-1, keepdims=True)
    result = inverse * (scaled - first - unit * second)
    return result, jnp.sum(upstream * unit, axis=0), jnp.sum(upstream, axis=0)


def gelu_parts(values):
    share = 0.5 * (1.0 + lax.erf(values * (1.0 / math.sqrt(2.0))))
    density = jnp.exp(-0.5 * values * values) * (1.0 / math.sqrt(2.0 * math.pi))
    return values * share, share + values * density


def shards(
    tokens, teacher, teach_mask, lengths, deal_group,
    ln1_gain, ln1_bias, qkv_weight, out_weight, ln2_gain, ln2_bias, up_weight, down_weight,
):
    pairs, cores, depth = (lax.axis_size(name) for name in AXES)
    p, c, z = (lax.axis_index(name) for name in AXES)
    groups = pairs * cores
    slot_rows, width = tokens.shape[1], tokens.shape[2]
    rows = 2 * slot_rows
    full_len = depth * slot_rows
    seq_count = lengths.shape[0]
    ff = up_weight.shape[1]
    own_rows = width // groups
    pair_rows = cores * own_rows
    half_width = width // 2
    half_ff = ff // 2
    is_first = c == 0

    def in_order(mine, other, axis):
        return jnp.concatenate(
            [jnp.where(is_first, mine, other), jnp.where(is_first, other, mine)], axis=axis
        )

    sequence = 2 * cores * p + z
    length = jnp.sum(jnp.where(jnp.arange(seq_count) == sequence, lengths, 0))
    base = c * rows
    counts = jnp.stack([length - base, length - (rows - base)])
    counts = jnp.clip(counts, 0, rows).astype(jnp.int32)

    heads_half = HEADS // 2
    head_pairs = heads_half // 2
    wide_half = 3 * half_width
    shard = qkv_weight.reshape(own_rows, 2, head_pairs, 2, 3, HEAD_DIM)
    shard = jnp.transpose(shard, (1, 0, 2, 4, 3, 5)).reshape(2, own_rows, wide_half)
    vectors = jnp.stack([ln1_gain, ln1_bias, ln2_gain, ln2_bias], axis=1)
    vectors = jnp.pad(vectors, ((0, 0), (0, 124)))
    vectors = jnp.broadcast_to(vectors[None], (2, own_rows, 128))
    shard = jnp.concatenate([shard, vectors], axis=2)
    keep = lax.dynamic_index_in_dim(shard, c, 0, keepdims=False)
    send = lax.dynamic_index_in_dim(shard, 1 - c, 0, keepdims=False)
    qkv_shard = in_order(keep, across_cores(send), 0)

    x_rows = turned(tokens).reshape(rows, width)

    masks = deal_group[0:2]
    group = p * cores + c
    sources = jnp.bitwise_xor(group, masks) * 2 + jnp.arange(2, dtype=jnp.int32)
    picked = jnp.arange(seq_count, dtype=jnp.int32)[None, :] == sources[:, None]
    dealt_len = jnp.sum(jnp.where(picked, lengths[None, :], 0), axis=1)
    positions = z * slot_rows + jnp.arange(slot_rows, dtype=jnp.int32)
    live = (positions[None, :] < dealt_len[:, None]) & (teach_mask == 1)
    tally = jnp.full((8, 128), jnp.sum(live.astype(FULL)))
    tally = tally + across_cores(tally)

    mask_rows = jnp.pad(
        teach_mask.astype(LOW)[:, None, :], ((0, 0), (0, 15), (0, width - slot_rows))
    )
    slots = jnp.concatenate([teacher, mask_rows], axis=1)

    def dealt(slots, level):
        flagged = jnp.bitwise_and(jnp.right_shift(masks[0], level), 1) == 1
        outgoing = jnp.where(flagged, slots[0], slots[1])
        incoming = across_cores(outgoing) if level == 0 else across_pairs(outgoing, 1 << (level - 1))
        return [flagged, slots, incoming]

    def settled(flagged, slots, incoming):
        return jnp.stack(
            [jnp.where(flagged, incoming, slots[0]), jnp.where(flagged, slots[1], incoming)]
        )

    levels = groups.bit_length() - 1
    deal = dealt(slots, 0)

    block = ff // groups

    def unit_blocks(part):
        return jnp.concatenate(
            [up_weight[:, (2 * q + part) * block : (2 * q + part + 1) * block] for q in range(pairs)],
            axis=1,
        )

    up_parts = [unit_blocks(0), unit_blocks(1)]
    keep = jnp.where(is_first, up_parts[0], up_parts[1])
    send = jnp.where(is_first, up_parts[1], up_parts[0])
    got = across_cores(jnp.concatenate([send[:, :width], send[:, width:], out_weight], axis=0))
    up_shard = in_order(keep, jnp.concatenate([got[:own_rows], got[own_rows : 2 * own_rows]], axis=1), 0)
    out_shard = in_order(out_weight, got[2 * own_rows :], 0)
    payload = jnp.concatenate(
        [down_weight, up_shard[:, :width], up_shard[:, width:], out_shard], axis=0
    )
    down_rows = down_weight.shape[0]
    payload_plan = (
        (0, 0, down_rows, 0, width, 0),
        (1, down_rows, pair_rows, 0, width, 0),
        (1, down_rows + pair_rows, pair_rows, 0, width, width),
        (2, down_rows + 2 * pair_rows, pair_rows, 0, width, 0),
    )
    depth_steps, plane_steps = sum_steps()
    for step in plane_steps[1:]:
        tally = tally + step(tally)
    payload_first = halves_first(payload)
    qkv_shard, payload_first = tied(qkv_shard, payload_first)
    qkv_pieces = gathered_over_pairs(qkv_shard)
    x_rows, tally = tied(x_rows, tally)

    x_full = x_rows.astype(FULL)
    unit_one, inverse_one = norm_parts(x_full)
    w_qkv, vectors = placed(
        qkv_pieces,
        ((0, 0, pair_rows, 0, wide_half, 0), (1, 0, pair_rows, wide_half, 128, 0)),
    )
    pick = lax.broadcasted_iota(jnp.int32, (8, 128), 0) == lax.broadcasted_iota(jnp.int32, (8, 128), 1)
    vectors = dot(pick.astype(LOW), vectors, NT)
    gain_one, shift_one, gain_two, shift_two = vectors[0], vectors[1], vectors[2], vectors[3]
    norm_mine = (unit_one * gain_one + shift_one).astype(LOW)
    norm_one = jnp.concatenate([norm_mine, across_cores(norm_mine)], axis=0)
    norm_one, tally, payload_first = tied(norm_one, tally, payload_first)
    payload_pieces = halves_second(payload_first)
    tally = tally + depth_steps[0](tally)
    qkv = dot(norm_one, w_qkv, NN).astype(LOW)
    qkv, deal, tally = tied(qkv, deal, tally)
    deal = dealt(settled(*deal), 1)
    for step in depth_steps[1:]:
        tally = tally + step(tally)
    mixed, lse = attention_forward(counts, qkv, 512)

    sources, *place_args = payload_pieces
    mixed, sources, deal, tally = tied(mixed, sources, deal, tally)
    mixed_got = across_cores(mixed[rows:])
    for level in range(2, levels):
        deal = dealt(settled(*deal), level)
    w_down, w_up, w_out = placed((sources, *place_args), payload_plan)

    attended = in_order(mixed[:rows], mixed_got, 1)
    middle = x_full + dot(attended, w_out, NN)
    unit_two, inverse_two = norm_parts(middle)
    norm_two = (unit_two * gain_two + shift_two).astype(LOW)
    norm_other = across_cores(norm_two)

    def expanded(low):
        value, slope = gelu_parts(dot(low, w_up, NN))
        return value.astype(LOW), slope.astype(LOW)

    active_mine, slope_mine = expanded(norm_two)
    active_mine, slope_mine, deal = tied(active_mine, slope_mine, deal)
    goal = turned(settled(*deal))
    active_other, slope_other = expanded(norm_other)
    part_other = row_major(dot(active_other, w_down, NN).astype(LOW))
    part_mine = row_major(dot(active_mine, w_down, NN))
    output = middle + part_mine + across_cores(part_other).astype(FULL)

    output, goal, tally = tied(output, goal, tally)
    valid_count = tally[0, 0]
    spots = base + jnp.arange(rows, dtype=jnp.int32)
    taught = goal[:, slot_rows, :slot_rows].reshape(rows)
    valid = ((spots < length) & (taught == 1)).astype(FULL)[:, None]
    error = output - goal[:, :slot_rows].reshape(rows, width).astype(FULL)
    squares = jnp.sum(valid * error * error)
    factor = seq_count * full_len * 1.0 / valid_count
    grad_out = valid * (2.0 * factor) * error
    grad_ff = grad_out.astype(LOW)
    grad_ff_other = across_cores(grad_ff)
    output_moved = turned_parts(output.astype(LOW).reshape(2, slot_rows, width))
    hidden_mine = (dot(grad_ff, w_down, NT) * slope_mine.astype(FULL)).astype(LOW)
    down_grad = (dot(active_mine, grad_ff, TN) + dot(active_other, grad_ff_other, TN)).astype(LOW)
    down_grad, grad_ff_other, hidden_mine = tied(down_grad, grad_ff_other, hidden_mine)
    down_sum = scattered_over_pairs(down_grad)
    hidden_other = (dot(grad_ff_other, w_down, NT) * slope_other.astype(FULL)).astype(LOW)
    back_other = dot(hidden_other, w_up, NT).astype(LOW)
    back_got = across_cores(back_other)
    back_mine = dot(hidden_mine, w_up, NT)
    up_grad = (dot(norm_two, hidden_mine, TN) + dot(norm_other, hidden_other, TN)).astype(LOW)
    grad_mid, gain_two_grad, shift_two_grad = norm_backward(
        back_mine + back_got.astype(FULL), unit_two, inverse_two, gain_two
    )
    grad_middle = grad_out + grad_mid
    grad_branch = grad_middle.astype(LOW)
    grad_attended = dot(grad_branch, w_out, NT).astype(LOW)
    keep = jnp.where(is_first, grad_attended[:, :half_width], grad_attended[:, half_width:])
    send = jnp.where(is_first, grad_attended[:, half_width:], grad_attended[:, :half_width])
    mixed_grad_got = across_cores(send)
    out_grad = dot(attended, grad_branch, TN).astype(LOW)
    rest_sum = scattered_over_pairs(jnp.concatenate([up_grad, out_grad], axis=1))
    grad_mixed = jnp.concatenate([keep, mixed_grad_got], axis=0)

    def attend(pair, gate):
        return attention_backward(gate, qkv, mixed, grad_mixed, lse, pair, 512, 512)

    def weight_part(grads):
        return dot(norm_one, grads, TN).astype(LOW)

    low_bit, high_bit = 1, depth // 2
    first = attend(0, counts)
    first, down_sum, output_moved, gate = tied(first, down_sum, output_moved, counts)
    activations = turned_settled(output_moved)
    down_step = depth_halved(added(down_sum), low_bit)
    second = attend(1, gate)
    second, first, down_step, rest_sum, gate = tied(second, first, down_step, rest_sum, counts)
    down_step = depth_halved(added(down_step), high_bit)
    rest_step = depth_halved(added(rest_sum), low_bit)
    early = scattered_over_pairs(weight_part(jnp.concatenate([first, second], axis=1)))
    third = attend(2, gate)
    third, first, second, down_step, rest_step, early = tied(
        third, first, second, down_step, rest_step, early
    )

    partial = row_major(dot(jnp.concatenate([first, second, third], axis=1), w_qkv, NT))
    back_got = across_cores(partial[rows:].astype(LOW))
    early = depth_halved(added(early), low_bit)
    rest_step = depth_halved(added(rest_step), high_bit)
    down_own = added(down_step)
    down_got = across_depth(down_own, high_bit)
    late = scattered_over_pairs(weight_part(third))
    grad_norm_one = partial[:rows] + back_got.astype(FULL)
    grad_in, gain_one_grad, shift_one_grad = norm_backward(
        grad_norm_one, unit_one, inverse_one, gain_one
    )
    grad_rows = row_major((grad_middle + grad_in).astype(LOW))
    grad_rows = grad_rows.reshape(2, slot_rows, width)
    parts = turned_piece(grad_rows, 0) + turned_piece(grad_rows, 1)
    sent = [turned_send(parts[0], 0)]

    row_index = lax.broadcasted_iota(jnp.int32, (8, width), 0)
    small = jnp.zeros((8, width), FULL)
    for index, value in enumerate(
        [gain_one_grad, shift_one_grad, gain_two_grad, shift_two_grad, jnp.full((width,), squares)]
    ):
        small = jnp.where(row_index == index, value[None, :], small)
    small = small + plane_steps[0](small)

    late = depth_halved(added(late), low_bit)
    rest_own = added(rest_step)
    rest_got = across_depth(rest_own, high_bit)
    late, early, small, parts[1] = tied(late, early, small, parts[1])
    qkv_step = depth_halved(jnp.concatenate([added(early), added(late)], axis=1), high_bit)
    sent.append(turned_send(parts[1], 0))
    small = small + plane_steps[1](small)
    qkv_step, small, rest_got, down_got, sent[0], parts[2] = tied(
        qkv_step, small, rest_got, down_got, sent[0], parts[2]
    )
    qkv_own = added(qkv_step)
    qkv_got = across_depth(qkv_own, high_bit)
    sent.append(turned_send(parts[2], 1))
    rest_own = depth_doubled(rest_own, rest_got, high_bit)
    rest_got = across_depth(rest_own, low_bit)
    down_own = depth_doubled(down_own, down_got, high_bit)
    down_got = across_depth(down_own, low_bit)
    for step in plane_steps[2:]:
        small = small + step(small)
    qkv_got, small, sent[1], parts[3] = tied(qkv_got, small, sent[1], parts[3])
    qkv_own = depth_doubled(qkv_own, qkv_got, high_bit)
    qkv_got = across_depth(qkv_own, low_bit)
    sent.append(turned_send(parts[3], 1))
    small = small + depth_steps[0](small)
    qkv_got, rest_got, down_got, small, sent[2] = tied(qkv_got, rest_got, down_got, small, sent[2])
    rest_own = depth_doubled(rest_own, rest_got, low_bit)
    down_own = depth_doubled(down_own, down_got, low_bit)

    def own_block(stack, index):
        return lax.dynamic_slice_in_dim(stack, index * own_rows, own_rows, 0)

    rest_mine = own_block(rest_own, c)
    rest_other = across_cores(own_block(rest_own, 1 - c))
    qkv_own = depth_doubled(qkv_own, qkv_got, low_bit)
    qkv_mine = own_block(qkv_own, c)
    qkv_other = across_cores(own_block(qkv_own, 1 - c))
    for step in depth_steps[1:]:
        small = small + step(small)
    input_grad = turned_settled(
        [jnp.concatenate(sent[0:2], axis=0), jnp.concatenate(sent[2:4], axis=0)]
    )

    loss = small[4, 0] / (valid_count * width)
    own_small = lax.dynamic_slice_in_dim(small, group * own_rows, own_rows, 1)
    out_own = rest_mine[:, half_ff:].astype(FULL) + rest_other[:, half_ff:].astype(FULL)
    sides = [jnp.where(is_first, rest_mine, rest_other), jnp.where(is_first, rest_other, rest_mine)]
    up_own = jnp.concatenate(
        [side[:, q * block : (q + 1) * block] for q in range(pairs) for side in sides], axis=1
    )
    qkv_own = jnp.stack(
        [jnp.where(is_first, qkv_mine, qkv_other), jnp.where(is_first, qkv_other, qkv_mine)]
    )
    qkv_own = qkv_own.reshape(2, own_rows, head_pairs, 3, 2, HEAD_DIM)
    qkv_own = jnp.transpose(qkv_own, (1, 0, 2, 4, 3, 5)).reshape(own_rows, 3 * width)
    return (
        activations, loss, input_grad, own_small[0], own_small[1], qkv_own.astype(FULL),
        out_own, own_small[2], own_small[3], up_own.astype(FULL), down_own.astype(FULL),
    )


def solution(mesh):
    groups, depth = mesh.shape["dp"], mesh.shape["seq"]
    split = Mesh(mesh.devices.reshape(groups // 2, 2, depth), AXES)
    dp = ("pair", "core")
    rows3 = P(dp, "seq", None)
    in_specs = (
        rows3, rows3, P(dp, "seq"), P(), P(), P(dp), P(dp), P(dp, None), P(dp, None),
        P(dp), P(dp), P(dp, None), P(dp, None),
    )
    out_specs = (
        rows3, P(), rows3, P(dp), P(dp), P(dp, None), P(dp, None), P(dp), P(dp),
        P(dp, None), P(dp, None),
    )
    return jax.shard_map(shards, mesh=split, in_specs=in_specs, out_specs=out_specs, check_vma=False)
```

```python
import functools
import math

import jax
import jax.numpy as jnp
from jax import lax
from jax.experimental import pallas as pl
from jax.experimental.layout import Layout, with_layout_constraint
from jax.experimental.pallas import tpu as pltpu
from jax.sharding import Mesh
from jax.sharding import PartitionSpec as P

HEADS = 12
HEAD_DIM = 64
EPSILON = 1e-12
NEGATIVE = -1e30
SCALE = 1.0 / math.sqrt(HEAD_DIM)
AXES = ("pair", "core", "seq")
NT = (((1,), (1,)), ((), ()))
NN = (((1,), (0,)), ((), ()))
TN = (((0,), (0,)), ((), ()))
LOW = jnp.bfloat16
FULL = jnp.float32


def dot(left, right, form):
    return lax.dot_general(left, right, form, preferred_element_type=FULL)


def row_major(value):
    return with_layout_constraint(value, Layout(major_to_minor=tuple(range(value.ndim))))


def moved(value, target):
    pairs, cores, depth = (lax.axis_size(name) for name in AXES)
    links = []
    for p in range(pairs):
        for c in range(cores):
            for z in range(depth):
                q, e, w = target(p, c, z)
                links.append(((p * cores + c) * depth + z, (q * cores + e) * depth + w))
    return lax.ppermute(value, AXES, links)


def across_cores(value):
    return moved(value, lambda p, c, z: (p, 1 - c, z))


def across_pairs(value, bit):
    return moved(value, lambda p, c, z: (p ^ bit, c, z))


def across_depth(value, bit):
    return moved(value, lambda p, c, z: (p, c, z ^ bit))


def pair_bits():
    return [1 << level for level in range(lax.axis_size("pair").bit_length() - 1)]


def turned_parts(stack):
    z = lax.axis_index("seq")
    got = []
    for step in range(2):
        piece = lax.dynamic_index_in_dim(stack, (z + step) % 2, 0, keepdims=False)
        got.append(moved(piece, lambda p, c, w: (p, w // 2, 2 * c + (w + step) % 2)))
    return got


def turned_settled(got):
    even = lax.axis_index("seq") % 2 == 0
    return jnp.stack([jnp.where(even, got[0], got[1]), jnp.where(even, got[1], got[0])])


def turned(stack):
    return turned_settled(turned_parts(stack))


def sum_steps():
    depth_steps = [
        functools.partial(across_depth, bit=1 << level)
        for level in range(lax.axis_size("seq").bit_length() - 1)
    ]
    pair_steps = [functools.partial(across_pairs, bit=bit) for bit in pair_bits()]
    return depth_steps, [across_cores] + pair_steps


def gathered_over_pairs(value):
    p = lax.axis_index("pair")
    if lax.axis_size("pair") <= 4:
        count = lax.axis_size("pair")
        layout = tuple((k, k, 0, 0, value.shape[0]) for k in range(count))
        return [value] + [across_pairs(value, k) for k in range(1, count)], p, layout
    rows, width = value.shape
    bits = pair_bits()
    count = 1 << len(bits)
    halves = []
    for which in range(2):
        order = bits if which == 0 else bits[::-1]
        current = value[which * rows // 2 : (which + 1) * rows // 2]
        for bit in order:
            other = across_pairs(current, bit)
            flag = jnp.bitwise_and(p, bit) != 0
            current = jnp.stack(
                [jnp.where(flag, other, current), jnp.where(flag, current, other)]
            )
        if which == 1:
            lead = tuple(range(len(bits)))[::-1]
            current = jnp.transpose(current, lead + (len(bits), len(bits) + 1))
        halves.append(current.reshape(count, rows // 2, width))
    return [jnp.concatenate(halves, axis=1).reshape(count * rows, width)], None, ()


def place_kernel(p_ref, *refs, segments, layout, count):
    sources, results = refs[:count], refs[count:]
    for k, source, origin, first, size in layout:
        spot = jnp.bitwise_xor(p_ref[0], k)
        for index, row, rows, column, width, target in segments:
            low, high = max(row, first), min(row + rows, first + size)
            if low < high:
                start = pl.multiple_of(spot * rows + (low - row), 16)
                results[index][pl.ds(start, high - low), target : target + width] = sources[source][
                    low - first + origin : high - first + origin, column : column + width
                ]


def placed(gathered, segments):
    pieces, p, layout = gathered
    pairs = lax.axis_size("pair")
    outs = 1 + max(segment[0] for segment in segments)
    if p is None:
        stack = pieces[0].reshape(pairs, -1, pieces[0].shape[1])
        results = []
        for index in range(outs):
            parts = [
                stack[:, row : row + rows, column : column + width].reshape(pairs * rows, width)
                for which, row, rows, column, width, _ in segments
                if which == index
            ]
            results.append(jnp.concatenate(parts, axis=1))
        return results
    shapes = []
    for index in range(outs):
        mine = [segment for segment in segments if segment[0] == index]
        shapes.append(
            jax.ShapeDtypeStruct((pairs * mine[0][2], sum(part[4] for part in mine)), LOW)
        )
    local = pl.BlockSpec(memory_space=pltpu.VMEM)
    return pl.pallas_call(
        functools.partial(place_kernel, segments=segments, layout=layout, count=len(pieces)),
        in_specs=[pl.BlockSpec(memory_space=pltpu.SMEM)] + [local] * len(pieces),
        out_specs=[local] * outs,
        out_shape=shapes,
        name="place",
    )(p.astype(jnp.int32).reshape(1), *pieces)


def scattered_over_pairs(value):
    p = lax.axis_index("pair")
    if lax.axis_size("pair") <= 4:
        rows = value.shape[0] // lax.axis_size("pair")
        pieces = []
        for k in range(lax.axis_size("pair")):
            piece = lax.dynamic_slice_in_dim(value, jnp.bitwise_xor(p, k) * rows, rows, 0)
            pieces.append(across_pairs(piece, k) if k else piece)
        return pieces
    bits = pair_bits()
    count = 1 << len(bits)
    rows, width = value.shape[0] // count, value.shape[1]
    blocks = value.reshape(count, rows, width)
    halves = []
    for which in range(2):
        order = bits if which == 0 else bits[::-1]
        current = blocks[:, which * rows // 2 : (which + 1) * rows // 2]
        current = current.reshape((2,) * len(bits) + (rows // 2, width))
        left = bits[::-1]
        for bit in order:
            axis = left.index(bit)
            mine = jnp.where(jnp.bitwise_and(p, bit) != 0, 1, 0)
            keep = lax.dynamic_index_in_dim(current, mine, axis, keepdims=False)
            send = lax.dynamic_index_in_dim(current, 1 - mine, axis, keepdims=False)
            current = keep + across_pairs(send, bit)
            left = [other for other in left if other != bit]
        halves.append(current)
    return [jnp.concatenate(halves, axis=0)]


def added(pieces):
    total = pieces[0].astype(FULL)
    for piece in pieces[1:]:
        total = total + piece.astype(FULL)
    return total.astype(LOW)


def depth_flag(bit):
    return jnp.where(jnp.bitwise_and(lax.axis_index("seq"), bit) != 0, 1, 0)


def depth_halved(value, bit):
    mine = depth_flag(bit)
    parts = value.reshape((2, value.shape[0] // 2) + value.shape[1:])
    keep = lax.dynamic_index_in_dim(parts, mine, 0, keepdims=False)
    send = lax.dynamic_index_in_dim(parts, 1 - mine, 0, keepdims=False)
    return [keep, across_depth(send, bit)]


def depth_doubled(value, other, bit):
    mine = depth_flag(bit)
    return jnp.concatenate(
        [jnp.where(mine == 0, value, other), jnp.where(mine == 0, other, value)], axis=0
    )


def tied(*values):
    return lax.optimization_barrier(values)


def keys_with_mask(k_ref, counts_ref, ka, rows):
    lane = lax.broadcasted_iota(jnp.int32, (rows, 128), 1)
    spot = lax.broadcasted_iota(jnp.int32, (rows, 128), 0)
    limit = jnp.where(spot < rows // 2, counts_ref[0], counts_ref[1] + rows // 2)
    bias = jnp.where(spot < limit, 0.0, NEGATIVE)
    k = k_ref[...].astype(FULL)
    ka[0] = jnp.where(lane < 64, k, jnp.where(lane == 64, bias, 0.0)).astype(LOW)
    ka[1] = jnp.where(lane >= 64, k, jnp.where(lane == 0, bias, 0.0)).astype(LOW)


def forward_kernel(counts_ref, q_ref, k_ref, v_ref, o_ref, lse_ref, ka, vt, *, rows, block):
    @pl.when(pl.program_id(1) == 0)
    def _():
        keys_with_mask(k_ref, counts_ref, ka, rows)
        vt[...] = v_ref[...].T

    lane = lax.broadcasted_iota(jnp.int32, (block, 128), 1)
    q = q_ref[...].astype(FULL) * SCALE
    mixed = []
    for h in range(2):
        mine = (lane < 64) if h == 0 else (lane >= 64)
        flag = lane == (64 if h == 0 else 0)
        qa = jnp.where(mine, q, jnp.where(flag, 1.0, 0.0)).astype(LOW)
        scores = dot(ka[h], qa, NT)
        highest = jnp.max(scores, axis=0, keepdims=True)
        exponent = jnp.exp(scores - highest)
        totals = jnp.sum(exponent, axis=0, keepdims=True)
        part = dot(vt[pl.ds(64 * h, 64), :], exponent.astype(LOW), NN)
        mixed.append(part * (1.0 / totals))
        lse_ref[0, pl.ds(h, 1), :] = highest + jnp.log(totals)
    o_ref[...] = jnp.concatenate(mixed, axis=0).T.astype(LOW)


def attention_forward(counts, qkv, block):
    rows, width = qkv.shape
    pairs = width // 384
    return pl.pallas_call(
        functools.partial(forward_kernel, rows=rows, block=block),
        grid_spec=pltpu.PrefetchScalarGridSpec(
            num_scalar_prefetch=1,
            grid=(pairs, rows // block),
            in_specs=[
                pl.BlockSpec((block, 128), lambda h, i, n: (i, 3 * h)),
                pl.BlockSpec((rows, 128), lambda h, i, n: (0, 3 * h + 1)),
                pl.BlockSpec((rows, 128), lambda h, i, n: (0, 3 * h + 2)),
            ],
            out_specs=[
                pl.BlockSpec((block, 128), lambda h, i, n: (i, h)),
                pl.BlockSpec((1, 2, block), lambda h, i, n: (h, 0, i)),
            ],
            scratch_shapes=[pltpu.VMEM((2, rows, 128), LOW), pltpu.VMEM((128, rows), LOW)],
        ),
        out_shape=[
            jax.ShapeDtypeStruct((rows, pairs * 128), LOW),
            jax.ShapeDtypeStruct((pairs, 2, rows), FULL),
        ],
        cost_estimate=pl.CostEstimate(flops=1, bytes_accessed=1, transcendentals=0),
        name="attention_forward",
    )(counts, qkv, qkv, qkv)


def backward_kernel(
    counts_ref, q_ref, k_ref, v_ref, o_ref, g_ref, lse_ref, grad_ref,
    ka, va, kt, dk, dv, *, rows, block, steps, chunk,
):
    step = pl.program_id(0)

    @pl.when(step == 0)
    def _():
        keys_with_mask(k_ref, counts_ref, ka, rows)
        lane = lax.broadcasted_iota(jnp.int32, (rows, 128), 1)
        v = v_ref[...].astype(FULL)
        va[0] = jnp.where(lane < 64, v, 0.0).astype(LOW)
        va[1] = jnp.where(lane >= 64, v, 0.0).astype(LOW)
        kt[...] = k_ref[...].T
        dk[...] = jnp.zeros_like(dk)
        dv[...] = jnp.zeros_like(dv)

    lane = lax.broadcasted_iota(jnp.int32, (block, 128), 1)
    q = q_ref[...].astype(FULL)
    g = g_ref[...]
    wide = g.astype(FULL)
    product = (wide * o_ref[...].astype(FULL)).T
    scaled = q * SCALE
    columns = []
    for h in range(2):
        mine = (lane < 64) if h == 0 else (lane >= 64)
        flag = lane == (64 if h == 0 else 0)
        qa = jnp.where(mine, scaled, jnp.where(flag, 1.0, 0.0)).astype(LOW)
        qm = jnp.where(mine, q, 0.0).astype(LOW)
        gm = jnp.where(mine, wide, 0.0).astype(LOW)
        delta = jnp.sum(product[64 * h : 64 * h + 64], axis=0, keepdims=True)
        lse = lse_ref[0, pl.ds(h, 1), :]
        total = jnp.zeros((64, block), FULL)
        for c in range(rows // chunk):
            part = pl.ds(c * chunk, chunk)
            probs = jnp.exp(dot(ka[h, part, :], qa, NT) - lse)
            grad_probs = dot(va[h, part, :], g, NT)
            grad_scores = (probs * (grad_probs - delta)).astype(LOW)
            dv[part, :] += dot(probs.astype(LOW), gm, NN)
            dk[part, :] += dot(grad_scores, qm, NN)
            total = total + dot(kt[pl.ds(64 * h, 64), part], grad_scores, NN)
        columns.append(total)
    spot = pl.ds(pl.multiple_of(step * block, block), block)
    grad_ref[spot, 0:128] = (jnp.concatenate(columns, axis=0).T * SCALE).astype(LOW)

    @pl.when(step == steps - 1)
    def _():
        grad_ref[:, 128:256] = (dk[...] * SCALE).astype(LOW)
        grad_ref[:, 256:384] = dv[...].astype(LOW)


def attention_backward(counts, qkv, mixed, grad, lse, pair, block, chunk):
    rows = qkv.shape[0]
    steps = rows // block
    return pl.pallas_call(
        functools.partial(backward_kernel, rows=rows, block=block, steps=steps, chunk=chunk),
        grid_spec=pltpu.PrefetchScalarGridSpec(
            num_scalar_prefetch=1,
            grid=(steps,),
            in_specs=[
                pl.BlockSpec((block, 128), lambda i, n: (i, 3 * pair)),
                pl.BlockSpec((rows, 128), lambda i, n: (0, 3 * pair + 1)),
                pl.BlockSpec((rows, 128), lambda i, n: (0, 3 * pair + 2)),
                pl.BlockSpec((block, 128), lambda i, n: (i, pair)),
                pl.BlockSpec((block, 128), lambda i, n: (i, pair)),
                pl.BlockSpec((1, 2, block), lambda i, n: (pair, 0, i)),
            ],
            out_specs=pl.BlockSpec((rows, 384), lambda i, n: (0, 0)),
            scratch_shapes=[
                pltpu.VMEM((2, rows, 128), LOW),
                pltpu.VMEM((2, rows, 128), LOW),
                pltpu.VMEM((128, rows), LOW),
                pltpu.VMEM((rows, 128), FULL),
                pltpu.VMEM((rows, 128), FULL),
            ],
        ),
        out_shape=jax.ShapeDtypeStruct((rows, 384), LOW),
        cost_estimate=pl.CostEstimate(flops=1, bytes_accessed=1, transcendentals=0),
        name="attention_backward",
    )(counts, qkv, qkv, qkv, mixed, grad, lse)


def norm_parts(values):
    center = values - jnp.mean(values, axis=-1, keepdims=True)
    inverse = lax.rsqrt(jnp.mean(center * center, axis=-1, keepdims=True) + EPSILON)
    return center * inverse, inverse


def norm_backward(upstream, unit, inverse, gain):
    scaled = upstream * gain
    first = jnp.mean(scaled, axis=-1, keepdims=True)
    second = jnp.mean(scaled * unit, axis=-1, keepdims=True)
    result = inverse * (scaled - first - unit * second)
    return result, jnp.sum(upstream * unit, axis=0), jnp.sum(upstream, axis=0)


def gelu_parts(values):
    share = 0.5 * (1.0 + lax.erf(values * (1.0 / math.sqrt(2.0))))
    density = jnp.exp(-0.5 * values * values) * (1.0 / math.sqrt(2.0 * math.pi))
    return values * share, share + values * density


def shards(
    tokens, teacher, teach_mask, lengths, deal_group,
    ln1_gain, ln1_bias, qkv_weight, out_weight, ln2_gain, ln2_bias, up_weight, down_weight,
):
    pairs, cores, depth = (lax.axis_size(name) for name in AXES)
    p, c, z = (lax.axis_index(name) for name in AXES)
    groups = pairs * cores
    slot_rows, width = tokens.shape[1], tokens.shape[2]
    rows = 2 * slot_rows
    full_len = depth * slot_rows
    seq_count = lengths.shape[0]
    ff = up_weight.shape[1]
    own_rows = width // groups
    pair_rows = cores * own_rows
    half_width = width // 2
    half_ff = ff // 2
    is_first = c == 0

    def in_order(mine, other, axis):
        return jnp.concatenate(
            [jnp.where(is_first, mine, other), jnp.where(is_first, other, mine)], axis=axis
        )

    sequence = 2 * cores * p + z
    length = jnp.sum(jnp.where(jnp.arange(seq_count) == sequence, lengths, 0))
    base = c * rows
    counts = jnp.stack([length - base, length - (rows - base)])
    counts = jnp.clip(counts, 0, rows).astype(jnp.int32)

    heads_half = HEADS // 2
    head_pairs = heads_half // 2
    wide_half = 3 * half_width
    shard = qkv_weight.reshape(own_rows, 2, head_pairs, 2, 3, HEAD_DIM)
    shard = jnp.transpose(shard, (1, 0, 2, 4, 3, 5)).reshape(2, own_rows, wide_half)
    vectors = jnp.stack([ln1_gain, ln1_bias, ln2_gain, ln2_bias], axis=1)
    vectors = jnp.pad(vectors, ((0, 0), (0, 124)))
    vectors = jnp.broadcast_to(vectors[None], (2, own_rows, 128))
    shard = jnp.concatenate([shard, vectors], axis=2)
    keep = lax.dynamic_index_in_dim(shard, c, 0, keepdims=False)
    send = lax.dynamic_index_in_dim(shard, 1 - c, 0, keepdims=False)
    qkv_shard = in_order(keep, across_cores(send), 0)

    x_rows = turned(tokens).reshape(rows, width)

    masks = deal_group[0:2]
    group = p * cores + c
    sources = jnp.bitwise_xor(group, masks) * 2 + jnp.arange(2, dtype=jnp.int32)
    picked = jnp.arange(seq_count, dtype=jnp.int32)[None, :] == sources[:, None]
    dealt_len = jnp.sum(jnp.where(picked, lengths[None, :], 0), axis=1)
    positions = z * slot_rows + jnp.arange(slot_rows, dtype=jnp.int32)
    live = (positions[None, :] < dealt_len[:, None]) & (teach_mask == 1)
    tally = jnp.full((8, 128), jnp.sum(live.astype(FULL)))
    tally = tally + across_cores(tally)

    mask_rows = jnp.pad(
        teach_mask.astype(LOW)[:, None, :], ((0, 0), (0, 15), (0, width - slot_rows))
    )
    slots = jnp.concatenate([teacher, mask_rows], axis=1)

    def dealt(slots, level):
        flagged = jnp.bitwise_and(jnp.right_shift(masks[0], level), 1) == 1
        outgoing = jnp.where(flagged, slots[0], slots[1])
        incoming = across_cores(outgoing) if level == 0 else across_pairs(outgoing, 1 << (level - 1))
        return [flagged, slots, incoming]

    def settled(flagged, slots, incoming):
        return jnp.stack(
            [jnp.where(flagged, incoming, slots[0]), jnp.where(flagged, slots[1], incoming)]
        )

    levels = groups.bit_length() - 1
    deal = dealt(slots, 0)
    deal, tally = tied(deal, tally)
    depth_steps, plane_steps = sum_steps()
    tally = tally + plane_steps[1](tally)
    deal = dealt(settled(*deal), 1)
    qkv_shard, deal, tally = tied(qkv_shard, deal, tally)
    qkv_pieces = gathered_over_pairs(qkv_shard)

    block = ff // groups

    def unit_blocks(part):
        return jnp.concatenate(
            [up_weight[:, (2 * q + part) * block : (2 * q + part + 1) * block] for q in range(pairs)],
            axis=1,
        )

    up_parts = [unit_blocks(0), unit_blocks(1)]
    keep = jnp.where(is_first, up_parts[0], up_parts[1])
    send = jnp.where(is_first, up_parts[1], up_parts[0])
    got = across_cores(jnp.concatenate([send[:, :width], send[:, width:], out_weight], axis=0))
    up_shard = in_order(keep, jnp.concatenate([got[:own_rows], got[own_rows : 2 * own_rows]], axis=1), 0)
    out_shard = in_order(out_weight, got[2 * own_rows :], 0)
    payload = jnp.concatenate(
        [down_weight, up_shard[:, :width], up_shard[:, width:], out_shard], axis=0
    )
    down_rows = down_weight.shape[0]
    payload_plan = (
        (0, 0, down_rows, 0, width, 0),
        (1, down_rows, pair_rows, 0, width, 0),
        (1, down_rows + pair_rows, pair_rows, 0, width, width),
        (2, down_rows + 2 * pair_rows, pair_rows, 0, width, 0),
    )
    for step in plane_steps[2:]:
        tally = tally + step(tally)
    x_rows, payload, tally, deal = tied(x_rows, payload, tally, deal)
    for level in range(2, levels):
        deal = dealt(settled(*deal), level)
    tally = tally + depth_steps[0](tally)

    x_full = x_rows.astype(FULL)
    unit_one, inverse_one = norm_parts(x_full)
    w_qkv, vectors = placed(
        qkv_pieces,
        ((0, 0, pair_rows, 0, wide_half, 0), (1, 0, pair_rows, wide_half, 128, 0)),
    )
    pick = lax.broadcasted_iota(jnp.int32, (8, 128), 0) == lax.broadcasted_iota(jnp.int32, (8, 128), 1)
    vectors = dot(pick.astype(LOW), vectors, NT)
    gain_one, shift_one, gain_two, shift_two = vectors[0], vectors[1], vectors[2], vectors[3]
    norm_mine = (unit_one * gain_one + shift_one).astype(LOW)
    norm_got = across_cores(norm_mine)
    norm_got, deal, payload, tally = tied(norm_got, deal, payload, tally)
    goal_moved = turned_parts(settled(*deal))
    payload_pieces = gathered_over_pairs(payload)
    norm_one = jnp.concatenate([norm_mine, norm_got], axis=0)
    for step in depth_steps[1:]:
        tally = tally + step(tally)
    qkv = dot(norm_one, w_qkv, NN).astype(LOW)
    mixed, lse = attention_forward(counts, qkv, 512)

    sources, *place_args = payload_pieces
    mixed, sources, goal_moved, tally = tied(mixed, sources, goal_moved, tally)
    mixed_got = across_cores(mixed[rows:])
    goal = turned_settled(goal_moved)
    w_down, w_up, w_out = placed((sources, *place_args), payload_plan)

    attended = in_order(mixed[:rows], mixed_got, 1)
    middle = x_full + dot(attended, w_out, NN)
    unit_two, inverse_two = norm_parts(middle)
    norm_two = (unit_two * gain_two + shift_two).astype(LOW)
    norm_other = across_cores(norm_two)

    def expanded(low):
        value, slope = gelu_parts(dot(low, w_up, NN))
        return value.astype(LOW), slope.astype(LOW)

    active_mine, slope_mine = expanded(norm_two)
    active_other, slope_other = expanded(norm_other)
    part_other = row_major(dot(active_other, w_down, NN).astype(LOW))
    part_mine = row_major(dot(active_mine, w_down, NN))
    output = middle + part_mine + across_cores(part_other).astype(FULL)

    output, goal, tally = tied(output, goal, tally)
    valid_count = tally[0, 0]
    spots = base + jnp.arange(rows, dtype=jnp.int32)
    taught = goal[:, slot_rows, :slot_rows].reshape(rows)
    valid = ((spots < length) & (taught == 1)).astype(FULL)[:, None]
    error = output - goal[:, :slot_rows].reshape(rows, width).astype(FULL)
    squares = jnp.sum(valid * error * error)
    factor = seq_count * full_len * 1.0 / valid_count
    grad_out = valid * (2.0 * factor) * error
    grad_ff = grad_out.astype(LOW)
    grad_ff_other = across_cores(grad_ff)
    output_moved = turned_parts(output.astype(LOW).reshape(2, slot_rows, width))
    hidden_mine = (dot(grad_ff, w_down, NT) * slope_mine.astype(FULL)).astype(LOW)
    down_grad = (dot(active_mine, grad_ff, TN) + dot(active_other, grad_ff_other, TN)).astype(LOW)
    down_grad, grad_ff_other, hidden_mine = tied(down_grad, grad_ff_other, hidden_mine)
    down_sum = scattered_over_pairs(down_grad)
    hidden_other = (dot(grad_ff_other, w_down, NT) * slope_other.astype(FULL)).astype(LOW)
    back_other = dot(hidden_other, w_up, NT).astype(LOW)
    back_got = across_cores(back_other)
    back_mine = dot(hidden_mine, w_up, NT)
    up_grad = (dot(norm_two, hidden_mine, TN) + dot(norm_other, hidden_other, TN)).astype(LOW)
    grad_mid, gain_two_grad, shift_two_grad = norm_backward(
        back_mine + back_got.astype(FULL), unit_two, inverse_two, gain_two
    )
    grad_middle = grad_out + grad_mid
    grad_branch = grad_middle.astype(LOW)
    grad_attended = dot(grad_branch, w_out, NT).astype(LOW)
    keep = jnp.where(is_first, grad_attended[:, :half_width], grad_attended[:, half_width:])
    send = jnp.where(is_first, grad_attended[:, half_width:], grad_attended[:, :half_width])
    mixed_grad_got = across_cores(send)
    out_grad = dot(attended, grad_branch, TN).astype(LOW)
    rest_sum = scattered_over_pairs(jnp.concatenate([up_grad, out_grad], axis=1))
    grad_mixed = jnp.concatenate([keep, mixed_grad_got], axis=0)

    def attend(pair, gate):
        return attention_backward(gate, qkv, mixed, grad_mixed, lse, pair, 512, 512)

    def weight_part(grads):
        return dot(norm_one, grads, TN).astype(LOW)

    low_bit, high_bit = 1, depth // 2
    first = attend(0, counts)
    first, down_sum, output_moved, gate = tied(first, down_sum, output_moved, counts)
    activations = turned_settled(output_moved)
    down_step = depth_halved(added(down_sum), low_bit)
    second = attend(1, gate)
    second, first, down_step, rest_sum, gate = tied(second, first, down_step, rest_sum, counts)
    down_step = depth_halved(added(down_step), high_bit)
    rest_step = depth_halved(added(rest_sum), low_bit)
    early = scattered_over_pairs(weight_part(jnp.concatenate([first, second], axis=1)))
    third = attend(2, gate)
    third, first, second, down_step, rest_step, early = tied(
        third, first, second, down_step, rest_step, early
    )

    partial = row_major(dot(jnp.concatenate([first, second, third], axis=1), w_qkv, NT))
    back_got = across_cores(partial[rows:].astype(LOW))
    early = depth_halved(added(early), low_bit)
    rest_step = depth_halved(added(rest_step), high_bit)
    down_own = added(down_step)
    down_got = across_depth(down_own, high_bit)
    late = scattered_over_pairs(weight_part(third))
    grad_norm_one = partial[:rows] + back_got.astype(FULL)
    grad_in, gain_one_grad, shift_one_grad = norm_backward(
        grad_norm_one, unit_one, inverse_one, gain_one
    )
    grad_rows = row_major((grad_middle + grad_in).astype(LOW))
    input_moved = turned_parts(grad_rows.reshape(2, slot_rows, width))

    row_index = lax.broadcasted_iota(jnp.int32, (8, width), 0)
    small = jnp.zeros((8, width), FULL)
    for index, value in enumerate(
        [gain_one_grad, shift_one_grad, gain_two_grad, shift_two_grad, jnp.full((width,), squares)]
    ):
        small = jnp.where(row_index == index, value[None, :], small)
    small = small + plane_steps[0](small)

    late = depth_halved(added(late), low_bit)
    rest_own = added(rest_step)
    rest_got = across_depth(rest_own, high_bit)
    late, early, small = tied(late, early, small)
    qkv_step = depth_halved(jnp.concatenate([added(early), added(late)], axis=1), high_bit)
    small = small + depth_steps[0](small)
    qkv_step, small, rest_got, down_got, near = tied(
        qkv_step, small, rest_got, down_got, input_moved[0]
    )
    qkv_own = added(qkv_step)
    qkv_got = across_depth(qkv_own, high_bit)
    for step in depth_steps[1:]:
        small = small + step(small)
    rest_own = depth_doubled(rest_own, rest_got, high_bit)
    rest_got = across_depth(rest_own, low_bit)
    down_own = depth_doubled(down_own, down_got, high_bit)
    down_got = across_depth(down_own, low_bit)
    qkv_got, small, far = tied(qkv_got, small, input_moved[1])
    qkv_own = depth_doubled(qkv_own, qkv_got, high_bit)
    qkv_got = across_depth(qkv_own, low_bit)
    small = small + plane_steps[1](small)
    qkv_got, rest_got, down_got, small = tied(qkv_got, rest_got, down_got, small)
    rest_own = depth_doubled(rest_own, rest_got, low_bit)
    down_own = depth_doubled(down_own, down_got, low_bit)

    def own_block(stack, index):
        return lax.dynamic_slice_in_dim(stack, index * own_rows, own_rows, 0)

    rest_mine = own_block(rest_own, c)
    rest_other = across_cores(own_block(rest_own, 1 - c))
    qkv_own = depth_doubled(qkv_own, qkv_got, low_bit)
    qkv_mine = own_block(qkv_own, c)
    qkv_other = across_cores(own_block(qkv_own, 1 - c))
    for step in plane_steps[2:]:
        small = small + step(small)
    input_grad = turned_settled([near, far])

    loss = small[4, 0] / (valid_count * width)
    own_small = lax.dynamic_slice_in_dim(small, group * own_rows, own_rows, 1)
    out_own = rest_mine[:, half_ff:].astype(FULL) + rest_other[:, half_ff:].astype(FULL)
    sides = [jnp.where(is_first, rest_mine, rest_other), jnp.where(is_first, rest_other, rest_mine)]
    up_own = jnp.concatenate(
        [side[:, q * block : (q + 1) * block] for q in range(pairs) for side in sides], axis=1
    )
    qkv_own = jnp.stack(
        [jnp.where(is_first, qkv_mine, qkv_other), jnp.where(is_first, qkv_other, qkv_mine)]
    )
    qkv_own = qkv_own.reshape(2, own_rows, head_pairs, 3, 2, HEAD_DIM)
    qkv_own = jnp.transpose(qkv_own, (1, 0, 2, 4, 3, 5)).reshape(own_rows, 3 * width)
    return (
        activations, loss, input_grad, own_small[0], own_small[1], qkv_own.astype(FULL),
        out_own, own_small[2], own_small[3], up_own.astype(FULL), down_own.astype(FULL),
    )


def solution(mesh):
    groups, depth = mesh.shape["dp"], mesh.shape["seq"]
    split = Mesh(mesh.devices.reshape(groups // 2, 2, depth), AXES)
    dp = ("pair", "core")
    rows3 = P(dp, "seq", None)
    in_specs = (
        rows3, rows3, P(dp, "seq"), P(), P(), P(dp), P(dp), P(dp, None), P(dp, None),
        P(dp), P(dp), P(dp, None), P(dp, None),
    )
    out_specs = (
        rows3, P(), rows3, P(dp), P(dp), P(dp, None), P(dp, None), P(dp), P(dp),
        P(dp, None), P(dp, None),
    )
    return jax.shard_map(shards, mesh=split, in_specs=in_specs, out_specs=out_specs, check_vma=False)
```

```python
import functools
import math

import jax
import jax.numpy as jnp
from jax import lax
from jax.experimental import pallas as pl
from jax.experimental.layout import Layout, with_layout_constraint
from jax.experimental.pallas import tpu as pltpu
from jax.sharding import Mesh
from jax.sharding import PartitionSpec as P

HEADS = 12
HEAD_DIM = 64
EPSILON = 1e-12
NEGATIVE = -1e30
SCALE = 1.0 / math.sqrt(HEAD_DIM)
AXES = ("pair", "core", "seq")
NT = (((1,), (1,)), ((), ()))
NN = (((1,), (0,)), ((), ()))
TN = (((0,), (0,)), ((), ()))
LOW = jnp.bfloat16
FULL = jnp.float32


def dot(left, right, form):
    return lax.dot_general(left, right, form, preferred_element_type=FULL)


def row_major(value):
    return with_layout_constraint(value, Layout(major_to_minor=tuple(range(value.ndim))))


def moved(value, target):
    pairs, cores, depth = (lax.axis_size(name) for name in AXES)
    links = []
    for p in range(pairs):
        for c in range(cores):
            for z in range(depth):
                q, e, w = target(p, c, z)
                links.append(((p * cores + c) * depth + z, (q * cores + e) * depth + w))
    return lax.ppermute(value, AXES, links)


def across_cores(value):
    return moved(value, lambda p, c, z: (p, 1 - c, z))


def across_pairs(value, bit):
    return moved(value, lambda p, c, z: (p ^ bit, c, z))


def across_depth(value, bit):
    return moved(value, lambda p, c, z: (p, c, z ^ bit))


def pair_bits():
    return [1 << level for level in range(lax.axis_size("pair").bit_length() - 1)]


def turned_parts(stack):
    z = lax.axis_index("seq")
    got = []
    for step in range(2):
        piece = lax.dynamic_index_in_dim(stack, (z + step) % 2, 0, keepdims=False)
        got.append(moved(piece, lambda p, c, w: (p, w // 2, 2 * c + (w + step) % 2)))
    return got


def turned_settled(got):
    even = lax.axis_index("seq") % 2 == 0
    return jnp.stack([jnp.where(even, got[0], got[1]), jnp.where(even, got[1], got[0])])


def turned(stack):
    return turned_settled(turned_parts(stack))


def sum_steps():
    depth_steps = [
        functools.partial(across_depth, bit=1 << level)
        for level in range(lax.axis_size("seq").bit_length() - 1)
    ]
    pair_steps = [functools.partial(across_pairs, bit=bit) for bit in pair_bits()]
    return depth_steps, [across_cores] + pair_steps


def gathered_over_pairs(value):
    p = lax.axis_index("pair")
    if lax.axis_size("pair") <= 4:
        count = lax.axis_size("pair")
        layout = tuple((k, k, 0, 0, value.shape[0]) for k in range(count))
        return [value] + [across_pairs(value, k) for k in range(1, count)], p, layout
    rows, width = value.shape
    bits = pair_bits()
    count = 1 << len(bits)
    halves = []
    for which in range(2):
        order = bits if which == 0 else bits[::-1]
        current = value[which * rows // 2 : (which + 1) * rows // 2]
        for bit in order:
            other = across_pairs(current, bit)
            flag = jnp.bitwise_and(p, bit) != 0
            current = jnp.stack(
                [jnp.where(flag, other, current), jnp.where(flag, current, other)]
            )
        if which == 1:
            lead = tuple(range(len(bits)))[::-1]
            current = jnp.transpose(current, lead + (len(bits), len(bits) + 1))
        halves.append(current.reshape(count, rows // 2, width))
    return [jnp.concatenate(halves, axis=1).reshape(count * rows, width)], None, ()


def halves_first(value):
    if lax.axis_size("pair") != 4:
        return value, None
    rows = value.shape[0] // 2
    return value, (across_pairs(value[:rows], 1), across_pairs(value[rows:], 2))


def halves_second(state):
    value, near = state
    if near is None:
        return gathered_over_pairs(value)
    rows = value.shape[0] // 2
    upper = across_pairs(jnp.concatenate([value[:rows], near[0]], axis=0), 2)
    lower = across_pairs(jnp.concatenate([value[rows:], near[1]], axis=0), 1)
    layout = (
        (0, 0, 0, 0, 2 * rows),
        (1, 1, 0, 0, rows), (1, 4, 0, rows, rows),
        (2, 3, 0, 0, rows), (2, 2, 0, rows, rows),
        (3, 3, rows, 0, rows), (3, 4, rows, rows, rows),
    )
    return [value, near[0], near[1], upper, lower], lax.axis_index("pair"), layout


def place_kernel(p_ref, *refs, segments, layout, count):
    sources, results = refs[:count], refs[count:]
    for k, source, origin, first, size in layout:
        spot = jnp.bitwise_xor(p_ref[0], k)
        for index, row, rows, column, width, target in segments:
            low, high = max(row, first), min(row + rows, first + size)
            if low < high:
                start = pl.multiple_of(spot * rows + (low - row), 16)
                results[index][pl.ds(start, high - low), target : target + width] = sources[source][
                    low - first + origin : high - first + origin, column : column + width
                ]


def placed(gathered, segments):
    pieces, p, layout = gathered
    pairs = lax.axis_size("pair")
    outs = 1 + max(segment[0] for segment in segments)
    if p is None:
        stack = pieces[0].reshape(pairs, -1, pieces[0].shape[1])
        results = []
        for index in range(outs):
            parts = [
                stack[:, row : row + rows, column : column + width].reshape(pairs * rows, width)
                for which, row, rows, column, width, _ in segments
                if which == index
            ]
            results.append(jnp.concatenate(parts, axis=1))
        return results
    shapes = []
    for index in range(outs):
        mine = [segment for segment in segments if segment[0] == index]
        shapes.append(
            jax.ShapeDtypeStruct((pairs * mine[0][2], sum(part[4] for part in mine)), LOW)
        )
    local = pl.BlockSpec(memory_space=pltpu.VMEM)
    return pl.pallas_call(
        functools.partial(place_kernel, segments=segments, layout=layout, count=len(pieces)),
        in_specs=[pl.BlockSpec(memory_space=pltpu.SMEM)] + [local] * len(pieces),
        out_specs=[local] * outs,
        out_shape=shapes,
        name="place",
    )(p.astype(jnp.int32).reshape(1), *pieces)


def scattered_over_pairs(value):
    p = lax.axis_index("pair")
    if lax.axis_size("pair") <= 4:
        rows = value.shape[0] // lax.axis_size("pair")
        pieces = []
        for k in range(lax.axis_size("pair")):
            piece = lax.dynamic_slice_in_dim(value, jnp.bitwise_xor(p, k) * rows, rows, 0)
            pieces.append(across_pairs(piece, k) if k else piece)
        return pieces
    bits = pair_bits()
    count = 1 << len(bits)
    rows, width = value.shape[0] // count, value.shape[1]
    blocks = value.reshape(count, rows, width)
    halves = []
    for which in range(2):
        order = bits if which == 0 else bits[::-1]
        current = blocks[:, which * rows // 2 : (which + 1) * rows // 2]
        current = current.reshape((2,) * len(bits) + (rows // 2, width))
        left = bits[::-1]
        for bit in order:
            axis = left.index(bit)
            mine = jnp.where(jnp.bitwise_and(p, bit) != 0, 1, 0)
            keep = lax.dynamic_index_in_dim(current, mine, axis, keepdims=False)
            send = lax.dynamic_index_in_dim(current, 1 - mine, axis, keepdims=False)
            current = keep + across_pairs(send, bit)
            left = [other for other in left if other != bit]
        halves.append(current)
    return [jnp.concatenate(halves, axis=0)]


def added(pieces):
    total = pieces[0].astype(FULL)
    for piece in pieces[1:]:
        total = total + piece.astype(FULL)
    return total.astype(LOW)


def depth_flag(bit):
    return jnp.where(jnp.bitwise_and(lax.axis_index("seq"), bit) != 0, 1, 0)


def depth_halved(value, bit):
    mine = depth_flag(bit)
    parts = value.reshape((2, value.shape[0] // 2) + value.shape[1:])
    keep = lax.dynamic_index_in_dim(parts, mine, 0, keepdims=False)
    send = lax.dynamic_index_in_dim(parts, 1 - mine, 0, keepdims=False)
    return [keep, across_depth(send, bit)]


def depth_doubled(value, other, bit):
    mine = depth_flag(bit)
    return jnp.concatenate(
        [jnp.where(mine == 0, value, other), jnp.where(mine == 0, other, value)], axis=0
    )


def tied(*values):
    return lax.optimization_barrier(values)


def keys_with_mask(k_ref, counts_ref, ka, rows):
    lane = lax.broadcasted_iota(jnp.int32, (rows, 128), 1)
    spot = lax.broadcasted_iota(jnp.int32, (rows, 128), 0)
    limit = jnp.where(spot < rows // 2, counts_ref[0], counts_ref[1] + rows // 2)
    bias = jnp.where(spot < limit, 0.0, NEGATIVE)
    k = k_ref[...].astype(FULL)
    ka[0] = jnp.where(lane < 64, k, jnp.where(lane == 64, bias, 0.0)).astype(LOW)
    ka[1] = jnp.where(lane >= 64, k, jnp.where(lane == 0, bias, 0.0)).astype(LOW)


def forward_kernel(counts_ref, q_ref, k_ref, v_ref, o_ref, lse_ref, ka, vt, *, rows, block):
    @pl.when(pl.program_id(1) == 0)
    def _():
        keys_with_mask(k_ref, counts_ref, ka, rows)
        vt[...] = v_ref[...].T

    lane = lax.broadcasted_iota(jnp.int32, (block, 128), 1)
    q = q_ref[...].astype(FULL) * SCALE
    mixed = []
    for h in range(2):
        mine = (lane < 64) if h == 0 else (lane >= 64)
        flag = lane == (64 if h == 0 else 0)
        qa = jnp.where(mine, q, jnp.where(flag, 1.0, 0.0)).astype(LOW)
        scores = dot(ka[h], qa, NT)
        highest = jnp.max(scores, axis=0, keepdims=True)
        exponent = jnp.exp(scores - highest)
        totals = jnp.sum(exponent, axis=0, keepdims=True)
        part = dot(vt[pl.ds(64 * h, 64), :], exponent.astype(LOW), NN)
        mixed.append(part * (1.0 / totals))
        lse_ref[0, pl.ds(h, 1), :] = highest + jnp.log(totals)
    o_ref[...] = jnp.concatenate(mixed, axis=0).T.astype(LOW)


def attention_forward(counts, qkv, block):
    rows, width = qkv.shape
    pairs = width // 384
    return pl.pallas_call(
        functools.partial(forward_kernel, rows=rows, block=block),
        grid_spec=pltpu.PrefetchScalarGridSpec(
            num_scalar_prefetch=1,
            grid=(pairs, rows // block),
            in_specs=[
                pl.BlockSpec((block, 128), lambda h, i, n: (i, 3 * h)),
                pl.BlockSpec((rows, 128), lambda h, i, n: (0, 3 * h + 1)),
                pl.BlockSpec((rows, 128), lambda h, i, n: (0, 3 * h + 2)),
            ],
            out_specs=[
                pl.BlockSpec((block, 128), lambda h, i, n: (i, h)),
                pl.BlockSpec((1, 2, block), lambda h, i, n: (h, 0, i)),
            ],
            scratch_shapes=[pltpu.VMEM((2, rows, 128), LOW), pltpu.VMEM((128, rows), LOW)],
        ),
        out_shape=[
            jax.ShapeDtypeStruct((rows, pairs * 128), LOW),
            jax.ShapeDtypeStruct((pairs, 2, rows), FULL),
        ],
        cost_estimate=pl.CostEstimate(flops=1, bytes_accessed=1, transcendentals=0),
        name="attention_forward",
    )(counts, qkv, qkv, qkv)


def backward_kernel(
    counts_ref, q_ref, k_ref, v_ref, o_ref, g_ref, lse_ref, grad_ref,
    ka, va, kt, dk, dv, *, rows, block, steps, chunk,
):
    step = pl.program_id(0)

    @pl.when(step == 0)
    def _():
        keys_with_mask(k_ref, counts_ref, ka, rows)
        lane = lax.broadcasted_iota(jnp.int32, (rows, 128), 1)
        v = v_ref[...].astype(FULL)
        va[0] = jnp.where(lane < 64, v, 0.0).astype(LOW)
        va[1] = jnp.where(lane >= 64, v, 0.0).astype(LOW)
        kt[...] = k_ref[...].T
        dk[...] = jnp.zeros_like(dk)
        dv[...] = jnp.zeros_like(dv)

    lane = lax.broadcasted_iota(jnp.int32, (block, 128), 1)
    q = q_ref[...].astype(FULL)
    g = g_ref[...]
    wide = g.astype(FULL)
    product = (wide * o_ref[...].astype(FULL)).T
    scaled = q * SCALE
    columns = []
    for h in range(2):
        mine = (lane < 64) if h == 0 else (lane >= 64)
        flag = lane == (64 if h == 0 else 0)
        qa = jnp.where(mine, scaled, jnp.where(flag, 1.0, 0.0)).astype(LOW)
        qm = jnp.where(mine, q, 0.0).astype(LOW)
        gm = jnp.where(mine, wide, 0.0).astype(LOW)
        delta = jnp.sum(product[64 * h : 64 * h + 64], axis=0, keepdims=True)
        lse = lse_ref[0, pl.ds(h, 1), :]
        total = jnp.zeros((64, block), FULL)
        for c in range(rows // chunk):
            part = pl.ds(c * chunk, chunk)
            probs = jnp.exp(dot(ka[h, part, :], qa, NT) - lse)
            grad_probs = dot(va[h, part, :], g, NT)
            grad_scores = (probs * (grad_probs - delta)).astype(LOW)
            dv[part, :] += dot(probs.astype(LOW), gm, NN)
            dk[part, :] += dot(grad_scores, qm, NN)
            total = total + dot(kt[pl.ds(64 * h, 64), part], grad_scores, NN)
        columns.append(total)
    spot = pl.ds(pl.multiple_of(step * block, block), block)
    grad_ref[spot, 0:128] = (jnp.concatenate(columns, axis=0).T * SCALE).astype(LOW)

    @pl.when(step == steps - 1)
    def _():
        grad_ref[:, 128:256] = (dk[...] * SCALE).astype(LOW)
        grad_ref[:, 256:384] = dv[...].astype(LOW)


def attention_backward(counts, qkv, mixed, grad, lse, pair, block, chunk):
    rows = qkv.shape[0]
    steps = rows // block
    return pl.pallas_call(
        functools.partial(backward_kernel, rows=rows, block=block, steps=steps, chunk=chunk),
        grid_spec=pltpu.PrefetchScalarGridSpec(
            num_scalar_prefetch=1,
            grid=(steps,),
            in_specs=[
                pl.BlockSpec((block, 128), lambda i, n: (i, 3 * pair)),
                pl.BlockSpec((rows, 128), lambda i, n: (0, 3 * pair + 1)),
                pl.BlockSpec((rows, 128), lambda i, n: (0, 3 * pair + 2)),
                pl.BlockSpec((block, 128), lambda i, n: (i, pair)),
                pl.BlockSpec((block, 128), lambda i, n: (i, pair)),
                pl.BlockSpec((1, 2, block), lambda i, n: (pair, 0, i)),
            ],
            out_specs=pl.BlockSpec((rows, 384), lambda i, n: (0, 0)),
            scratch_shapes=[
                pltpu.VMEM((2, rows, 128), LOW),
                pltpu.VMEM((2, rows, 128), LOW),
                pltpu.VMEM((128, rows), LOW),
                pltpu.VMEM((rows, 128), FULL),
                pltpu.VMEM((rows, 128), FULL),
            ],
        ),
        out_shape=jax.ShapeDtypeStruct((rows, 384), LOW),
        cost_estimate=pl.CostEstimate(flops=1, bytes_accessed=1, transcendentals=0),
        name="attention_backward",
    )(counts, qkv, qkv, qkv, mixed, grad, lse)


def norm_parts(values):
    center = values - jnp.mean(values, axis=-1, keepdims=True)
    inverse = lax.rsqrt(jnp.mean(center * center, axis=-1, keepdims=True) + EPSILON)
    return center * inverse, inverse


def norm_backward(upstream, unit, inverse, gain):
    scaled = upstream * gain
    first = jnp.mean(scaled, axis=-1, keepdims=True)
    second = jnp.mean(scaled * unit, axis=-1, keepdims=True)
    result = inverse * (scaled - first - unit * second)
    return result, jnp.sum(upstream * unit, axis=0), jnp.sum(upstream, axis=0)


def gelu_parts(values):
    share = 0.5 * (1.0 + lax.erf(values * (1.0 / math.sqrt(2.0))))
    density = jnp.exp(-0.5 * values * values) * (1.0 / math.sqrt(2.0 * math.pi))
    return values * share, share + values * density


def shards(
    tokens, teacher, teach_mask, lengths, deal_group,
    ln1_gain, ln1_bias, qkv_weight, out_weight, ln2_gain, ln2_bias, up_weight, down_weight,
):
    pairs, cores, depth = (lax.axis_size(name) for name in AXES)
    p, c, z = (lax.axis_index(name) for name in AXES)
    groups = pairs * cores
    slot_rows, width = tokens.shape[1], tokens.shape[2]
    rows = 2 * slot_rows
    full_len = depth * slot_rows
    seq_count = lengths.shape[0]
    ff = up_weight.shape[1]
    own_rows = width // groups
    pair_rows = cores * own_rows
    half_width = width // 2
    half_ff = ff // 2
    is_first = c == 0

    def in_order(mine, other, axis):
        return jnp.concatenate(
            [jnp.where(is_first, mine, other), jnp.where(is_first, other, mine)], axis=axis
        )

    sequence = 2 * cores * p + z
    length = jnp.sum(jnp.where(jnp.arange(seq_count) == sequence, lengths, 0))
    base = c * rows
    counts = jnp.stack([length - base, length - (rows - base)])
    counts = jnp.clip(counts, 0, rows).astype(jnp.int32)

    heads_half = HEADS // 2
    head_pairs = heads_half // 2
    wide_half = 3 * half_width
    shard = qkv_weight.reshape(own_rows, 2, head_pairs, 2, 3, HEAD_DIM)
    shard = jnp.transpose(shard, (1, 0, 2, 4, 3, 5)).reshape(2, own_rows, wide_half)
    vectors = jnp.stack([ln1_gain, ln1_bias, ln2_gain, ln2_bias], axis=1)
    vectors = jnp.pad(vectors, ((0, 0), (0, 124)))
    vectors = jnp.broadcast_to(vectors[None], (2, own_rows, 128))
    shard = jnp.concatenate([shard, vectors], axis=2)
    keep = lax.dynamic_index_in_dim(shard, c, 0, keepdims=False)
    send = lax.dynamic_index_in_dim(shard, 1 - c, 0, keepdims=False)
    qkv_shard = in_order(keep, across_cores(send), 0)
    down_sources, *down_args = gathered_over_pairs(down_weight)
    qkv_pieces = gathered_over_pairs(qkv_shard)

    x_rows = turned(tokens).reshape(rows, width)

    masks = deal_group[0:2]
    group = p * cores + c
    sources = jnp.bitwise_xor(group, masks) * 2 + jnp.arange(2, dtype=jnp.int32)
    picked = jnp.arange(seq_count, dtype=jnp.int32)[None, :] == sources[:, None]
    dealt_len = jnp.sum(jnp.where(picked, lengths[None, :], 0), axis=1)
    positions = z * slot_rows + jnp.arange(slot_rows, dtype=jnp.int32)
    live = (positions[None, :] < dealt_len[:, None]) & (teach_mask == 1)
    tally = jnp.full((8, 128), jnp.sum(live.astype(FULL)))
    tally = tally + across_cores(tally)

    mask_rows = jnp.pad(
        teach_mask.astype(LOW)[:, None, :], ((0, 0), (0, 15), (0, width - slot_rows))
    )
    slots = jnp.concatenate([teacher, mask_rows], axis=1)

    def dealt(slots, level):
        flagged = jnp.bitwise_and(jnp.right_shift(masks[0], level), 1) == 1
        outgoing = jnp.where(flagged, slots[0], slots[1])
        incoming = across_cores(outgoing) if level == 0 else across_pairs(outgoing, 1 << (level - 1))
        return [flagged, slots, incoming]

    def settled(flagged, slots, incoming):
        return jnp.stack(
            [jnp.where(flagged, incoming, slots[0]), jnp.where(flagged, slots[1], incoming)]
        )

    levels = groups.bit_length() - 1
    deal = dealt(slots, 0)

    block = ff // groups

    def unit_blocks(part):
        return jnp.concatenate(
            [up_weight[:, (2 * q + part) * block : (2 * q + part + 1) * block] for q in range(pairs)],
            axis=1,
        )

    up_parts = [unit_blocks(0), unit_blocks(1)]
    keep = jnp.where(is_first, up_parts[0], up_parts[1])
    send = jnp.where(is_first, up_parts[1], up_parts[0])
    got = across_cores(jnp.concatenate([send[:, :width], send[:, width:], out_weight], axis=0))
    up_shard = in_order(keep, jnp.concatenate([got[:own_rows], got[own_rows : 2 * own_rows]], axis=1), 0)
    out_shard = in_order(out_weight, got[2 * own_rows :], 0)
    payload = jnp.concatenate([up_shard[:, :width], up_shard[:, width:], out_shard], axis=0)
    payload_plan = (
        (0, 0, pair_rows, 0, width, 0),
        (0, pair_rows, pair_rows, 0, width, width),
        (1, 2 * pair_rows, pair_rows, 0, width, 0),
    )
    depth_steps, plane_steps = sum_steps()
    x_rows, payload, tally, down_sources = tied(x_rows, payload, tally, down_sources)
    payload_first = halves_first(payload)
    for step in depth_steps:
        tally = tally + step(tally)

    x_full = x_rows.astype(FULL)
    unit_one, inverse_one = norm_parts(x_full)
    w_qkv, vectors = placed(
        qkv_pieces,
        ((0, 0, pair_rows, 0, wide_half, 0), (1, 0, pair_rows, wide_half, 128, 0)),
    )
    pick = lax.broadcasted_iota(jnp.int32, (8, 128), 0) == lax.broadcasted_iota(jnp.int32, (8, 128), 1)
    vectors = dot(pick.astype(LOW), vectors, NT)
    gain_one, shift_one, gain_two, shift_two = vectors[0], vectors[1], vectors[2], vectors[3]
    norm_mine = (unit_one * gain_one + shift_one).astype(LOW)
    norm_one = jnp.concatenate([norm_mine, across_cores(norm_mine)], axis=0)
    norm_one, tally, deal = tied(norm_one, tally, deal)
    deal = dealt(settled(*deal), 1)
    tally = tally + plane_steps[1](tally)
    qkv = dot(norm_one, w_qkv, NN).astype(LOW)
    qkv, deal, tally, payload_first = tied(qkv, deal, tally, payload_first)
    payload_pieces = halves_second(payload_first)
    for level in range(2, levels):
        deal = dealt(settled(*deal), level)
    mixed, lse = attention_forward(counts, qkv, 512)

    sources, *place_args = payload_pieces
    mixed, sources, deal, tally = tied(mixed, sources, deal, tally)
    for step in plane_steps[2:]:
        tally = tally + step(tally)
    mixed_got = across_cores(mixed[rows:])
    goal = turned(settled(*deal))
    w_up, w_out = placed((sources, *place_args), payload_plan)
    (w_down,) = placed(
        (down_sources, *down_args), ((0, 0, down_weight.shape[0], 0, width, 0),)
    )

    attended = in_order(mixed[:rows], mixed_got, 1)
    middle = x_full + dot(attended, w_out, NN)
    unit_two, inverse_two = norm_parts(middle)
    norm_two = (unit_two * gain_two + shift_two).astype(LOW)
    norm_other = across_cores(norm_two)

    def expanded(low):
        value, slope = gelu_parts(dot(low, w_up, NN))
        return value.astype(LOW), slope.astype(LOW)

    active_mine, slope_mine = expanded(norm_two)
    active_other, slope_other = expanded(norm_other)
    part_other = row_major(dot(active_other, w_down, NN).astype(LOW))
    part_mine = row_major(dot(active_mine, w_down, NN))
    output = middle + part_mine + across_cores(part_other).astype(FULL)

    output, goal, tally = tied(output, goal, tally)
    valid_count = tally[0, 0]
    spots = base + jnp.arange(rows, dtype=jnp.int32)
    taught = goal[:, slot_rows, :slot_rows].reshape(rows)
    valid = ((spots < length) & (taught == 1)).astype(FULL)[:, None]
    error = output - goal[:, :slot_rows].reshape(rows, width).astype(FULL)
    squares = jnp.sum(valid * error * error)
    factor = seq_count * full_len * 1.0 / valid_count
    grad_out = valid * (2.0 * factor) * error
    grad_ff = grad_out.astype(LOW)
    grad_ff_other = across_cores(grad_ff)
    output_moved = turned_parts(output.astype(LOW).reshape(2, slot_rows, width))
    hidden_mine = (dot(grad_ff, w_down, NT) * slope_mine.astype(FULL)).astype(LOW)
    down_grad = (dot(active_mine, grad_ff, TN) + dot(active_other, grad_ff_other, TN)).astype(LOW)
    down_grad, grad_ff_other, hidden_mine = tied(down_grad, grad_ff_other, hidden_mine)
    down_sum = scattered_over_pairs(down_grad)
    hidden_other = (dot(grad_ff_other, w_down, NT) * slope_other.astype(FULL)).astype(LOW)
    back_other = dot(hidden_other, w_up, NT).astype(LOW)
    back_got = across_cores(back_other)
    back_mine = dot(hidden_mine, w_up, NT)
    up_grad = (dot(norm_two, hidden_mine, TN) + dot(norm_other, hidden_other, TN)).astype(LOW)
    grad_mid, gain_two_grad, shift_two_grad = norm_backward(
        back_mine + back_got.astype(FULL), unit_two, inverse_two, gain_two
    )
    grad_middle = grad_out + grad_mid
    grad_branch = grad_middle.astype(LOW)
    grad_attended = dot(grad_branch, w_out, NT).astype(LOW)
    keep = jnp.where(is_first, grad_attended[:, :half_width], grad_attended[:, half_width:])
    send = jnp.where(is_first, grad_attended[:, half_width:], grad_attended[:, :half_width])
    mixed_grad_got = across_cores(send)
    out_grad = dot(attended, grad_branch, TN).astype(LOW)
    rest_sum = scattered_over_pairs(jnp.concatenate([up_grad, out_grad], axis=1))
    grad_mixed = jnp.concatenate([keep, mixed_grad_got], axis=0)

    def attend(pair, gate):
        return attention_backward(gate, qkv, mixed, grad_mixed, lse, pair, 512, 512)

    def weight_part(grads):
        return dot(norm_one, grads, TN).astype(LOW)

    low_bit, high_bit = 1, depth // 2
    first = attend(0, counts)
    first, down_sum, output_moved, gate = tied(first, down_sum, output_moved, counts)
    activations = turned_settled(output_moved)
    down_step = depth_halved(added(down_sum), low_bit)
    second = attend(1, gate)
    second, first, down_step, rest_sum, gate = tied(second, first, down_step, rest_sum, counts)
    down_step = depth_halved(added(down_step), high_bit)
    rest_step = depth_halved(added(rest_sum), low_bit)
    early = scattered_over_pairs(weight_part(jnp.concatenate([first, second], axis=1)))
    third = attend(2, gate)
    third, first, second, down_step, rest_step, early = tied(
        third, first, second, down_step, rest_step, early
    )

    partial = row_major(dot(jnp.concatenate([first, second, third], axis=1), w_qkv, NT))
    back_got = across_cores(partial[rows:].astype(LOW))
    early = depth_halved(added(early), low_bit)
    rest_step = depth_halved(added(rest_step), high_bit)
    down_own = added(down_step)
    down_got = across_depth(down_own, high_bit)
    late = scattered_over_pairs(weight_part(third))
    grad_norm_one = partial[:rows] + back_got.astype(FULL)
    grad_in, gain_one_grad, shift_one_grad = norm_backward(
        grad_norm_one, unit_one, inverse_one, gain_one
    )
    grad_rows = row_major((grad_middle + grad_in).astype(LOW))
    input_moved = turned_parts(grad_rows.reshape(2, slot_rows, width))

    row_index = lax.broadcasted_iota(jnp.int32, (8, width), 0)
    small = jnp.zeros((8, width), FULL)
    for index, value in enumerate(
        [gain_one_grad, shift_one_grad, gain_two_grad, shift_two_grad, jnp.full((width,), squares)]
    ):
        small = jnp.where(row_index == index, value[None, :], small)
    small = small + plane_steps[0](small)

    late = depth_halved(added(late), low_bit)
    rest_own = added(rest_step)
    rest_got = across_depth(rest_own, high_bit)
    late, early, rest_got, small, down_got, near = tied(
        late, early, rest_got, small, down_got, input_moved[0]
    )
    down_own = depth_doubled(down_own, down_got, high_bit)
    down_got = across_depth(down_own, low_bit)
    qkv_step = depth_halved(jnp.concatenate([added(early), added(late)], axis=1), high_bit)
    rest_own = depth_doubled(rest_own, rest_got, high_bit)
    rest_got = across_depth(rest_own, low_bit)
    small = small + plane_steps[1](small)
    qkv_step, small, down_got, far = tied(qkv_step, small, down_got, input_moved[1])
    input_grad = turned_settled([near, far])
    down_own = depth_doubled(down_own, down_got, low_bit)
    qkv_own = added(qkv_step)
    qkv_got = across_depth(qkv_own, high_bit)
    for step in plane_steps[2:]:
        small = small + step(small)
    qkv_got, rest_got, small = tied(qkv_got, rest_got, small)
    qkv_own = depth_doubled(qkv_own, qkv_got, high_bit)
    qkv_got = across_depth(qkv_own, low_bit)
    rest_own = depth_doubled(rest_own, rest_got, low_bit)
    small = small + depth_steps[0](small)

    def own_block(stack, index):
        return lax.dynamic_slice_in_dim(stack, index * own_rows, own_rows, 0)

    rest_mine = own_block(rest_own, c)
    rest_other = across_cores(own_block(rest_own, 1 - c))
    qkv_got, rest_other, small = tied(qkv_got, rest_other, small)
    qkv_own = depth_doubled(qkv_own, qkv_got, low_bit)
    qkv_mine = own_block(qkv_own, c)
    qkv_other = across_cores(own_block(qkv_own, 1 - c))
    for step in depth_steps[1:]:
        small = small + step(small)

    loss = small[4, 0] / (valid_count * width)
    own_small = lax.dynamic_slice_in_dim(small, group * own_rows, own_rows, 1)
    out_own = rest_mine[:, half_ff:].astype(FULL) + rest_other[:, half_ff:].astype(FULL)
    sides = [jnp.where(is_first, rest_mine, rest_other), jnp.where(is_first, rest_other, rest_mine)]
    up_own = jnp.concatenate(
        [side[:, q * block : (q + 1) * block] for q in range(pairs) for side in sides], axis=1
    )
    qkv_own = jnp.stack(
        [jnp.where(is_first, qkv_mine, qkv_other), jnp.where(is_first, qkv_other, qkv_mine)]
    )
    qkv_own = qkv_own.reshape(2, own_rows, head_pairs, 3, 2, HEAD_DIM)
    qkv_own = jnp.transpose(qkv_own, (1, 0, 2, 4, 3, 5)).reshape(own_rows, 3 * width)
    return (
        activations, loss, input_grad, own_small[0], own_small[1], qkv_own.astype(FULL),
        out_own, own_small[2], own_small[3], up_own.astype(FULL), down_own.astype(FULL),
    )


def solution(mesh):
    groups, depth = mesh.shape["dp"], mesh.shape["seq"]
    split = Mesh(mesh.devices.reshape(groups // 2, 2, depth), AXES)
    dp = ("pair", "core")
    rows3 = P(dp, "seq", None)
    in_specs = (
        rows3, rows3, P(dp, "seq"), P(), P(), P(dp), P(dp), P(dp, None), P(dp, None),
        P(dp), P(dp), P(dp, None), P(dp, None),
    )
    out_specs = (
        rows3, P(), rows3, P(dp), P(dp), P(dp, None), P(dp, None), P(dp), P(dp),
        P(dp, None), P(dp, None),
    )
    return jax.shard_map(shards, mesh=split, in_specs=in_specs, out_specs=out_specs, check_vma=False)
```

```python
import functools
import math

import jax
import jax.numpy as jnp
from jax import lax
from jax.experimental import pallas as pl
from jax.experimental.layout import Layout, with_layout_constraint
from jax.experimental.pallas import tpu as pltpu
from jax.sharding import Mesh
from jax.sharding import PartitionSpec as P

HEADS = 12
HEAD_DIM = 64
EPSILON = 1e-12
NEGATIVE = -1e30
SCALE = 1.0 / math.sqrt(HEAD_DIM)
AXES = ("pair", "core", "seq")
NT = (((1,), (1,)), ((), ()))
NN = (((1,), (0,)), ((), ()))
TN = (((0,), (0,)), ((), ()))
LOW = jnp.bfloat16
FULL = jnp.float32


def dot(left, right, form):
    return lax.dot_general(left, right, form, preferred_element_type=FULL)


def row_major(value):
    return with_layout_constraint(value, Layout(major_to_minor=tuple(range(value.ndim))))


def moved(value, target):
    pairs, cores, depth = (lax.axis_size(name) for name in AXES)
    links = []
    for p in range(pairs):
        for c in range(cores):
            for z in range(depth):
                q, e, w = target(p, c, z)
                links.append(((p * cores + c) * depth + z, (q * cores + e) * depth + w))
    return lax.ppermute(value, AXES, links)


def across_cores(value):
    return moved(value, lambda p, c, z: (p, 1 - c, z))


def across_pairs(value, bit):
    return moved(value, lambda p, c, z: (p ^ bit, c, z))


def across_depth(value, bit):
    return moved(value, lambda p, c, z: (p, c, z ^ bit))


def pair_bits():
    return [1 << level for level in range(lax.axis_size("pair").bit_length() - 1)]


def turned_parts(stack):
    z = lax.axis_index("seq")
    got = []
    for step in range(2):
        piece = lax.dynamic_index_in_dim(stack, (z + step) % 2, 0, keepdims=False)
        got.append(moved(piece, lambda p, c, w: (p, w // 2, 2 * c + (w + step) % 2)))
    return got


def turned_settled(got):
    even = lax.axis_index("seq") % 2 == 0
    return jnp.stack([jnp.where(even, got[0], got[1]), jnp.where(even, got[1], got[0])])


def turned(stack):
    return turned_settled(turned_parts(stack))


def sum_steps():
    depth_steps = [
        functools.partial(across_depth, bit=1 << level)
        for level in range(lax.axis_size("seq").bit_length() - 1)
    ]
    pair_steps = [functools.partial(across_pairs, bit=bit) for bit in pair_bits()]
    return depth_steps, [across_cores] + pair_steps


def gathered_over_pairs(value):
    p = lax.axis_index("pair")
    if lax.axis_size("pair") <= 4:
        count = lax.axis_size("pair")
        layout = tuple((k, k, 0, 0, value.shape[0]) for k in range(count))
        return [value] + [across_pairs(value, k) for k in range(1, count)], p, layout
    rows, width = value.shape
    bits = pair_bits()
    count = 1 << len(bits)
    halves = []
    for which in range(2):
        order = bits if which == 0 else bits[::-1]
        current = value[which * rows // 2 : (which + 1) * rows // 2]
        for bit in order:
            other = across_pairs(current, bit)
            flag = jnp.bitwise_and(p, bit) != 0
            current = jnp.stack(
                [jnp.where(flag, other, current), jnp.where(flag, current, other)]
            )
        if which == 1:
            lead = tuple(range(len(bits)))[::-1]
            current = jnp.transpose(current, lead + (len(bits), len(bits) + 1))
        halves.append(current.reshape(count, rows // 2, width))
    return [jnp.concatenate(halves, axis=1).reshape(count * rows, width)], None, ()


def halves_first(value):
    if lax.axis_size("pair") != 4:
        return value, None
    rows = value.shape[0] // 2
    return value, (across_pairs(value[:rows], 1), across_pairs(value[rows:], 2))


def halves_second(state):
    value, near = state
    if near is None:
        return gathered_over_pairs(value)
    rows = value.shape[0] // 2
    upper = across_pairs(jnp.concatenate([value[:rows], near[0]], axis=0), 2)
    lower = across_pairs(jnp.concatenate([value[rows:], near[1]], axis=0), 1)
    layout = (
        (0, 0, 0, 0, 2 * rows),
        (1, 1, 0, 0, rows), (1, 4, 0, rows, rows),
        (2, 3, 0, 0, rows), (2, 2, 0, rows, rows),
        (3, 3, rows, 0, rows), (3, 4, rows, rows, rows),
    )
    return [value, near[0], near[1], upper, lower], lax.axis_index("pair"), layout


def place_kernel(p_ref, *refs, segments, layout, count):
    sources, results = refs[:count], refs[count:]
    for k, source, origin, first, size in layout:
        spot = jnp.bitwise_xor(p_ref[0], k)
        for index, row, rows, column, width, target in segments:
            low, high = max(row, first), min(row + rows, first + size)
            if low < high:
                start = pl.multiple_of(spot * rows + (low - row), 16)
                results[index][pl.ds(start, high - low), target : target + width] = sources[source][
                    low - first + origin : high - first + origin, column : column + width
                ]


def placed(gathered, segments):
    pieces, p, layout = gathered
    pairs = lax.axis_size("pair")
    outs = 1 + max(segment[0] for segment in segments)
    if p is None:
        stack = pieces[0].reshape(pairs, -1, pieces[0].shape[1])
        results = []
        for index in range(outs):
            parts = [
                stack[:, row : row + rows, column : column + width].reshape(pairs * rows, width)
                for which, row, rows, column, width, _ in segments
                if which == index
            ]
            results.append(jnp.concatenate(parts, axis=1))
        return results
    shapes = []
    for index in range(outs):
        mine = [segment for segment in segments if segment[0] == index]
        shapes.append(
            jax.ShapeDtypeStruct((pairs * mine[0][2], sum(part[4] for part in mine)), LOW)
        )
    local = pl.BlockSpec(memory_space=pltpu.VMEM)
    return pl.pallas_call(
        functools.partial(place_kernel, segments=segments, layout=layout, count=len(pieces)),
        in_specs=[pl.BlockSpec(memory_space=pltpu.SMEM)] + [local] * len(pieces),
        out_specs=[local] * outs,
        out_shape=shapes,
        name="place",
    )(p.astype(jnp.int32).reshape(1), *pieces)


def scattered_over_pairs(value):
    p = lax.axis_index("pair")
    if lax.axis_size("pair") <= 4:
        rows = value.shape[0] // lax.axis_size("pair")
        pieces = []
        for k in range(lax.axis_size("pair")):
            piece = lax.dynamic_slice_in_dim(value, jnp.bitwise_xor(p, k) * rows, rows, 0)
            pieces.append(across_pairs(piece, k) if k else piece)
        return pieces
    bits = pair_bits()
    count = 1 << len(bits)
    rows, width = value.shape[0] // count, value.shape[1]
    blocks = value.reshape(count, rows, width)
    halves = []
    for which in range(2):
        order = bits if which == 0 else bits[::-1]
        current = blocks[:, which * rows // 2 : (which + 1) * rows // 2]
        current = current.reshape((2,) * len(bits) + (rows // 2, width))
        left = bits[::-1]
        for bit in order:
            axis = left.index(bit)
            mine = jnp.where(jnp.bitwise_and(p, bit) != 0, 1, 0)
            keep = lax.dynamic_index_in_dim(current, mine, axis, keepdims=False)
            send = lax.dynamic_index_in_dim(current, 1 - mine, axis, keepdims=False)
            current = keep + across_pairs(send, bit)
            left = [other for other in left if other != bit]
        halves.append(current)
    return [jnp.concatenate(halves, axis=0)]


def added(pieces):
    total = pieces[0].astype(FULL)
    for piece in pieces[1:]:
        total = total + piece.astype(FULL)
    return total.astype(LOW)


def depth_flag(bit):
    return jnp.where(jnp.bitwise_and(lax.axis_index("seq"), bit) != 0, 1, 0)


def depth_halved(value, bit):
    mine = depth_flag(bit)
    parts = value.reshape((2, value.shape[0] // 2) + value.shape[1:])
    keep = lax.dynamic_index_in_dim(parts, mine, 0, keepdims=False)
    send = lax.dynamic_index_in_dim(parts, 1 - mine, 0, keepdims=False)
    return [keep, across_depth(send, bit)]


def depth_doubled(value, other, bit):
    mine = depth_flag(bit)
    return jnp.concatenate(
        [jnp.where(mine == 0, value, other), jnp.where(mine == 0, other, value)], axis=0
    )


def tied(*values):
    return lax.optimization_barrier(values)


def keys_with_mask(k_ref, counts_ref, ka, rows):
    lane = lax.broadcasted_iota(jnp.int32, (rows, 128), 1)
    spot = lax.broadcasted_iota(jnp.int32, (rows, 128), 0)
    limit = jnp.where(spot < rows // 2, counts_ref[0], counts_ref[1] + rows // 2)
    bias = jnp.where(spot < limit, 0.0, NEGATIVE)
    k = k_ref[...].astype(FULL)
    ka[0] = jnp.where(lane < 64, k, jnp.where(lane == 64, bias, 0.0)).astype(LOW)
    ka[1] = jnp.where(lane >= 64, k, jnp.where(lane == 0, bias, 0.0)).astype(LOW)


def forward_kernel(counts_ref, q_ref, k_ref, v_ref, o_ref, lse_ref, ka, vt, *, rows, block):
    @pl.when(pl.program_id(1) == 0)
    def _():
        keys_with_mask(k_ref, counts_ref, ka, rows)
        vt[...] = v_ref[...].T

    lane = lax.broadcasted_iota(jnp.int32, (block, 128), 1)
    q = q_ref[...].astype(FULL) * SCALE
    mixed = []
    for h in range(2):
        mine = (lane < 64) if h == 0 else (lane >= 64)
        flag = lane == (64 if h == 0 else 0)
        qa = jnp.where(mine, q, jnp.where(flag, 1.0, 0.0)).astype(LOW)
        scores = dot(ka[h], qa, NT)
        highest = jnp.max(scores, axis=0, keepdims=True)
        exponent = jnp.exp(scores - highest)
        totals = jnp.sum(exponent, axis=0, keepdims=True)
        part = dot(vt[pl.ds(64 * h, 64), :], exponent.astype(LOW), NN)
        mixed.append(part * (1.0 / totals))
        lse_ref[0, pl.ds(h, 1), :] = highest + jnp.log(totals)
    o_ref[...] = jnp.concatenate(mixed, axis=0).T.astype(LOW)


def attention_forward(counts, qkv, block):
    rows, width = qkv.shape
    pairs = width // 384
    return pl.pallas_call(
        functools.partial(forward_kernel, rows=rows, block=block),
        grid_spec=pltpu.PrefetchScalarGridSpec(
            num_scalar_prefetch=1,
            grid=(pairs, rows // block),
            in_specs=[
                pl.BlockSpec((block, 128), lambda h, i, n: (i, 3 * h)),
                pl.BlockSpec((rows, 128), lambda h, i, n: (0, 3 * h + 1)),
                pl.BlockSpec((rows, 128), lambda h, i, n: (0, 3 * h + 2)),
            ],
            out_specs=[
                pl.BlockSpec((block, 128), lambda h, i, n: (i, h)),
                pl.BlockSpec((1, 2, block), lambda h, i, n: (h, 0, i)),
            ],
            scratch_shapes=[pltpu.VMEM((2, rows, 128), LOW), pltpu.VMEM((128, rows), LOW)],
        ),
        out_shape=[
            jax.ShapeDtypeStruct((rows, pairs * 128), LOW),
            jax.ShapeDtypeStruct((pairs, 2, rows), FULL),
        ],
        cost_estimate=pl.CostEstimate(flops=1, bytes_accessed=1, transcendentals=0),
        name="attention_forward",
    )(counts, qkv, qkv, qkv)


def backward_kernel(
    counts_ref, q_ref, k_ref, v_ref, o_ref, g_ref, lse_ref, grad_ref,
    ka, va, kt, dk, dv, *, rows, block, steps, chunk,
):
    step = pl.program_id(0)

    @pl.when(step == 0)
    def _():
        keys_with_mask(k_ref, counts_ref, ka, rows)
        lane = lax.broadcasted_iota(jnp.int32, (rows, 128), 1)
        v = v_ref[...].astype(FULL)
        va[0] = jnp.where(lane < 64, v, 0.0).astype(LOW)
        va[1] = jnp.where(lane >= 64, v, 0.0).astype(LOW)
        kt[...] = k_ref[...].T
        dk[...] = jnp.zeros_like(dk)
        dv[...] = jnp.zeros_like(dv)

    lane = lax.broadcasted_iota(jnp.int32, (block, 128), 1)
    q = q_ref[...].astype(FULL)
    g = g_ref[...]
    wide = g.astype(FULL)
    product = (wide * o_ref[...].astype(FULL)).T
    scaled = q * SCALE
    columns = []
    for h in range(2):
        mine = (lane < 64) if h == 0 else (lane >= 64)
        flag = lane == (64 if h == 0 else 0)
        qa = jnp.where(mine, scaled, jnp.where(flag, 1.0, 0.0)).astype(LOW)
        qm = jnp.where(mine, q, 0.0).astype(LOW)
        gm = jnp.where(mine, wide, 0.0).astype(LOW)
        delta = jnp.sum(product[64 * h : 64 * h + 64], axis=0, keepdims=True)
        lse = lse_ref[0, pl.ds(h, 1), :]
        total = jnp.zeros((64, block), FULL)
        for c in range(rows // chunk):
            part = pl.ds(c * chunk, chunk)
            probs = jnp.exp(dot(ka[h, part, :], qa, NT) - lse)
            grad_probs = dot(va[h, part, :], g, NT)
            grad_scores = (probs * (grad_probs - delta)).astype(LOW)
            dv[part, :] += dot(probs.astype(LOW), gm, NN)
            dk[part, :] += dot(grad_scores, qm, NN)
            total = total + dot(kt[pl.ds(64 * h, 64), part], grad_scores, NN)
        columns.append(total)
    spot = pl.ds(pl.multiple_of(step * block, block), block)
    grad_ref[spot, 0:128] = (jnp.concatenate(columns, axis=0).T * SCALE).astype(LOW)

    @pl.when(step == steps - 1)
    def _():
        grad_ref[:, 128:256] = (dk[...] * SCALE).astype(LOW)
        grad_ref[:, 256:384] = dv[...].astype(LOW)


def attention_backward(counts, qkv, mixed, grad, lse, pair, block, chunk):
    rows = qkv.shape[0]
    steps = rows // block
    return pl.pallas_call(
        functools.partial(backward_kernel, rows=rows, block=block, steps=steps, chunk=chunk),
        grid_spec=pltpu.PrefetchScalarGridSpec(
            num_scalar_prefetch=1,
            grid=(steps,),
            in_specs=[
                pl.BlockSpec((block, 128), lambda i, n: (i, 3 * pair)),
                pl.BlockSpec((rows, 128), lambda i, n: (0, 3 * pair + 1)),
                pl.BlockSpec((rows, 128), lambda i, n: (0, 3 * pair + 2)),
                pl.BlockSpec((block, 128), lambda i, n: (i, pair)),
                pl.BlockSpec((block, 128), lambda i, n: (i, pair)),
                pl.BlockSpec((1, 2, block), lambda i, n: (pair, 0, i)),
            ],
            out_specs=pl.BlockSpec((rows, 384), lambda i, n: (0, 0)),
            scratch_shapes=[
                pltpu.VMEM((2, rows, 128), LOW),
                pltpu.VMEM((2, rows, 128), LOW),
                pltpu.VMEM((128, rows), LOW),
                pltpu.VMEM((rows, 128), FULL),
                pltpu.VMEM((rows, 128), FULL),
            ],
        ),
        out_shape=jax.ShapeDtypeStruct((rows, 384), LOW),
        cost_estimate=pl.CostEstimate(flops=1, bytes_accessed=1, transcendentals=0),
        name="attention_backward",
    )(counts, qkv, qkv, qkv, mixed, grad, lse)


def norm_parts(values):
    center = values - jnp.mean(values, axis=-1, keepdims=True)
    inverse = lax.rsqrt(jnp.mean(center * center, axis=-1, keepdims=True) + EPSILON)
    return center * inverse, inverse


def norm_backward(upstream, unit, inverse, gain):
    scaled = upstream * gain
    first = jnp.mean(scaled, axis=-1, keepdims=True)
    second = jnp.mean(scaled * unit, axis=-1, keepdims=True)
    result = inverse * (scaled - first - unit * second)
    return result, jnp.sum(upstream * unit, axis=0), jnp.sum(upstream, axis=0)


def gelu_parts(values):
    share = 0.5 * (1.0 + lax.erf(values * (1.0 / math.sqrt(2.0))))
    density = jnp.exp(-0.5 * values * values) * (1.0 / math.sqrt(2.0 * math.pi))
    return values * share, share + values * density


def shards(
    tokens, teacher, teach_mask, lengths, deal_group,
    ln1_gain, ln1_bias, qkv_weight, out_weight, ln2_gain, ln2_bias, up_weight, down_weight,
):
    pairs, cores, depth = (lax.axis_size(name) for name in AXES)
    p, c, z = (lax.axis_index(name) for name in AXES)
    groups = pairs * cores
    slot_rows, width = tokens.shape[1], tokens.shape[2]
    rows = 2 * slot_rows
    full_len = depth * slot_rows
    seq_count = lengths.shape[0]
    ff = up_weight.shape[1]
    own_rows = width // groups
    pair_rows = cores * own_rows
    half_width = width // 2
    half_ff = ff // 2
    is_first = c == 0

    def in_order(mine, other, axis):
        return jnp.concatenate(
            [jnp.where(is_first, mine, other), jnp.where(is_first, other, mine)], axis=axis
        )

    sequence = 2 * cores * p + z
    length = jnp.sum(jnp.where(jnp.arange(seq_count) == sequence, lengths, 0))
    base = c * rows
    counts = jnp.stack([length - base, length - (rows - base)])
    counts = jnp.clip(counts, 0, rows).astype(jnp.int32)

    heads_half = HEADS // 2
    head_pairs = heads_half // 2
    wide_half = 3 * half_width
    shard = qkv_weight.reshape(own_rows, 2, head_pairs, 2, 3, HEAD_DIM)
    shard = jnp.transpose(shard, (1, 0, 2, 4, 3, 5)).reshape(2, own_rows, wide_half)
    vectors = jnp.stack([ln1_gain, ln1_bias, ln2_gain, ln2_bias], axis=1)
    vectors = jnp.pad(vectors, ((0, 0), (0, 124)))
    vectors = jnp.broadcast_to(vectors[None], (2, own_rows, 128))
    shard = jnp.concatenate([shard, vectors], axis=2)
    keep = lax.dynamic_index_in_dim(shard, c, 0, keepdims=False)
    send = lax.dynamic_index_in_dim(shard, 1 - c, 0, keepdims=False)
    qkv_shard = in_order(keep, across_cores(send), 0)
    qkv_pieces = gathered_over_pairs(qkv_shard)

    x_rows = turned(tokens).reshape(rows, width)

    masks = deal_group[0:2]
    group = p * cores + c
    sources = jnp.bitwise_xor(group, masks) * 2 + jnp.arange(2, dtype=jnp.int32)
    picked = jnp.arange(seq_count, dtype=jnp.int32)[None, :] == sources[:, None]
    dealt_len = jnp.sum(jnp.where(picked, lengths[None, :], 0), axis=1)
    positions = z * slot_rows + jnp.arange(slot_rows, dtype=jnp.int32)
    live = (positions[None, :] < dealt_len[:, None]) & (teach_mask == 1)
    tally = jnp.full((8, 128), jnp.sum(live.astype(FULL)))
    tally = tally + across_cores(tally)

    mask_rows = jnp.pad(
        teach_mask.astype(LOW)[:, None, :], ((0, 0), (0, 15), (0, width - slot_rows))
    )
    slots = jnp.concatenate([teacher, mask_rows], axis=1)

    def dealt(slots, level):
        flagged = jnp.bitwise_and(jnp.right_shift(masks[0], level), 1) == 1
        outgoing = jnp.where(flagged, slots[0], slots[1])
        incoming = across_cores(outgoing) if level == 0 else across_pairs(outgoing, 1 << (level - 1))
        return [flagged, slots, incoming]

    def settled(flagged, slots, incoming):
        return jnp.stack(
            [jnp.where(flagged, incoming, slots[0]), jnp.where(flagged, slots[1], incoming)]
        )

    levels = groups.bit_length() - 1
    deal = dealt(slots, 0)

    block = ff // groups

    def unit_blocks(part):
        return jnp.concatenate(
            [up_weight[:, (2 * q + part) * block : (2 * q + part + 1) * block] for q in range(pairs)],
            axis=1,
        )

    up_parts = [unit_blocks(0), unit_blocks(1)]
    keep = jnp.where(is_first, up_parts[0], up_parts[1])
    send = jnp.where(is_first, up_parts[1], up_parts[0])
    got = across_cores(jnp.concatenate([send[:, :width], send[:, width:], out_weight], axis=0))
    up_shard = in_order(keep, jnp.concatenate([got[:own_rows], got[own_rows : 2 * own_rows]], axis=1), 0)
    out_shard = in_order(out_weight, got[2 * own_rows :], 0)
    payload = jnp.concatenate(
        [down_weight, up_shard[:, :width], up_shard[:, width:], out_shard], axis=0
    )
    down_rows = down_weight.shape[0]
    payload_plan = (
        (0, 0, down_rows, 0, width, 0),
        (1, down_rows, pair_rows, 0, width, 0),
        (1, down_rows + pair_rows, pair_rows, 0, width, width),
        (2, down_rows + 2 * pair_rows, pair_rows, 0, width, 0),
    )
    depth_steps, plane_steps = sum_steps()
    for step in plane_steps[1:]:
        tally = tally + step(tally)
    x_rows, payload, tally = tied(x_rows, payload, tally)
    payload_first = halves_first(payload)

    x_full = x_rows.astype(FULL)
    unit_one, inverse_one = norm_parts(x_full)
    w_qkv, vectors = placed(
        qkv_pieces,
        ((0, 0, pair_rows, 0, wide_half, 0), (1, 0, pair_rows, wide_half, 128, 0)),
    )
    pick = lax.broadcasted_iota(jnp.int32, (8, 128), 0) == lax.broadcasted_iota(jnp.int32, (8, 128), 1)
    vectors = dot(pick.astype(LOW), vectors, NT)
    gain_one, shift_one, gain_two, shift_two = vectors[0], vectors[1], vectors[2], vectors[3]
    norm_mine = (unit_one * gain_one + shift_one).astype(LOW)
    norm_one = jnp.concatenate([norm_mine, across_cores(norm_mine)], axis=0)
    norm_one, tally, deal = tied(norm_one, tally, deal)
    deal = dealt(settled(*deal), 1)
    tally = tally + depth_steps[0](tally)
    qkv = dot(norm_one, w_qkv, NN).astype(LOW)
    qkv, deal, tally, payload_first = tied(qkv, deal, tally, payload_first)
    payload_pieces = halves_second(payload_first)
    for level in range(2, levels):
        deal = dealt(settled(*deal), level)
    for step in depth_steps[1:]:
        tally = tally + step(tally)
    mixed, lse = attention_forward(counts, qkv, 512)

    sources, *place_args = payload_pieces
    mixed, sources, deal, tally = tied(mixed, sources, deal, tally)
    mixed_got = across_cores(mixed[rows:])
    goal_moved = turned_parts(settled(*deal))
    w_down, w_up, w_out = placed((sources, *place_args), payload_plan)

    attended = in_order(mixed[:rows], mixed_got, 1)
    middle = x_full + dot(attended, w_out, NN)
    unit_two, inverse_two = norm_parts(middle)
    norm_two = (unit_two * gain_two + shift_two).astype(LOW)
    norm_other = across_cores(norm_two)

    def expanded(low):
        value, slope = gelu_parts(dot(low, w_up, NN))
        return value.astype(LOW), slope.astype(LOW)

    active_mine, slope_mine = expanded(norm_two)
    active_other, slope_other = expanded(norm_other)
    active_other, slope_other, goal_moved = tied(active_other, slope_other, goal_moved)
    goal = turned_settled(goal_moved)
    part_other = row_major(dot(active_other, w_down, NN).astype(LOW))
    part_mine = row_major(dot(active_mine, w_down, NN))
    output = middle + part_mine + across_cores(part_other).astype(FULL)

    output, goal, tally = tied(output, goal, tally)
    valid_count = tally[0, 0]
    spots = base + jnp.arange(rows, dtype=jnp.int32)
    taught = goal[:, slot_rows, :slot_rows].reshape(rows)
    valid = ((spots < length) & (taught == 1)).astype(FULL)[:, None]
    error = output - goal[:, :slot_rows].reshape(rows, width).astype(FULL)
    squares = jnp.sum(valid * error * error)
    factor = seq_count * full_len * 1.0 / valid_count
    grad_out = valid * (2.0 * factor) * error
    grad_ff = grad_out.astype(LOW)
    grad_ff_other = across_cores(grad_ff)
    output_moved = turned_parts(output.astype(LOW).reshape(2, slot_rows, width))
    hidden_mine = (dot(grad_ff, w_down, NT) * slope_mine.astype(FULL)).astype(LOW)
    down_grad = (dot(active_mine, grad_ff, TN) + dot(active_other, grad_ff_other, TN)).astype(LOW)
    down_grad, grad_ff_other, hidden_mine = tied(down_grad, grad_ff_other, hidden_mine)
    down_sum = scattered_over_pairs(down_grad)
    hidden_other = (dot(grad_ff_other, w_down, NT) * slope_other.astype(FULL)).astype(LOW)
    back_other = dot(hidden_other, w_up, NT).astype(LOW)
    back_got = across_cores(back_other)
    back_mine = dot(hidden_mine, w_up, NT)
    up_grad = (dot(norm_two, hidden_mine, TN) + dot(norm_other, hidden_other, TN)).astype(LOW)
    grad_mid, gain_two_grad, shift_two_grad = norm_backward(
        back_mine + back_got.astype(FULL), unit_two, inverse_two, gain_two
    )
    grad_middle = grad_out + grad_mid
    grad_branch = grad_middle.astype(LOW)
    grad_attended = dot(grad_branch, w_out, NT).astype(LOW)
    keep = jnp.where(is_first, grad_attended[:, :half_width], grad_attended[:, half_width:])
    send = jnp.where(is_first, grad_attended[:, half_width:], grad_attended[:, :half_width])
    mixed_grad_got = across_cores(send)
    out_grad = dot(attended, grad_branch, TN).astype(LOW)
    rest_sum = scattered_over_pairs(jnp.concatenate([up_grad, out_grad], axis=1))
    grad_mixed = jnp.concatenate([keep, mixed_grad_got], axis=0)

    def attend(pair, gate):
        return attention_backward(gate, qkv, mixed, grad_mixed, lse, pair, 512, 512)

    def weight_part(grads):
        return dot(norm_one, grads, TN).astype(LOW)

    low_bit, high_bit = 1, depth // 2
    first = attend(0, counts)
    first, down_sum, output_moved, gate = tied(first, down_sum, output_moved, counts)
    activations = turned_settled(output_moved)
    down_step = depth_halved(added(down_sum), low_bit)
    second = attend(1, gate)
    second, first, down_step, rest_sum, gate = tied(second, first, down_step, rest_sum, counts)
    down_step = depth_halved(added(down_step), high_bit)
    rest_step = depth_halved(added(rest_sum), low_bit)
    early = scattered_over_pairs(weight_part(jnp.concatenate([first, second], axis=1)))
    third = attend(2, gate)
    third, first, second, down_step, rest_step, early = tied(
        third, first, second, down_step, rest_step, early
    )

    partial = row_major(dot(jnp.concatenate([first, second, third], axis=1), w_qkv, NT))
    back_got = across_cores(partial[rows:].astype(LOW))
    early = depth_halved(added(early), low_bit)
    rest_step = depth_halved(added(rest_step), high_bit)
    down_own = added(down_step)
    down_got = across_depth(down_own, high_bit)
    late = scattered_over_pairs(weight_part(third))
    grad_norm_one = partial[:rows] + back_got.astype(FULL)
    grad_in, gain_one_grad, shift_one_grad = norm_backward(
        grad_norm_one, unit_one, inverse_one, gain_one
    )
    grad_rows = row_major((grad_middle + grad_in).astype(LOW))
    input_moved = turned_parts(grad_rows.reshape(2, slot_rows, width))

    row_index = lax.broadcasted_iota(jnp.int32, (8, width), 0)
    small = jnp.zeros((8, width), FULL)
    for index, value in enumerate(
        [gain_one_grad, shift_one_grad, gain_two_grad, shift_two_grad, jnp.full((width,), squares)]
    ):
        small = jnp.where(row_index == index, value[None, :], small)
    small = small + plane_steps[0](small)

    late = depth_halved(added(late), low_bit)
    rest_own = added(rest_step)
    rest_got = across_depth(rest_own, high_bit)
    late, early, rest_got, small, down_got, near = tied(
        late, early, rest_got, small, down_got, input_moved[0]
    )
    down_own = depth_doubled(down_own, down_got, high_bit)
    down_got = across_depth(down_own, low_bit)
    qkv_step = depth_halved(jnp.concatenate([added(early), added(late)], axis=1), high_bit)
    rest_own = depth_doubled(rest_own, rest_got, high_bit)
    rest_got = across_depth(rest_own, low_bit)
    small = small + plane_steps[1](small)
    qkv_step, small, down_got, far = tied(qkv_step, small, down_got, input_moved[1])
    input_grad = turned_settled([near, far])
    down_own = depth_doubled(down_own, down_got, low_bit)
    qkv_own = added(qkv_step)
    qkv_got = across_depth(qkv_own, high_bit)
    for step in plane_steps[2:]:
        small = small + step(small)
    qkv_got, rest_got, small = tied(qkv_got, rest_got, small)
    qkv_own = depth_doubled(qkv_own, qkv_got, high_bit)
    qkv_got = across_depth(qkv_own, low_bit)
    rest_own = depth_doubled(rest_own, rest_got, low_bit)
    small = small + depth_steps[0](small)

    def own_block(stack, index):
        return lax.dynamic_slice_in_dim(stack, index * own_rows, own_rows, 0)

    rest_mine = own_block(rest_own, c)
    rest_other = across_cores(own_block(rest_own, 1 - c))
    qkv_got, rest_other, small = tied(qkv_got, rest_other, small)
    qkv_own = depth_doubled(qkv_own, qkv_got, low_bit)
    qkv_mine = own_block(qkv_own, c)
    qkv_other = across_cores(own_block(qkv_own, 1 - c))
    for step in depth_steps[1:]:
        small = small + step(small)

    loss = small[4, 0] / (valid_count * width)
    own_small = lax.dynamic_slice_in_dim(small, group * own_rows, own_rows, 1)
    out_own = rest_mine[:, half_ff:].astype(FULL) + rest_other[:, half_ff:].astype(FULL)
    sides = [jnp.where(is_first, rest_mine, rest_other), jnp.where(is_first, rest_other, rest_mine)]
    up_own = jnp.concatenate(
        [side[:, q * block : (q + 1) * block] for q in range(pairs) for side in sides], axis=1
    )
    qkv_own = jnp.stack(
        [jnp.where(is_first, qkv_mine, qkv_other), jnp.where(is_first, qkv_other, qkv_mine)]
    )
    qkv_own = qkv_own.reshape(2, own_rows, head_pairs, 3, 2, HEAD_DIM)
    qkv_own = jnp.transpose(qkv_own, (1, 0, 2, 4, 3, 5)).reshape(own_rows, 3 * width)
    return (
        activations, loss, input_grad, own_small[0], own_small[1], qkv_own.astype(FULL),
        out_own, own_small[2], own_small[3], up_own.astype(FULL), down_own.astype(FULL),
    )


def solution(mesh):
    groups, depth = mesh.shape["dp"], mesh.shape["seq"]
    split = Mesh(mesh.devices.reshape(groups // 2, 2, depth), AXES)
    dp = ("pair", "core")
    rows3 = P(dp, "seq", None)
    in_specs = (
        rows3, rows3, P(dp, "seq"), P(), P(), P(dp), P(dp), P(dp, None), P(dp, None),
        P(dp), P(dp), P(dp, None), P(dp, None),
    )
    out_specs = (
        rows3, P(), rows3, P(dp), P(dp), P(dp, None), P(dp, None), P(dp), P(dp),
        P(dp, None), P(dp, None),
    )
    return jax.shard_map(shards, mesh=split, in_specs=in_specs, out_specs=out_specs, check_vma=False)
```

```python
import functools
import math

import jax
import jax.numpy as jnp
from jax import lax
from jax.experimental import pallas as pl
from jax.experimental.layout import Layout, with_layout_constraint
from jax.experimental.pallas import tpu as pltpu
from jax.sharding import Mesh
from jax.sharding import PartitionSpec as P

HEADS = 12
HEAD_DIM = 64
EPSILON = 1e-12
NEGATIVE = -1e30
SCALE = 1.0 / math.sqrt(HEAD_DIM)
AXES = ("pair", "core", "seq")
NT = (((1,), (1,)), ((), ()))
NN = (((1,), (0,)), ((), ()))
TN = (((0,), (0,)), ((), ()))
LOW = jnp.bfloat16
FULL = jnp.float32


def dot(left, right, form):
    return lax.dot_general(left, right, form, preferred_element_type=FULL)


def row_major(value):
    return with_layout_constraint(value, Layout(major_to_minor=tuple(range(value.ndim))))


def moved(value, target):
    pairs, cores, depth = (lax.axis_size(name) for name in AXES)
    links = []
    for p in range(pairs):
        for c in range(cores):
            for z in range(depth):
                q, e, w = target(p, c, z)
                links.append(((p * cores + c) * depth + z, (q * cores + e) * depth + w))
    return lax.ppermute(value, AXES, links)


def across_cores(value):
    return moved(value, lambda p, c, z: (p, 1 - c, z))


def across_pairs(value, bit):
    return moved(value, lambda p, c, z: (p ^ bit, c, z))


def across_depth(value, bit):
    return moved(value, lambda p, c, z: (p, c, z ^ bit))


def pair_bits():
    return [1 << level for level in range(lax.axis_size("pair").bit_length() - 1)]


def turned_parts(stack):
    z = lax.axis_index("seq")
    got = []
    for step in range(2):
        piece = lax.dynamic_index_in_dim(stack, (z + step) % 2, 0, keepdims=False)
        got.append(moved(piece, lambda p, c, w: (p, w // 2, 2 * c + (w + step) % 2)))
    return got


def turned_settled(got):
    even = lax.axis_index("seq") % 2 == 0
    return jnp.stack([jnp.where(even, got[0], got[1]), jnp.where(even, got[1], got[0])])


def turned(stack):
    return turned_settled(turned_parts(stack))


def sum_steps():
    depth_steps = [
        functools.partial(across_depth, bit=1 << level)
        for level in range(lax.axis_size("seq").bit_length() - 1)
    ]
    pair_steps = [functools.partial(across_pairs, bit=bit) for bit in pair_bits()]
    return depth_steps, [across_cores] + pair_steps


def gathered_over_pairs(value):
    p = lax.axis_index("pair")
    if lax.axis_size("pair") <= 4:
        count = lax.axis_size("pair")
        layout = tuple((k, k, 0, 0, value.shape[0]) for k in range(count))
        return [value] + [across_pairs(value, k) for k in range(1, count)], p, layout
    rows, width = value.shape
    bits = pair_bits()
    count = 1 << len(bits)
    halves = []
    for which in range(2):
        order = bits if which == 0 else bits[::-1]
        current = value[which * rows // 2 : (which + 1) * rows // 2]
        for bit in order:
            other = across_pairs(current, bit)
            flag = jnp.bitwise_and(p, bit) != 0
            current = jnp.stack(
                [jnp.where(flag, other, current), jnp.where(flag, current, other)]
            )
        if which == 1:
            lead = tuple(range(len(bits)))[::-1]
            current = jnp.transpose(current, lead + (len(bits), len(bits) + 1))
        halves.append(current.reshape(count, rows // 2, width))
    return [jnp.concatenate(halves, axis=1).reshape(count * rows, width)], None, ()


def halves_first(value):
    if lax.axis_size("pair") != 4:
        return value, None
    rows = value.shape[0] // 2
    return value, (across_pairs(value[:rows], 1), across_pairs(value[rows:], 2))


def halves_second(state):
    value, near = state
    if near is None:
        return gathered_over_pairs(value)
    rows = value.shape[0] // 2
    upper = across_pairs(jnp.concatenate([value[:rows], near[0]], axis=0), 2)
    lower = across_pairs(jnp.concatenate([value[rows:], near[1]], axis=0), 1)
    layout = (
        (0, 0, 0, 0, 2 * rows),
        (1, 1, 0, 0, rows), (1, 4, 0, rows, rows),
        (2, 3, 0, 0, rows), (2, 2, 0, rows, rows),
        (3, 3, rows, 0, rows), (3, 4, rows, rows, rows),
    )
    return [value, near[0], near[1], upper, lower], lax.axis_index("pair"), layout


def place_kernel(p_ref, *refs, segments, layout, count):
    sources, results = refs[:count], refs[count:]
    for k, source, origin, first, size in layout:
        spot = jnp.bitwise_xor(p_ref[0], k)
        for index, row, rows, column, width, target in segments:
            low, high = max(row, first), min(row + rows, first + size)
            if low < high:
                start = pl.multiple_of(spot * rows + (low - row), 16)
                results[index][pl.ds(start, high - low), target : target + width] = sources[source][
                    low - first + origin : high - first + origin, column : column + width
                ]


def placed(gathered, segments):
    pieces, p, layout = gathered
    pairs = lax.axis_size("pair")
    outs = 1 + max(segment[0] for segment in segments)
    if p is None:
        stack = pieces[0].reshape(pairs, -1, pieces[0].shape[1])
        results = []
        for index in range(outs):
            parts = [
                stack[:, row : row + rows, column : column + width].reshape(pairs * rows, width)
                for which, row, rows, column, width, _ in segments
                if which == index
            ]
            results.append(jnp.concatenate(parts, axis=1))
        return results
    shapes = []
    for index in range(outs):
        mine = [segment for segment in segments if segment[0] == index]
        shapes.append(
            jax.ShapeDtypeStruct((pairs * mine[0][2], sum(part[4] for part in mine)), LOW)
        )
    local = pl.BlockSpec(memory_space=pltpu.VMEM)
    return pl.pallas_call(
        functools.partial(place_kernel, segments=segments, layout=layout, count=len(pieces)),
        in_specs=[pl.BlockSpec(memory_space=pltpu.SMEM)] + [local] * len(pieces),
        out_specs=[local] * outs,
        out_shape=shapes,
        name="place",
    )(p.astype(jnp.int32).reshape(1), *pieces)


def scattered_over_pairs(value):
    p = lax.axis_index("pair")
    if lax.axis_size("pair") <= 4:
        rows = value.shape[0] // lax.axis_size("pair")
        pieces = []
        for k in range(lax.axis_size("pair")):
            piece = lax.dynamic_slice_in_dim(value, jnp.bitwise_xor(p, k) * rows, rows, 0)
            pieces.append(across_pairs(piece, k) if k else piece)
        return pieces
    bits = pair_bits()
    count = 1 << len(bits)
    rows, width = value.shape[0] // count, value.shape[1]
    blocks = value.reshape(count, rows, width)
    halves = []
    for which in range(2):
        order = bits if which == 0 else bits[::-1]
        current = blocks[:, which * rows // 2 : (which + 1) * rows // 2]
        current = current.reshape((2,) * len(bits) + (rows // 2, width))
        left = bits[::-1]
        for bit in order:
            axis = left.index(bit)
            mine = jnp.where(jnp.bitwise_and(p, bit) != 0, 1, 0)
            keep = lax.dynamic_index_in_dim(current, mine, axis, keepdims=False)
            send = lax.dynamic_index_in_dim(current, 1 - mine, axis, keepdims=False)
            current = keep + across_pairs(send, bit)
            left = [other for other in left if other != bit]
        halves.append(current)
    return [jnp.concatenate(halves, axis=0)]


def added(pieces):
    total = pieces[0].astype(FULL)
    for piece in pieces[1:]:
        total = total + piece.astype(FULL)
    return total.astype(LOW)


def depth_flag(bit):
    return jnp.where(jnp.bitwise_and(lax.axis_index("seq"), bit) != 0, 1, 0)


def depth_halved(value, bit):
    mine = depth_flag(bit)
    parts = value.reshape((2, value.shape[0] // 2) + value.shape[1:])
    keep = lax.dynamic_index_in_dim(parts, mine, 0, keepdims=False)
    send = lax.dynamic_index_in_dim(parts, 1 - mine, 0, keepdims=False)
    return [keep, across_depth(send, bit)]


def depth_doubled(value, other, bit):
    mine = depth_flag(bit)
    return jnp.concatenate(
        [jnp.where(mine == 0, value, other), jnp.where(mine == 0, other, value)], axis=0
    )


def tied(*values):
    return lax.optimization_barrier(values)


def keys_with_mask(k_ref, counts_ref, ka, rows):
    lane = lax.broadcasted_iota(jnp.int32, (rows, 128), 1)
    spot = lax.broadcasted_iota(jnp.int32, (rows, 128), 0)
    limit = jnp.where(spot < rows // 2, counts_ref[0], counts_ref[1] + rows // 2)
    bias = jnp.where(spot < limit, 0.0, NEGATIVE)
    k = k_ref[...].astype(FULL)
    ka[0] = jnp.where(lane < 64, k, jnp.where(lane == 64, bias, 0.0)).astype(LOW)
    ka[1] = jnp.where(lane >= 64, k, jnp.where(lane == 0, bias, 0.0)).astype(LOW)


def forward_kernel(counts_ref, q_ref, k_ref, v_ref, o_ref, lse_ref, ka, vt, *, rows, block):
    @pl.when(pl.program_id(1) == 0)
    def _():
        keys_with_mask(k_ref, counts_ref, ka, rows)
        vt[...] = v_ref[...].T

    lane = lax.broadcasted_iota(jnp.int32, (block, 128), 1)
    q = q_ref[...].astype(FULL) * SCALE
    mixed = []
    for h in range(2):
        mine = (lane < 64) if h == 0 else (lane >= 64)
        flag = lane == (64 if h == 0 else 0)
        qa = jnp.where(mine, q, jnp.where(flag, 1.0, 0.0)).astype(LOW)
        scores = dot(ka[h], qa, NT)
        highest = jnp.max(scores, axis=0, keepdims=True)
        exponent = jnp.exp(scores - highest)
        totals = jnp.sum(exponent, axis=0, keepdims=True)
        part = dot(vt[pl.ds(64 * h, 64), :], exponent.astype(LOW), NN)
        mixed.append(part * (1.0 / totals))
        lse_ref[0, pl.ds(h, 1), :] = highest + jnp.log(totals)
    o_ref[...] = jnp.concatenate(mixed, axis=0).T.astype(LOW)


def attention_forward(counts, qkv, block):
    rows, width = qkv.shape
    pairs = width // 384
    return pl.pallas_call(
        functools.partial(forward_kernel, rows=rows, block=block),
        grid_spec=pltpu.PrefetchScalarGridSpec(
            num_scalar_prefetch=1,
            grid=(pairs, rows // block),
            in_specs=[
                pl.BlockSpec((block, 128), lambda h, i, n: (i, 3 * h)),
                pl.BlockSpec((rows, 128), lambda h, i, n: (0, 3 * h + 1)),
                pl.BlockSpec((rows, 128), lambda h, i, n: (0, 3 * h + 2)),
            ],
            out_specs=[
                pl.BlockSpec((block, 128), lambda h, i, n: (i, h)),
                pl.BlockSpec((1, 2, block), lambda h, i, n: (h, 0, i)),
            ],
            scratch_shapes=[pltpu.VMEM((2, rows, 128), LOW), pltpu.VMEM((128, rows), LOW)],
        ),
        out_shape=[
            jax.ShapeDtypeStruct((rows, pairs * 128), LOW),
            jax.ShapeDtypeStruct((pairs, 2, rows), FULL),
        ],
        cost_estimate=pl.CostEstimate(flops=1, bytes_accessed=1, transcendentals=0),
        name="attention_forward",
    )(counts, qkv, qkv, qkv)


def backward_kernel(
    counts_ref, q_ref, k_ref, v_ref, o_ref, g_ref, lse_ref, grad_ref,
    ka, va, kt, dk, dv, *, rows, block, steps, chunk,
):
    step = pl.program_id(0)

    @pl.when(step == 0)
    def _():
        keys_with_mask(k_ref, counts_ref, ka, rows)
        lane = lax.broadcasted_iota(jnp.int32, (rows, 128), 1)
        v = v_ref[...].astype(FULL)
        va[0] = jnp.where(lane < 64, v, 0.0).astype(LOW)
        va[1] = jnp.where(lane >= 64, v, 0.0).astype(LOW)
        kt[...] = k_ref[...].T
        dk[...] = jnp.zeros_like(dk)
        dv[...] = jnp.zeros_like(dv)

    lane = lax.broadcasted_iota(jnp.int32, (block, 128), 1)
    q = q_ref[...].astype(FULL)
    g = g_ref[...]
    wide = g.astype(FULL)
    product = (wide * o_ref[...].astype(FULL)).T
    scaled = q * SCALE
    columns = []
    for h in range(2):
        mine = (lane < 64) if h == 0 else (lane >= 64)
        flag = lane == (64 if h == 0 else 0)
        qa = jnp.where(mine, scaled, jnp.where(flag, 1.0, 0.0)).astype(LOW)
        qm = jnp.where(mine, q, 0.0).astype(LOW)
        gm = jnp.where(mine, wide, 0.0).astype(LOW)
        delta = jnp.sum(product[64 * h : 64 * h + 64], axis=0, keepdims=True)
        lse = lse_ref[0, pl.ds(h, 1), :]
        total = jnp.zeros((64, block), FULL)
        for c in range(rows // chunk):
            part = pl.ds(c * chunk, chunk)
            probs = jnp.exp(dot(ka[h, part, :], qa, NT) - lse)
            grad_probs = dot(va[h, part, :], g, NT)
            grad_scores = (probs * (grad_probs - delta)).astype(LOW)
            dv[part, :] += dot(probs.astype(LOW), gm, NN)
            dk[part, :] += dot(grad_scores, qm, NN)
            total = total + dot(kt[pl.ds(64 * h, 64), part], grad_scores, NN)
        columns.append(total)
    spot = pl.ds(pl.multiple_of(step * block, block), block)
    grad_ref[spot, 0:128] = (jnp.concatenate(columns, axis=0).T * SCALE).astype(LOW)

    @pl.when(step == steps - 1)
    def _():
        grad_ref[:, 128:256] = (dk[...] * SCALE).astype(LOW)
        grad_ref[:, 256:384] = dv[...].astype(LOW)


def attention_backward(counts, qkv, mixed, grad, lse, pair, block, chunk):
    rows = qkv.shape[0]
    steps = rows // block
    return pl.pallas_call(
        functools.partial(backward_kernel, rows=rows, block=block, steps=steps, chunk=chunk),
        grid_spec=pltpu.PrefetchScalarGridSpec(
            num_scalar_prefetch=1,
            grid=(steps,),
            in_specs=[
                pl.BlockSpec((block, 128), lambda i, n: (i, 3 * pair)),
                pl.BlockSpec((rows, 128), lambda i, n: (0, 3 * pair + 1)),
                pl.BlockSpec((rows, 128), lambda i, n: (0, 3 * pair + 2)),
                pl.BlockSpec((block, 128), lambda i, n: (i, pair)),
                pl.BlockSpec((block, 128), lambda i, n: (i, pair)),
                pl.BlockSpec((1, 2, block), lambda i, n: (pair, 0, i)),
            ],
            out_specs=pl.BlockSpec((rows, 384), lambda i, n: (0, 0)),
            scratch_shapes=[
                pltpu.VMEM((2, rows, 128), LOW),
                pltpu.VMEM((2, rows, 128), LOW),
                pltpu.VMEM((128, rows), LOW),
                pltpu.VMEM((rows, 128), FULL),
                pltpu.VMEM((rows, 128), FULL),
            ],
        ),
        out_shape=jax.ShapeDtypeStruct((rows, 384), LOW),
        cost_estimate=pl.CostEstimate(flops=1, bytes_accessed=1, transcendentals=0),
        name="attention_backward",
    )(counts, qkv, qkv, qkv, mixed, grad, lse)


def norm_parts(values):
    center = values - jnp.mean(values, axis=-1, keepdims=True)
    inverse = lax.rsqrt(jnp.mean(center * center, axis=-1, keepdims=True) + EPSILON)
    return center * inverse, inverse


def norm_backward(upstream, unit, inverse, gain):
    scaled = upstream * gain
    first = jnp.mean(scaled, axis=-1, keepdims=True)
    second = jnp.mean(scaled * unit, axis=-1, keepdims=True)
    result = inverse * (scaled - first - unit * second)
    return result, jnp.sum(upstream * unit, axis=0), jnp.sum(upstream, axis=0)


def gelu_parts(values):
    share = 0.5 * (1.0 + lax.erf(values * (1.0 / math.sqrt(2.0))))
    density = jnp.exp(-0.5 * values * values) * (1.0 / math.sqrt(2.0 * math.pi))
    return values * share, share + values * density


def shards(
    tokens, teacher, teach_mask, lengths, deal_group,
    ln1_gain, ln1_bias, qkv_weight, out_weight, ln2_gain, ln2_bias, up_weight, down_weight,
):
    pairs, cores, depth = (lax.axis_size(name) for name in AXES)
    p, c, z = (lax.axis_index(name) for name in AXES)
    groups = pairs * cores
    slot_rows, width = tokens.shape[1], tokens.shape[2]
    rows = 2 * slot_rows
    full_len = depth * slot_rows
    seq_count = lengths.shape[0]
    ff = up_weight.shape[1]
    own_rows = width // groups
    pair_rows = cores * own_rows
    half_width = width // 2
    half_ff = ff // 2
    is_first = c == 0

    def in_order(mine, other, axis):
        return jnp.concatenate(
            [jnp.where(is_first, mine, other), jnp.where(is_first, other, mine)], axis=axis
        )

    sequence = 2 * cores * p + z
    length = jnp.sum(jnp.where(jnp.arange(seq_count) == sequence, lengths, 0))
    base = c * rows
    counts = jnp.stack([length - base, length - (rows - base)])
    counts = jnp.clip(counts, 0, rows).astype(jnp.int32)

    heads_half = HEADS // 2
    head_pairs = heads_half // 2
    wide_half = 3 * half_width
    shard = qkv_weight.reshape(own_rows, 2, head_pairs, 2, 3, HEAD_DIM)
    shard = jnp.transpose(shard, (1, 0, 2, 4, 3, 5)).reshape(2, own_rows, wide_half)
    vectors = jnp.stack([ln1_gain, ln1_bias, ln2_gain, ln2_bias], axis=1)
    vectors = jnp.pad(vectors, ((0, 0), (0, 124)))
    vectors = jnp.broadcast_to(vectors[None], (2, own_rows, 128))
    shard = jnp.concatenate([shard, vectors], axis=2)
    keep = lax.dynamic_index_in_dim(shard, c, 0, keepdims=False)
    send = lax.dynamic_index_in_dim(shard, 1 - c, 0, keepdims=False)
    qkv_shard = in_order(keep, across_cores(send), 0)
    qkv_pieces = gathered_over_pairs(qkv_shard)

    x_rows = turned(tokens).reshape(rows, width)

    masks = deal_group[0:2]
    group = p * cores + c
    sources = jnp.bitwise_xor(group, masks) * 2 + jnp.arange(2, dtype=jnp.int32)
    picked = jnp.arange(seq_count, dtype=jnp.int32)[None, :] == sources[:, None]
    dealt_len = jnp.sum(jnp.where(picked, lengths[None, :], 0), axis=1)
    positions = z * slot_rows + jnp.arange(slot_rows, dtype=jnp.int32)
    live = (positions[None, :] < dealt_len[:, None]) & (teach_mask == 1)
    tally = jnp.full((8, 128), jnp.sum(live.astype(FULL)))
    tally = tally + across_cores(tally)

    mask_rows = jnp.pad(
        teach_mask.astype(LOW)[:, None, :], ((0, 0), (0, 15), (0, width - slot_rows))
    )
    slots = jnp.concatenate([teacher, mask_rows], axis=1)

    def dealt(slots, level):
        flagged = jnp.bitwise_and(jnp.right_shift(masks[0], level), 1) == 1
        outgoing = jnp.where(flagged, slots[0], slots[1])
        incoming = across_cores(outgoing) if level == 0 else across_pairs(outgoing, 1 << (level - 1))
        return [flagged, slots, incoming]

    def settled(flagged, slots, incoming):
        return jnp.stack(
            [jnp.where(flagged, incoming, slots[0]), jnp.where(flagged, slots[1], incoming)]
        )

    levels = groups.bit_length() - 1
    deal = dealt(slots, 0)

    block = ff // groups

    def unit_blocks(part):
        return jnp.concatenate(
            [up_weight[:, (2 * q + part) * block : (2 * q + part + 1) * block] for q in range(pairs)],
            axis=1,
        )

    up_parts = [unit_blocks(0), unit_blocks(1)]
    keep = jnp.where(is_first, up_parts[0], up_parts[1])
    send = jnp.where(is_first, up_parts[1], up_parts[0])
    got = across_cores(jnp.concatenate([send[:, :width], send[:, width:], out_weight], axis=0))
    up_shard = in_order(keep, jnp.concatenate([got[:own_rows], got[own_rows : 2 * own_rows]], axis=1), 0)
    out_shard = in_order(out_weight, got[2 * own_rows :], 0)
    payload = jnp.concatenate(
        [down_weight, up_shard[:, :width], up_shard[:, width:], out_shard], axis=0
    )
    down_rows = down_weight.shape[0]
    payload_plan = (
        (0, 0, down_rows, 0, width, 0),
        (1, down_rows, pair_rows, 0, width, 0),
        (1, down_rows + pair_rows, pair_rows, 0, width, width),
        (2, down_rows + 2 * pair_rows, pair_rows, 0, width, 0),
    )
    depth_steps, plane_steps = sum_steps()
    for step in plane_steps[1:]:
        tally = tally + step(tally)
    x_rows, payload, tally = tied(x_rows, payload, tally)
    payload_first = halves_first(payload)

    x_full = x_rows.astype(FULL)
    unit_one, inverse_one = norm_parts(x_full)
    w_qkv, vectors = placed(
        qkv_pieces,
        ((0, 0, pair_rows, 0, wide_half, 0), (1, 0, pair_rows, wide_half, 128, 0)),
    )
    pick = lax.broadcasted_iota(jnp.int32, (8, 128), 0) == lax.broadcasted_iota(jnp.int32, (8, 128), 1)
    vectors = dot(pick.astype(LOW), vectors, NT)
    gain_one, shift_one, gain_two, shift_two = vectors[0], vectors[1], vectors[2], vectors[3]
    norm_mine = (unit_one * gain_one + shift_one).astype(LOW)
    norm_one = jnp.concatenate([norm_mine, across_cores(norm_mine)], axis=0)
    norm_one, tally, deal = tied(norm_one, tally, deal)
    deal = dealt(settled(*deal), 1)
    tally = tally + depth_steps[0](tally)
    qkv = dot(norm_one, w_qkv, NN).astype(LOW)
    qkv, deal, tally, payload_first = tied(qkv, deal, tally, payload_first)
    payload_pieces = halves_second(payload_first)
    for level in range(2, levels):
        deal = dealt(settled(*deal), level)
    for step in depth_steps[1:]:
        tally = tally + step(tally)
    mixed, lse = attention_forward(counts, qkv, 512)

    sources, *place_args = payload_pieces
    mixed, sources, deal, tally = tied(mixed, sources, deal, tally)
    mixed_got = across_cores(mixed[rows:])
    goal_moved = turned_parts(settled(*deal))
    w_down, w_up, w_out = placed((sources, *place_args), payload_plan)

    attended = in_order(mixed[:rows], mixed_got, 1)
    middle = x_full + dot(attended, w_out, NN)
    unit_two, inverse_two = norm_parts(middle)
    norm_two = (unit_two * gain_two + shift_two).astype(LOW)
    norm_other = across_cores(norm_two)

    def expanded(low):
        value, slope = gelu_parts(dot(low, w_up, NN))
        return value.astype(LOW), slope.astype(LOW)

    active_mine, slope_mine = expanded(norm_two)
    active_other, slope_other = expanded(norm_other)
    active_other, slope_other, goal_moved = tied(active_other, slope_other, goal_moved)
    goal = turned_settled(goal_moved)
    part_other = row_major(dot(active_other, w_down, NN).astype(LOW))
    part_mine = row_major(dot(active_mine, w_down, NN))
    output = middle + part_mine + across_cores(part_other).astype(FULL)

    output, goal, tally = tied(output, goal, tally)
    valid_count = tally[0, 0]
    spots = base + jnp.arange(rows, dtype=jnp.int32)
    taught = goal[:, slot_rows, :slot_rows].reshape(rows)
    valid = ((spots < length) & (taught == 1)).astype(FULL)[:, None]
    error = output - goal[:, :slot_rows].reshape(rows, width).astype(FULL)
    squares = jnp.sum(valid * error * error)
    factor = seq_count * full_len * 1.0 / valid_count
    grad_out = valid * (2.0 * factor) * error
    grad_ff = grad_out.astype(LOW)
    grad_ff_other = across_cores(grad_ff)
    output_moved = turned_parts(output.astype(LOW).reshape(2, slot_rows, width))
    hidden_mine = (dot(grad_ff, w_down, NT) * slope_mine.astype(FULL)).astype(LOW)
    down_grad = (dot(active_mine, grad_ff, TN) + dot(active_other, grad_ff_other, TN)).astype(LOW)
    down_grad, grad_ff_other, hidden_mine = tied(down_grad, grad_ff_other, hidden_mine)
    down_sum = scattered_over_pairs(down_grad)
    hidden_other = (dot(grad_ff_other, w_down, NT) * slope_other.astype(FULL)).astype(LOW)
    back_other = dot(hidden_other, w_up, NT).astype(LOW)
    back_got = across_cores(back_other)
    back_mine = dot(hidden_mine, w_up, NT)
    up_grad = (dot(norm_two, hidden_mine, TN) + dot(norm_other, hidden_other, TN)).astype(LOW)
    grad_mid, gain_two_grad, shift_two_grad = norm_backward(
        back_mine + back_got.astype(FULL), unit_two, inverse_two, gain_two
    )
    grad_middle = grad_out + grad_mid
    grad_branch = grad_middle.astype(LOW)
    grad_attended = dot(grad_branch, w_out, NT).astype(LOW)
    keep = jnp.where(is_first, grad_attended[:, :half_width], grad_attended[:, half_width:])
    send = jnp.where(is_first, grad_attended[:, half_width:], grad_attended[:, :half_width])
    mixed_grad_got = across_cores(send)
    out_grad = dot(attended, grad_branch, TN).astype(LOW)
    rest_sum = scattered_over_pairs(jnp.concatenate([up_grad, out_grad], axis=1))
    grad_mixed = jnp.concatenate([keep, mixed_grad_got], axis=0)

    def attend(pair, gate):
        return attention_backward(gate, qkv, mixed, grad_mixed, lse, pair, 512, 512)

    def weight_part(grads):
        return dot(norm_one, grads, TN).astype(LOW)

    low_bit, high_bit = 1, depth // 2
    first = attend(0, counts)
    first, down_sum, output_moved, gate = tied(first, down_sum, output_moved, counts)
    activations = turned_settled(output_moved)
    down_step = depth_halved(added(down_sum), low_bit)
    second = attend(1, gate)
    second, first, down_step, rest_sum, gate = tied(second, first, down_step, rest_sum, counts)
    down_step = depth_halved(added(down_step), high_bit)
    rest_step = depth_halved(added(rest_sum), low_bit)
    early = scattered_over_pairs(weight_part(jnp.concatenate([first, second], axis=1)))
    third = attend(2, gate)
    third, first, second, down_step, rest_step, early = tied(
        third, first, second, down_step, rest_step, early
    )

    partial = row_major(dot(jnp.concatenate([first, second, third], axis=1), w_qkv, NT))
    back_got = across_cores(partial[rows:].astype(LOW))
    early = depth_halved(added(early), low_bit)
    rest_step = depth_halved(added(rest_step), high_bit)
    down_own = added(down_step)
    down_got = across_depth(down_own, high_bit)
    late = scattered_over_pairs(weight_part(third))
    grad_norm_one = partial[:rows] + back_got.astype(FULL)
    grad_in, gain_one_grad, shift_one_grad = norm_backward(
        grad_norm_one, unit_one, inverse_one, gain_one
    )
    grad_rows = row_major((grad_middle + grad_in).astype(LOW))
    input_moved = turned_parts(grad_rows.reshape(2, slot_rows, width))

    row_index = lax.broadcasted_iota(jnp.int32, (8, width), 0)
    small = jnp.zeros((8, width), FULL)
    for index, value in enumerate(
        [gain_one_grad, shift_one_grad, gain_two_grad, shift_two_grad, jnp.full((width,), squares)]
    ):
        small = jnp.where(row_index == index, value[None, :], small)
    small = small + plane_steps[0](small)

    late = depth_halved(added(late), low_bit)
    rest_own = added(rest_step)
    rest_got = across_depth(rest_own, high_bit)
    late, early, small, near = tied(late, early, small, input_moved[0])
    down_own = depth_doubled(down_own, down_got, high_bit)
    down_got = across_depth(down_own, low_bit)
    qkv_step = depth_halved(jnp.concatenate([added(early), added(late)], axis=1), high_bit)
    rest_own = depth_doubled(rest_own, rest_got, high_bit)
    rest_got = across_depth(rest_own, low_bit)
    small = small + plane_steps[1](small)
    qkv_step, small, down_got, far = tied(qkv_step, small, down_got, input_moved[1])
    input_grad = turned_settled([near, far])
    down_own = depth_doubled(down_own, down_got, low_bit)
    qkv_own = added(qkv_step)
    qkv_got = across_depth(qkv_own, high_bit)
    for step in plane_steps[2:]:
        small = small + step(small)
    qkv_got, rest_got, small = tied(qkv_got, rest_got, small)
    qkv_own = depth_doubled(qkv_own, qkv_got, high_bit)
    qkv_got = across_depth(qkv_own, low_bit)
    rest_own = depth_doubled(rest_own, rest_got, low_bit)
    small = small + depth_steps[0](small)

    def own_block(stack, index):
        return lax.dynamic_slice_in_dim(stack, index * own_rows, own_rows, 0)

    rest_mine = own_block(rest_own, c)
    rest_other = across_cores(own_block(rest_own, 1 - c))
    qkv_got, rest_other, small = tied(qkv_got, rest_other, small)
    qkv_own = depth_doubled(qkv_own, qkv_got, low_bit)
    qkv_mine = own_block(qkv_own, c)
    qkv_other = across_cores(own_block(qkv_own, 1 - c))
    for step in depth_steps[1:]:
        small = small + step(small)

    loss = small[4, 0] / (valid_count * width)
    own_small = lax.dynamic_slice_in_dim(small, group * own_rows, own_rows, 1)
    out_own = rest_mine[:, half_ff:].astype(FULL) + rest_other[:, half_ff:].astype(FULL)
    sides = [jnp.where(is_first, rest_mine, rest_other), jnp.where(is_first, rest_other, rest_mine)]
    up_own = jnp.concatenate(
        [side[:, q * block : (q + 1) * block] for q in range(pairs) for side in sides], axis=1
    )
    qkv_own = jnp.stack(
        [jnp.where(is_first, qkv_mine, qkv_other), jnp.where(is_first, qkv_other, qkv_mine)]
    )
    qkv_own = qkv_own.reshape(2, own_rows, head_pairs, 3, 2, HEAD_DIM)
    qkv_own = jnp.transpose(qkv_own, (1, 0, 2, 4, 3, 5)).reshape(own_rows, 3 * width)
    return (
        activations, loss, input_grad, own_small[0], own_small[1], qkv_own.astype(FULL),
        out_own, own_small[2], own_small[3], up_own.astype(FULL), down_own.astype(FULL),
    )


def solution(mesh):
    groups, depth = mesh.shape["dp"], mesh.shape["seq"]
    split = Mesh(mesh.devices.reshape(groups // 2, 2, depth), AXES)
    dp = ("pair", "core")
    rows3 = P(dp, "seq", None)
    in_specs = (
        rows3, rows3, P(dp, "seq"), P(), P(), P(dp), P(dp), P(dp, None), P(dp, None),
        P(dp), P(dp), P(dp, None), P(dp, None),
    )
    out_specs = (
        rows3, P(), rows3, P(dp), P(dp), P(dp, None), P(dp, None), P(dp), P(dp),
        P(dp, None), P(dp, None),
    )
    return jax.shard_map(shards, mesh=split, in_specs=in_specs, out_specs=out_specs, check_vma=False)
```
